32 devices in a mesh: lat: 8 (over z, y), rad: 4 (over x, core).
Axes of the slice: x: 2, y: 2, z: 4, core: 2. Of those that a mesh axis runs over, the one named last changes fastest.
Arguments:
- source: float32 [128, 32768], P('rad', 'lat'), may hold values from -6 to 6
- to_modes: float32 [128, 128], replicated, may hold values from -0.5 to 0.5
- from_modes: float32 [128, 128], replicated, may hold values from -0.5 to 0.5
- eigenvalue: float32 [128], replicated, may hold values from 0.1 to 20
- shifts: float32 [32768], P('lat'), may hold values from 0.5 to 2
- weights: float32 [31, 32768], P(None, 'lat'), may hold values from 0.02 to 0.12
- neighbors: int32 [31, 256], P(None, 'lat'), may hold values from -8 to 8, as said below
Outputs:
- smoothed: float32 [128, 32768], P('rad', 'lat')
- residual_norm: float32 [128], P('rad')
The draws below stay inside these ranges and needn't reach their ends.
Inputs may be any that keep to these rules, and one draw needn't show every extreme that they name: `neighbors`: every entry is nonzero; some entry equals -8.
All inputs are finite; a program needn't handle non-finite values.
Results may differ from the reference program's by a relative error of at most 0.000073.
Values sent between devices are 32-bit elements; how exact they have to be, the bound alone decides.
A program may use at most 64 MiB of HBM per device.

```python
import math
import jax
import jax.numpy as jnp
from jax import lax

LEVELS = 128
STENCIL = 31
BLOCK = 128
HALO_BLOCKS = 8
NODES = 32768


def draw_neighbors(key, part):
    offsets = jax.random.randint(key, (STENCIL, NODES // BLOCK), -HALO_BLOCKS, HALO_BLOCKS + 1).astype(jnp.int32)
    offsets = jnp.where(offsets == 0, HALO_BLOCKS, offsets)
    offsets = offsets.at[0, 0].set(-HALO_BLOCKS)
    return offsets.astype(jnp.int32)


def shard_levels(rng, shape, split, smallest, largest):
    factor_of = 1.0
    for dim, parts in split:
        draws = jax.random.uniform(jax.random.fold_in(jax.random.fold_in(rng, 6), dim), (parts,), jnp.float32, smallest / len(split), largest / len(split))
        factor_of = factor_of * jnp.repeat(jnp.exp(draws), shape[dim] // parts).reshape((-1,) + (1,) * (len(shape) - 1 - dim))
    return factor_of


def scatter_about(stream_key, extent, width, most, split=(), held_as=jnp.bfloat16):
    values = jax.random.normal(stream_key, extent, jnp.float32) * width
    if len(split) > 0:
        values = shard_levels(stream_key, extent, split, -0.22, 0.18) * values
    return jnp.clip(values, min=-most, max=most).astype(held_as)


def setup_inputs(seed: int = 0) -> dict:
    key_list = jax.random.split(jax.random.key(seed), 8)
    return {
        "source": scatter_about(key_list[0], (LEVELS, NODES), 1.0, 6.0, ((0, 4), (1, 8)), jnp.float32),
        "to_modes": scatter_about(key_list[1], (LEVELS, LEVELS), LEVELS ** -0.5, 0.5, (), jnp.float32),
        "from_modes": scatter_about(key_list[2], (LEVELS, LEVELS), LEVELS ** -0.5, 0.5, (), jnp.float32),
        "eigenvalue": jnp.clip(jnp.exp(jax.random.uniform(key_list[3], (LEVELS,), jnp.float32, math.log(0.1), math.log(20.0))), 0.1, 20.0),
        "shifts": jnp.clip(0.5 + 1.5 * jax.random.uniform(key_list[4], (NODES,), jnp.float32) ** shard_levels(key_list[4], (NODES,), ((0, 8),), -0.2, 0.2), 0.5, 2.0),
        "weights": jnp.clip(0.02 + 0.09999999776482582 * jax.random.uniform(key_list[5], (STENCIL, NODES), jnp.float32) ** shard_levels(key_list[5], (STENCIL, NODES), ((1, 8),), -0.2, 0.2), 0.02, 0.12),
        "neighbors": draw_neighbors(jax.random.fold_in(key_list[7], 71), 0),
    }


def operate(field, eigenvalue, shifts, weights, neighbors):
    total = lax.optimization_barrier(jnp.sum(weights, axis=0))
    coeffs = (shifts + total)[None, :] + eigenvalue[:, None]
    result = coeffs * field
    node_count = field.shape[1]
    node_ids = jnp.arange(node_count, dtype=jnp.int32)
    block_ids = (node_ids // BLOCK).astype(jnp.int32)
    lane_ids = (node_ids % BLOCK).astype(jnp.int32)
    for slot_index in range(weights.shape[0]):
        block_off = jnp.take(neighbors[slot_index].astype(jnp.int32), block_ids)
        target = (((block_ids + block_off) * BLOCK + (lane_ids + slot_index) % BLOCK) % node_count).astype(jnp.int32)
        result = result - weights[slot_index][None, :] * jnp.take(field, target, axis=1)
    return result

def reference(source, to_modes, from_modes, eigenvalue, shifts, weights, neighbors):
    modal = jnp.dot(to_modes, source, precision=lax.Precision.HIGHEST, preferred_element_type=jnp.float32)
    image = operate(modal, eigenvalue, shifts, weights, neighbors)
    base = lax.optimization_barrier(jnp.sum(modal * modal, axis=1))
    power = lax.optimization_barrier(jnp.sum(image * image, axis=1))
    upper = 1.5 * jnp.sqrt(power / (base + 1e-06))
    lower = upper * 0.125
    center = ((upper + lower) * 0.5)[:, None]
    half_width = ((upper - lower) * 0.5)[:, None]
    sigma = center / half_width
    rho_zero = 1.0 / sigma
    rho_one = 1.0 / (2.0 * sigma - rho_zero)
    first = modal / center
    second_res = modal - image / center
    update = rho_one * rho_zero * first + 2.0 * rho_one / half_width * second_res
    iterate = first + update
    final_res = second_res - operate(update, eigenvalue, shifts, weights, neighbors)
    residual_norm = jnp.sqrt(lax.optimization_barrier(jnp.sum(final_res * final_res, axis=1)) / (base + 1e-06))
    smoothed = jnp.dot(from_modes, iterate, precision=lax.Precision.HIGHEST, preferred_element_type=jnp.float32)
    return (smoothed, residual_norm)
```

```python
import functools
import math

import jax
import jax.numpy as jnp
from jax import lax
from jax.experimental import pallas as pl
from jax.experimental.pallas import tpu as pltpu
from jax.sharding import PartitionSpec as P

BLOCK = 128
HALO = 8
CHUNKS = 4
GROUP = 8
UNROLL = 4
CORES = 2
HIGHEST = lax.Precision.HIGHEST
MESH = pl.DeviceIdType.MESH


def dot(a, b):
    return jnp.dot(a, b, precision=HIGHEST, preferred_element_type=jnp.float32)


def repeat(count, step, carry):
    width = math.gcd(count, UNROLL)

    def trip(n, carry):
        for j in range(width):
            carry = step(n * width + j, carry)
        return carry

    if count == width:
        return trip(0, carry)
    return lax.fori_loop(0, count // width, trip, carry)


def kernel(
    L, R, S,
    src, w_hbm, to_hbm, from_hbm, eig_hbm, shift_hbm, nbr_hbm,
    out, res_ref,
    gathered, wv, wr, outer1, inner1, outer2, inner2, others, modal, image, twice, eig_t, coef, part,
    rows, s1, s2, s3, to_ref, from_ref, eig_ref, nbr_ref,
    in_sem, own_sem, w_sem, ag_recv, im_recv, x_recv, send_sem, recv_sem, out_sem,
):
    T = CHUNKS
    X = R // CORES
    M = L * CORES
    slab, nodes = src.shape
    K = slab * CORES
    half = nodes // CORES
    NB = half // BLOCK
    CB = NB // T
    HC = HALO // CB
    CW = CB * BLOCK
    E = NB + HALO
    A = -(-S // GROUP)
    lat = lax.axis_index("lat")
    rad = lax.axis_index("rad")
    core = lax.rem(rad, CORES)
    chip = lax.div(rad, CORES)
    partner = chip * CORES + (1 - core)
    me = lat * CORES + core
    other_lat = lax.rem(lat + (L - 1) * (1 - core) + core, L)

    def order(t, c):
        return t * (1 - c) + (T - 1 - t) * c

    def own_copy(q):
        return pltpu.make_async_copy(
            src.at[:, pl.ds(pl.multiple_of(core * half + q * CW, BLOCK), CW)],
            gathered.at[q, pl.ds(pl.multiple_of(rad * slab, 8), slab), :],
            own_sem,
        )

    w_copy = pltpu.make_async_copy(
        w_hbm.at[:, pl.ds(pl.multiple_of(core * half, BLOCK), half)], wv, w_sem
    )
    inputs = [
        pltpu.make_async_copy(a, b, in_sem.at[i])
        for i, (a, b) in enumerate([
            (to_hbm, to_ref), (from_hbm, from_ref), (eig_hbm, eig_ref), (nbr_hbm, nbr_ref),
            (shift_hbm.at[pl.ds(pl.multiple_of(core * NB, 8), NB), :], rows),
        ])
    ]

    def plane_peer(j):
        m = lax.rem(me + j, M)
        return m, lax.div(m, CORES), chip * CORES + lax.rem(m, CORES)

    barrier = pltpu.get_barrier_semaphore()
    for j in range(1, R):
        r = lax.rem(rad + j, R)
        pl.semaphore_signal(
            barrier, inc=1, device_id={"lat": lat, "rad": r}, device_id_type=MESH
        )
    for j in range(1, M):
        m, to_lat, to_rad = plane_peer(j)
        pl.semaphore_signal(
            barrier, inc=1, device_id={"lat": to_lat, "rad": to_rad}, device_id_type=MESH
        )
    w_copy.start()
    for copy in inputs:
        copy.start()
    for q in range(T):
        own_copy(q).start()
    pl.semaphore_wait(barrier, R - 1 + M - 1)

    AG, O1, I1, O2, I2, OT, IM, S1, S2, S3, OUT = range(11)

    def remote(src_ref, dst_ref, kind, recv, lat_to, rad_to):
        pltpu.make_async_remote_copy(
            src_ref=src_ref, dst_ref=dst_ref, send_sem=send_sem.at[kind], recv_sem=recv,
            device_id={"lat": lat_to, "rad": rad_to}, device_id_type=MESH,
        ).start()

    def whole(ref, kind, recv):
        return pltpu.make_async_remote_copy(
            src_ref=ref, dst_ref=ref, send_sem=send_sem.at[kind], recv_sem=recv,
            device_id={"lat": lat, "rad": partner}, device_id_type=MESH,
        )

    def arrived(ref, recv):
        whole(ref, AG, recv).wait_recv()

    def slot(q, r):
        return gathered.at[q, pl.ds(pl.multiple_of(r * slab, 8), slab), :]

    for t in range(T):
        for j in range(1, R):
            to = lax.rem(rad + j, R)
            to_core = lax.rem(to, CORES)
            q = order(t, to_core)
            remote(
                src.at[:, pl.ds(pl.multiple_of(to_core * half + q * CW, BLOCK), CW)],
                slot(q, rad), AG, ag_recv.at[q], lat, to,
            )

    w_copy.wait()
    for copy in inputs:
        copy.wait()
    row_id = lax.broadcasted_iota(jnp.int32, (A * GROUP, BLOCK), 0)

    def prepare(b, carry):
        wr[b, pl.ds((A - 1) * GROUP, GROUP), :] = jnp.zeros((GROUP, BLOCK), jnp.float32)
        wr[b, pl.ds(0, S), :] = wv[:, pl.ds(pl.multiple_of(b * BLOCK, BLOCK), BLOCK)]
        tile = wr[b, pl.ds(0, A * GROUP), :]
        placed = tile
        for c in range(1, GROUP):
            placed = jnp.where(lax.rem(row_id, GROUP) == c, pltpu.roll(tile, c, 1), placed)
        wr[b, pl.ds(0, A * GROUP), :] = placed
        diagonal = jnp.sum(tile, axis=0, keepdims=True) + rows[pl.ds(b, 1), :]
        wr[b, pl.ds(A * GROUP, GROUP), :] = jnp.broadcast_to(diagonal, (GROUP, BLOCK))
        return carry

    repeat(NB, prepare, 0)
    levels = to_ref.shape[0]
    eig_t[...] = jnp.transpose(jnp.broadcast_to(eig_ref[...], (levels, levels)))

    o_at = HALO * (1 - core)
    i_at = HALO * core

    def outer_dst(c, q):
        return (1 - c) * (NB + q * CB) + c * (q * CB - NB + HALO)

    def inner_dst(c, q):
        return c * (NB + q * CB) + (1 - c) * (q * CB - NB + HALO)

    outer_halo = core * NB
    inner_halo = (1 - core) * NB

    def outer_send(buf, t, kind):
        q = order(t, core)
        remote(
            buf.at[pl.ds(o_at + q * CB, CB)], buf.at[pl.ds(outer_dst(core, q), CB)],
            kind, recv_sem.at[kind], other_lat, partner,
        )

    def outer_wait(buf, kind):
        arrived(buf.at[pl.ds(outer_halo, HALO)], recv_sem.at[kind])

    def inner_send(buf, base, t, kind, recv):
        q = order(t, core)
        remote(
            buf.at[pl.ds(base + i_at + q * CB, CB)],
            buf.at[pl.ds(base + inner_dst(core, q), CB)],
            kind, recv, lat, partner,
        )

    def inner_wait(buf, base, recv):
        arrived(buf.at[pl.ds(base + inner_halo, HALO)], recv)

    def spread_at(targets, value):
        for a in range(1, A):
            moved = pltpu.roll(value, BLOCK - a * GROUP, 1)
            for buf, k in targets:
                buf[a * E + k] = moved

    def spread_halo(buf, base, at):
        def step(k, carry):
            spread_at([(buf, base + at + k)], buf[base + at + k])
            return carry

        repeat(HALO, step, 0)

    def own_rows(x):
        return to_ref[pl.ds(pl.multiple_of(x * K, 8), K), :]

    def project_others(t):
        q = order(t, core)
        for j in range(1, X):
            x = lax.rem(chip + j, X)
            base = (j - 1) * A * E
            product = dot(own_rows(x), gathered[q])
            for i in range(CB):
                value = product[:, i * BLOCK:(i + 1) * BLOCK]
                modal[x, q * CB + i] = value
                others[base + i_at + q * CB + i] = value
            if t >= T - HC:
                inner_send(others, base, t, OT, x_recv.at[j - 1])
            for i in range(CB):
                spread_at(
                    [(others, base + i_at + q * CB + i)], product[:, i * BLOCK:(i + 1) * BLOCK]
                )

    def operate(buf, base, x, b, field):
        total = None
        for c in range(GROUP):
            inner = None
            for a in range(A):
                s = a * GROUP + c
                if s < S:
                    n = nbr_ref[s, core * NB + b]
                    term = buf[base + a * E + b + n] * wr[b, pl.ds(s, 1), :]
                    inner = term if inner is None else inner + term
            if inner is not None:
                moved = inner if c == 0 else pltpu.roll(inner, BLOCK - c, 1)
                total = moved if total is None else total + moved
        eig = eig_t[pl.ds(pl.multiple_of(x * K, 8), K), :]
        return (wr[b, pl.ds(A * GROUP, 1), :] + eig) * field - total

    def first_pass(buf, at):
        def step(b, carry):
            field = modal[chip, b]
            value = operate(buf, at, chip, b, field)
            outer2[o_at + b] = value
            inner2[i_at + b] = value
            image[chip, b] = value
            return (carry[0] + field * field, carry[1] + value * value)

        return step

    zero = jnp.zeros((K, BLOCK), jnp.float32)

    def first(t, buf, at, sums):
        q = order(t, core)
        step = first_pass(buf, at)
        sums = repeat(CB, lambda i, carry: step(q * CB + i, carry), sums)
        if t < HC:
            outer_send(outer2, t, O2)
            for j in range(1, X):
                to = lax.rem(chip + j, X)
                remote(
                    image.at[chip, pl.ds(q * CB, CB)], image.at[chip, pl.ds(q * CB, CB)],
                    IM, im_recv.at[q], lat, to * CORES + core,
                )
        if t >= T - HC:
            inner_send(inner2, 0, t, I2, recv_sem.at[I2])
        return sums

    sums = (zero, zero)
    for t in range(T):
        q = order(t, core)
        if t == 0:
            mine_at = gathered.at[:, pl.ds(pl.multiple_of(rad * slab, 8), slab), :]
            pltpu.make_async_copy(mine_at, mine_at, own_sem).wait()
        arrived(gathered.at[q, pl.ds(0, (R - 1) * slab), :], ag_recv.at[q])
        product = dot(own_rows(chip), gathered[q])
        for i in range(CB):
            value = product[:, i * BLOCK:(i + 1) * BLOCK]
            b = q * CB + i
            outer1[o_at + b] = value
            inner1[i_at + b] = value
            modal[chip, b] = value
        if t < HC:
            outer_send(outer1, t, O1)
        if t >= T - HC:
            inner_send(inner1, 0, t, I1, recv_sem.at[I1])
        for i in range(CB):
            b = q * CB + i
            spread_at(
                [(outer1, o_at + b), (inner1, i_at + b)], product[:, i * BLOCK:(i + 1) * BLOCK]
            )
        if t < T - 1:
            project_others(t)
        if t == HC:
            outer_wait(outer1, O1)
            spread_halo(outer1, 0, outer_halo)
        if t >= HC:
            sums = first(t - HC, outer1, o_at, sums)
    project_others(T - 1)
    inner_wait(inner1, 0, recv_sem.at[I1])
    spread_halo(inner1, 0, inner_halo)
    for t in range(T - HC, T):
        sums = first(t, inner1, i_at, sums)

    ones = jnp.ones((8, BLOCK), jnp.float32)

    def lanes(values):
        line = lax.dot_general(
            ones, values, (((1,), (1,)), ((), ())), precision=HIGHEST,
            preferred_element_type=jnp.float32,
        )
        width = line.shape[1]
        if width < BLOCK:
            line = jnp.concatenate(
                [line, jnp.zeros((8, BLOCK - width), jnp.float32)], axis=1
            )
        return line[0:1]

    def plane_send(buf, kind):
        for j in range(1, M):
            m, to_lat, to_rad = plane_peer(j)
            remote(buf.at[me], buf.at[me], kind, recv_sem.at[kind], to_lat, to_rad)

    def plane_sum(buf, kind):
        arrived(buf.at[pl.ds(0, M - 1)], recv_sem.at[kind])
        total = buf[0]
        for m in range(1, M):
            total = total + buf[m]
        return total

    s1[me] = lanes(jnp.concatenate(sums, axis=0))
    plane_send(s1, S1)

    inside = (NB // 2) * (1 - core)
    for j in range(1, X):
        x = lax.rem(chip + j, X)
        base = (j - 1) * A * E
        inner_wait(others, base, x_recv.at[j - 1])
        spread_halo(others, base, inner_halo)
    for j in range(1, X):
        x = lax.rem(chip + j, X)
        base = (j - 1) * A * E

        def others_pass(i, carry, x=x, base=base):
            b = inside + i
            image[x, b] = operate(others, base + i_at, x, b, modal[x, b])
            return carry

        repeat(NB // 2, others_pass, 0)

    mine = jnp.concatenate(
        [
            from_ref[pl.ds(pl.multiple_of(rad * slab, 8), slab), :],
            from_ref[pl.ds(pl.multiple_of(partner * slab, 8), slab), :],
        ],
        axis=0,
    )

    def columns(q):
        return out.at[:, pl.ds(pl.multiple_of(core * half + q * CW, BLOCK), CW)]

    def columns_of(c):
        return out.at[:, pl.ds(c * half, half)]

    def finish(t):
        q = order(t, core)
        if t < HC:
            for j in range(1, X):
                x = lax.rem(chip + j, X)
                if j == 1:
                    arrived(image.at[pl.ds(0, X - 1), pl.ds(q * CB, CB)], im_recv.at[q])
        blocks = []
        for i in range(CB):
            b = q * CB + i
            blocks.append(
                jnp.concatenate(
                    [coef[x, 0] * modal[x, b] + coef[x, 1] * image[x, b] for x in range(X)], axis=0
                )
            )
        product = dot(mine, jnp.concatenate(blocks, axis=1))
        part[q, 0] = product[0:slab]
        part[q, 1] = product[slab:K]
        remote(part.at[q, 1], columns(q), OUT, recv_sem.at[OUT], lat, partner)
        pltpu.make_async_copy(part.at[q, 0], columns(q), out_sem).start()

    def spread_own(b, carry):
        spread_at([(outer2, o_at + b), (inner2, i_at + b)], image[chip, b])
        return carry

    def residual(b, value, carry):
        final = modal[chip, b] - (coef[chip, 0] * image[chip, b] + coef[chip, 1] * value)
        return carry + final * final

    def second_inside(i, carry):
        b = inside + i
        twice[b] = operate(inner2, i_at, chip, b, image[chip, b])
        return carry

    def residual_inside(i, carry):
        b = inside + i
        return residual(b, twice[b], carry)

    outside = (NB // 2) * core

    def second_outside(i, carry):
        b = outside + i
        return residual(b, operate(outer2, o_at, chip, b, image[chip, b]), carry)

    repeat(NB, spread_own, 0)
    inner_wait(inner2, 0, recv_sem.at[I2])
    spread_halo(inner2, 0, inner_halo)
    s2[chip] = plane_sum(s1, S1)
    for j in range(1, X):
        x = lax.rem(chip + j, X)
        remote(s2.at[chip], s2.at[chip], S2, recv_sem.at[S2], lat, x * CORES + core)

    repeat(NB // 2, second_inside, 0)

    arrived(s2.at[pl.ds(0, X - 1)], recv_sem.at[S2])
    for x in range(X):
        column = jnp.transpose(jnp.broadcast_to(s2[x], (BLOCK, BLOCK)))
        base, power = column[0:K], column[K:2 * K]
        upper = 1.5 * jnp.sqrt(power / (base + 1e-06))
        lower = upper * 0.125
        center = (upper + lower) * 0.5
        half_width = (upper - lower) * 0.5
        sigma = center / half_width
        rho_zero = 1.0 / sigma
        rho_one = 1.0 / (2.0 * sigma - rho_zero)
        second = 2.0 * rho_one / half_width
        coef[x, 0] = (1.0 + rho_one * rho_zero) / center + second
        coef[x, 1] = -second / center

    final = repeat(NB // 2, residual_inside, zero)
    for t in range(HC, T):
        finish(t)
    outer_wait(outer2, O2)
    spread_halo(outer2, 0, outer_halo)
    s3[me] = lanes(repeat(NB // 2, second_outside, final))
    plane_send(s3, S3)
    for t in range(HC):
        finish(t)

    norm = jnp.sqrt(plane_sum(s3, S3) / (s2[chip] + 1e-06))
    res_ref[...] = jnp.where(core == 0, norm[:, 0:slab], norm[:, slab:2 * slab])

    everything = columns_of(0)
    pltpu.make_async_copy(everything, everything, out_sem).wait()
    whole(columns_of(0), OUT, recv_sem.at[OUT]).wait()
    whole(gathered.at[:, pl.ds(0, (R - 1) * slab), :], AG, ag_recv.at[0]).wait_send()
    for kind in (O1, I1, O2, I2):
        whole(outer1.at[pl.ds(0, HALO)], kind, recv_sem.at[kind]).wait_send()
    whole(others.at[pl.ds(0, (X - 1) * HALO)], OT, recv_sem.at[OT]).wait_send()
    whole(image.at[pl.ds(0, X - 1), pl.ds(0, HALO)], IM, recv_sem.at[IM]).wait_send()
    for buf, kind in ((s1, S1), (s3, S3)):
        whole(buf.at[pl.ds(0, M - 1)], kind, recv_sem.at[kind]).wait_send()
    whole(s2.at[pl.ds(0, X - 1)], S2, recv_sem.at[S2]).wait_send()


def on_device(L, R, source, to_modes, from_modes, eigenvalue, shifts, weights, neighbors):
    slab, nodes = source.shape
    S = weights.shape[0]
    levels = to_modes.shape[0]
    T, X, K = CHUNKS, R // CORES, slab * CORES
    half = nodes // CORES
    NB = half // BLOCK
    CW = half // T
    E = NB + HALO
    A = -(-S // GROUP)
    M = L * CORES
    f32 = jnp.float32

    def window(count):
        return pltpu.VMEM((count * A * E, K, BLOCK), f32)

    dma = pltpu.SemaphoreType.DMA
    vmem = pl.BlockSpec(memory_space=pltpu.VMEM)
    hbm = pl.BlockSpec(memory_space=pltpu.HBM)
    smoothed, norm = pl.pallas_call(
        functools.partial(kernel, L, R, S),
        name="smoother",
        out_shape=(
            pltpu.VMEM((slab, nodes), f32),
            pltpu.VMEM((1, slab), f32),
        ),
        in_specs=[hbm] * 7,
        out_specs=(vmem, vmem),
        scratch_shapes=[
            pltpu.VMEM((T, levels, CW), f32),
            pltpu.VMEM((S, half), f32),
            pltpu.VMEM((NB, (A + 1) * GROUP, BLOCK), f32),
            window(1), window(1), window(1), window(1), window(X - 1),
            pltpu.VMEM((X, NB, K, BLOCK), f32),
            pltpu.VMEM((X, NB, K, BLOCK), f32),
            pltpu.VMEM((NB, K, BLOCK), f32),
            pltpu.VMEM((levels, levels), f32),
            pltpu.VMEM((X, 2, K, BLOCK), f32),
            pltpu.VMEM((T, 2, slab, CW), f32),
            pltpu.VMEM((NB, BLOCK), f32),
            pltpu.VMEM((M, 1, BLOCK), f32),
            pltpu.VMEM((X, 1, BLOCK), f32),
            pltpu.VMEM((M, 1, BLOCK), f32),
            pltpu.VMEM((levels, levels), f32),
            pltpu.VMEM((levels, levels), f32),
            pltpu.VMEM((1, levels), f32),
            pltpu.SMEM(neighbors.shape, jnp.int32),
            dma((5,)), dma(()), dma(()),
            dma((T,)), dma((T,)), dma((X - 1,)),
            dma((11,)), dma((11,)), dma(()),
        ],
        compiler_params=pltpu.CompilerParams(
            collective_id=0, has_side_effects=True, vmem_limit_bytes=67043328 - 4 * slab * nodes - 4096
        ),
    )(
        source, weights, to_modes, from_modes, eigenvalue.reshape(1, levels),
        shifts.reshape(nodes // BLOCK, BLOCK), neighbors,
    )
    return smoothed, norm.reshape(slab)


def solution(mesh):
    return jax.shard_map(
        functools.partial(on_device, mesh.shape["lat"], mesh.shape["rad"]),
        mesh=mesh,
        in_specs=(P("rad", "lat"), P(), P(), P(), P("lat"), P(None, "lat"), P(None, "lat")),
        out_specs=(P("rad", "lat"), P("rad")),
        check_vma=False,
    )
```

```python
import functools
import math

import jax
import jax.numpy as jnp
from jax import lax
from jax.experimental import pallas as pl
from jax.experimental.pallas import tpu as pltpu
from jax.sharding import PartitionSpec as P

BLOCK = 128
HALO = 8
CHUNKS = 4
GROUP = 8
UNROLL = 4
STEP = 2
CORES = 2
HIGHEST = lax.Precision.HIGHEST
MESH = pl.DeviceIdType.MESH


def dot(a, b):
    return jnp.dot(a, b, precision=HIGHEST, preferred_element_type=jnp.float32)


def repeat(count, step, carry):
    width = math.gcd(count, UNROLL)

    def trip(n, carry):
        for j in range(width):
            carry = step(n * width + j, carry)
        return carry

    if count == width:
        return trip(0, carry)
    return lax.fori_loop(0, count // width, trip, carry)


def kernel(
    L, R, S,
    src, w_hbm, to_hbm, from_hbm, eig_hbm, shift_hbm, nbr_hbm,
    out, res_ref,
    gathered, wv, wr, outer1, inner1, outer2, inner2, others, modal, image, twice, eig_t, coef, part,
    rows, s1, s2, s3, to_ref, from_ref, eig_ref, nbr_ref,
    in_sem, own_sem, w_sem, ag_recv, im_recv, x_recv, send_sem, recv_sem, out_sem, passed,
):
    T = CHUNKS
    X = R // CORES
    M = L * CORES
    slab, nodes = src.shape
    K = slab * CORES
    half = nodes // CORES
    NB = half // BLOCK
    CB = NB // T
    HC = HALO // CB
    CW = CB * BLOCK
    E = NB + HALO
    A = -(-S // GROUP)
    lat = lax.axis_index("lat")
    rad = lax.axis_index("rad")
    core = lax.rem(rad, CORES)
    chip = lax.div(rad, CORES)
    partner = chip * CORES + (1 - core)
    me = lat * CORES + core
    other_lat = lax.rem(lat + (L - 1) * (1 - core) + core, L)

    def order(t, c):
        return t * (1 - c) + (T - 1 - t) * c

    def own_copy(q):
        return pltpu.make_async_copy(
            src.at[:, pl.ds(pl.multiple_of(core * half + q * CW, BLOCK), CW)],
            gathered.at[q, pl.ds(pl.multiple_of(rad * slab, 8), slab), :],
            own_sem,
        )

    w_copy = pltpu.make_async_copy(
        w_hbm.at[:, pl.ds(pl.multiple_of(core * half, BLOCK), half)], wv, w_sem
    )
    inputs = [
        pltpu.make_async_copy(a, b, in_sem.at[i])
        for i, (a, b) in enumerate([
            (to_hbm, to_ref), (from_hbm, from_ref), (eig_hbm, eig_ref), (nbr_hbm, nbr_ref),
            (shift_hbm.at[pl.ds(pl.multiple_of(core * NB, 8), NB), :], rows),
        ])
    ]

    def plane_peer(j):
        m = lax.rem(me + j, M)
        return m, lax.div(m, CORES), chip * CORES + lax.rem(m, CORES)

    barrier = pltpu.get_barrier_semaphore()
    for j in range(1, R):
        r = lax.rem(rad + j, R)
        pl.semaphore_signal(
            barrier, inc=1, device_id={"lat": lat, "rad": r}, device_id_type=MESH
        )
    pair = lat + 1 - 2 * lax.rem(lat, 2)
    below, above = lat >= STEP, lat + STEP < L

    def signal(sem, to_lat, to_rad):
        pl.semaphore_signal(
            sem, inc=1, device_id={"lat": to_lat, "rad": to_rad}, device_id_type=MESH
        )

    def signal_below(sem):
        pl.when(below)(lambda: signal(sem, lat - STEP, rad))

    def signal_above(sem):
        pl.when(above)(lambda: signal(sem, lat + STEP, rad))

    for c in range(CORES):
        signal(barrier, pair, chip * CORES + c)
    signal_below(barrier)
    signal_above(barrier)
    w_copy.start()
    for copy in inputs:
        copy.start()
    for q in range(T):
        own_copy(q).start()
    pl.semaphore_wait(
        barrier, R - 1 + CORES + below.astype(jnp.int32) + above.astype(jnp.int32)
    )

    AG, O1, I1, O2, I2, OT, IM, S1, S2, S3, OUT = range(11)

    def remote(src_ref, dst_ref, kind, recv, lat_to, rad_to):
        pltpu.make_async_remote_copy(
            src_ref=src_ref, dst_ref=dst_ref, send_sem=send_sem.at[kind], recv_sem=recv,
            device_id={"lat": lat_to, "rad": rad_to}, device_id_type=MESH,
        ).start()

    def whole(ref, kind, recv):
        return pltpu.make_async_remote_copy(
            src_ref=ref, dst_ref=ref, send_sem=send_sem.at[kind], recv_sem=recv,
            device_id={"lat": lat, "rad": partner}, device_id_type=MESH,
        )

    def arrived(ref, recv):
        whole(ref, AG, recv).wait_recv()

    def slot(q, r):
        return gathered.at[q, pl.ds(pl.multiple_of(r * slab, 8), slab), :]

    for t in range(T):
        for j in range(1, R):
            to = lax.rem(rad + j, R)
            to_core = lax.rem(to, CORES)
            q = order(t, to_core)
            remote(
                src.at[:, pl.ds(pl.multiple_of(to_core * half + q * CW, BLOCK), CW)],
                slot(q, rad), AG, ag_recv.at[q], lat, to,
            )

    up, down = passed.at[0], passed.at[1]
    pl.when(jnp.logical_not(below))(lambda: signal_above(up))
    pl.when(jnp.logical_not(above))(lambda: signal_below(down))

    w_copy.wait()
    for copy in inputs:
        copy.wait()
    row_id = lax.broadcasted_iota(jnp.int32, (A * GROUP, BLOCK), 0)

    def prepare(b, carry):
        wr[b, pl.ds((A - 1) * GROUP, GROUP), :] = jnp.zeros((GROUP, BLOCK), jnp.float32)
        wr[b, pl.ds(0, S), :] = wv[:, pl.ds(pl.multiple_of(b * BLOCK, BLOCK), BLOCK)]
        tile = wr[b, pl.ds(0, A * GROUP), :]
        placed = tile
        for c in range(1, GROUP):
            placed = jnp.where(lax.rem(row_id, GROUP) == c, pltpu.roll(tile, c, 1), placed)
        wr[b, pl.ds(0, A * GROUP), :] = placed
        diagonal = jnp.sum(tile, axis=0, keepdims=True) + rows[pl.ds(b, 1), :]
        wr[b, pl.ds(A * GROUP, GROUP), :] = jnp.broadcast_to(diagonal, (GROUP, BLOCK))
        return carry

    repeat(NB, prepare, 0)

    @pl.when(below)
    def _():
        pl.semaphore_wait(up, 1)
        signal_above(up)

    @pl.when(above)
    def _():
        pl.semaphore_wait(down, 1)
        signal_below(down)

    levels = to_ref.shape[0]
    eig_t[...] = jnp.transpose(jnp.broadcast_to(eig_ref[...], (levels, levels)))

    o_at = HALO * (1 - core)
    i_at = HALO * core

    def outer_dst(c, q):
        return (1 - c) * (NB + q * CB) + c * (q * CB - NB + HALO)

    def inner_dst(c, q):
        return c * (NB + q * CB) + (1 - c) * (q * CB - NB + HALO)

    outer_halo = core * NB
    inner_halo = (1 - core) * NB

    def outer_send(buf, t, kind):
        q = order(t, core)
        remote(
            buf.at[pl.ds(o_at + q * CB, CB)], buf.at[pl.ds(outer_dst(core, q), CB)],
            kind, recv_sem.at[kind], other_lat, partner,
        )

    def outer_wait(buf, kind):
        arrived(buf.at[pl.ds(outer_halo, HALO)], recv_sem.at[kind])

    def inner_send(buf, base, t, kind, recv):
        q = order(t, core)
        remote(
            buf.at[pl.ds(base + i_at + q * CB, CB)],
            buf.at[pl.ds(base + inner_dst(core, q), CB)],
            kind, recv, lat, partner,
        )

    def inner_wait(buf, base, recv):
        arrived(buf.at[pl.ds(base + inner_halo, HALO)], recv)

    def spread_at(targets, value):
        for a in range(1, A):
            moved = pltpu.roll(value, BLOCK - a * GROUP, 1)
            for buf, k in targets:
                buf[a * E + k] = moved

    def spread_halo(buf, base, at):
        def step(k, carry):
            spread_at([(buf, base + at + k)], buf[base + at + k])
            return carry

        repeat(HALO, step, 0)

    def own_rows(x):
        return to_ref[pl.ds(pl.multiple_of(x * K, 8), K), :]

    def project_others(t):
        q = order(t, core)
        for j in range(1, X):
            x = lax.rem(chip + j, X)
            base = (j - 1) * A * E
            product = dot(own_rows(x), gathered[q])
            for i in range(CB):
                value = product[:, i * BLOCK:(i + 1) * BLOCK]
                modal[x, q * CB + i] = value
                others[base + i_at + q * CB + i] = value
            if t >= T - HC:
                inner_send(others, base, t, OT, x_recv.at[j - 1])
            for i in range(CB):
                spread_at(
                    [(others, base + i_at + q * CB + i)], product[:, i * BLOCK:(i + 1) * BLOCK]
                )

    def operate(buf, base, x, b, field):
        total = None
        for c in range(GROUP):
            inner = None
            for a in range(A):
                s = a * GROUP + c
                if s < S:
                    n = nbr_ref[s, core * NB + b]
                    term = buf[base + a * E + b + n] * wr[b, pl.ds(s, 1), :]
                    inner = term if inner is None else inner + term
            if inner is not None:
                moved = inner if c == 0 else pltpu.roll(inner, BLOCK - c, 1)
                total = moved if total is None else total + moved
        eig = eig_t[pl.ds(pl.multiple_of(x * K, 8), K), :]
        return (wr[b, pl.ds(A * GROUP, 1), :] + eig) * field - total

    def first_pass(buf, at):
        def step(b, carry):
            field = modal[chip, b]
            value = operate(buf, at, chip, b, field)
            outer2[o_at + b] = value
            inner2[i_at + b] = value
            image[chip, b] = value
            return (carry[0] + field * field, carry[1] + value * value)

        return step

    zero = jnp.zeros((K, BLOCK), jnp.float32)

    def first(t, buf, at, sums):
        q = order(t, core)
        step = first_pass(buf, at)
        sums = repeat(CB, lambda i, carry: step(q * CB + i, carry), sums)
        if t < HC:
            outer_send(outer2, t, O2)
            for j in range(1, X):
                to = lax.rem(chip + j, X)
                remote(
                    image.at[chip, pl.ds(q * CB, CB)], image.at[chip, pl.ds(q * CB, CB)],
                    IM, im_recv.at[q], lat, to * CORES + core,
                )
        if t >= T - HC:
            inner_send(inner2, 0, t, I2, recv_sem.at[I2])
        return sums

    sums = (zero, zero)
    for t in range(T):
        q = order(t, core)
        if t == 0:
            mine_at = gathered.at[:, pl.ds(pl.multiple_of(rad * slab, 8), slab), :]
            pltpu.make_async_copy(mine_at, mine_at, own_sem).wait()
        arrived(gathered.at[q, pl.ds(0, (R - 1) * slab), :], ag_recv.at[q])
        product = dot(own_rows(chip), gathered[q])
        for i in range(CB):
            value = product[:, i * BLOCK:(i + 1) * BLOCK]
            b = q * CB + i
            outer1[o_at + b] = value
            inner1[i_at + b] = value
            modal[chip, b] = value
        if t < HC:
            outer_send(outer1, t, O1)
        if t >= T - HC:
            inner_send(inner1, 0, t, I1, recv_sem.at[I1])
        for i in range(CB):
            b = q * CB + i
            spread_at(
                [(outer1, o_at + b), (inner1, i_at + b)], product[:, i * BLOCK:(i + 1) * BLOCK]
            )
        if t < T - 1:
            project_others(t)
        if t == HC:
            outer_wait(outer1, O1)
            spread_halo(outer1, 0, outer_halo)
        if t >= HC:
            sums = first(t - HC, outer1, o_at, sums)
    project_others(T - 1)
    inner_wait(inner1, 0, recv_sem.at[I1])
    spread_halo(inner1, 0, inner_halo)
    for t in range(T - HC, T):
        sums = first(t, inner1, i_at, sums)

    ones = jnp.ones((8, BLOCK), jnp.float32)

    def lanes(values):
        line = lax.dot_general(
            ones, values, (((1,), (1,)), ((), ())), precision=HIGHEST,
            preferred_element_type=jnp.float32,
        )
        width = line.shape[1]
        if width < BLOCK:
            line = jnp.concatenate(
                [line, jnp.zeros((8, BLOCK - width), jnp.float32)], axis=1
            )
        return line[0:1]

    def plane_send(buf, kind):
        for j in range(1, M):
            m, to_lat, to_rad = plane_peer(j)
            remote(buf.at[me], buf.at[me], kind, recv_sem.at[kind], to_lat, to_rad)

    def plane_sum(buf, kind):
        arrived(buf.at[pl.ds(0, M - 1)], recv_sem.at[kind])
        total = buf[0]
        for m in range(1, M):
            total = total + buf[m]
        return total

    s1[me] = lanes(jnp.concatenate(sums, axis=0))
    plane_send(s1, S1)

    inside = (NB // 2) * (1 - core)
    for j in range(1, X):
        x = lax.rem(chip + j, X)
        base = (j - 1) * A * E
        inner_wait(others, base, x_recv.at[j - 1])
        spread_halo(others, base, inner_halo)
    for j in range(1, X):
        x = lax.rem(chip + j, X)
        base = (j - 1) * A * E

        def others_pass(i, carry, x=x, base=base):
            b = inside + i
            image[x, b] = operate(others, base + i_at, x, b, modal[x, b])
            return carry

        repeat(NB // 2, others_pass, 0)

    mine = jnp.concatenate(
        [
            from_ref[pl.ds(pl.multiple_of(rad * slab, 8), slab), :],
            from_ref[pl.ds(pl.multiple_of(partner * slab, 8), slab), :],
        ],
        axis=0,
    )

    def columns(q):
        return out.at[:, pl.ds(pl.multiple_of(core * half + q * CW, BLOCK), CW)]

    def columns_of(c):
        return out.at[:, pl.ds(c * half, half)]

    def finish(t):
        q = order(t, core)
        if t < HC:
            for j in range(1, X):
                x = lax.rem(chip + j, X)
                if j == 1:
                    arrived(image.at[pl.ds(0, X - 1), pl.ds(q * CB, CB)], im_recv.at[q])
        blocks = []
        for i in range(CB):
            b = q * CB + i
            blocks.append(
                jnp.concatenate(
                    [coef[x, 0] * modal[x, b] + coef[x, 1] * image[x, b] for x in range(X)], axis=0
                )
            )
        product = dot(mine, jnp.concatenate(blocks, axis=1))
        part[q, 0] = product[0:slab]
        part[q, 1] = product[slab:K]
        remote(part.at[q, 1], columns(q), OUT, recv_sem.at[OUT], lat, partner)
        pltpu.make_async_copy(part.at[q, 0], columns(q), out_sem).start()

    def spread_own(b, carry):
        spread_at([(outer2, o_at + b), (inner2, i_at + b)], image[chip, b])
        return carry

    def second_pass(buf, at, first_block):
        def step(i, carry):
            b = first_block + i
            twice[b] = operate(buf, at, chip, b, image[chip, b])
            return carry

        repeat(NB // 2, step, 0)

    def residual(b, carry):
        final = modal[chip, b] - (coef[chip, 0] * image[chip, b] + coef[chip, 1] * twice[b])
        return carry + final * final

    def chebyshev(x):
        column = jnp.transpose(jnp.broadcast_to(s2[x], (BLOCK, BLOCK)))
        base, power = column[0:K], column[K:2 * K]
        upper = 1.5 * jnp.sqrt(power / (base + 1e-06))
        lower = upper * 0.125
        center = (upper + lower) * 0.5
        half_width = (upper - lower) * 0.5
        sigma = center / half_width
        rho_zero = 1.0 / sigma
        rho_one = 1.0 / (2.0 * sigma - rho_zero)
        second = 2.0 * rho_one / half_width
        coef[x, 0] = (1.0 + rho_one * rho_zero) / center + second
        coef[x, 1] = -second / center

    repeat(NB, spread_own, 0)
    inner_wait(inner2, 0, recv_sem.at[I2])
    spread_halo(inner2, 0, inner_halo)
    second_pass(inner2, i_at, inside)
    outer_wait(outer2, O2)
    spread_halo(outer2, 0, outer_halo)
    second_pass(outer2, o_at, (NB // 2) * core)

    s2[chip] = plane_sum(s1, S1)
    for j in range(1, X):
        x = lax.rem(chip + j, X)
        remote(s2.at[chip], s2.at[chip], S2, recv_sem.at[S2], lat, x * CORES + core)
    chebyshev(chip)
    s3[me] = lanes(repeat(NB, residual, zero))
    plane_send(s3, S3)

    arrived(s2.at[pl.ds(0, X - 1)], recv_sem.at[S2])
    for j in range(1, X):
        chebyshev(lax.rem(chip + j, X))
    for t in range(HC, T):
        finish(t)
    for t in range(HC):
        finish(t)

    norm = jnp.sqrt(plane_sum(s3, S3) / (s2[chip] + 1e-06))
    res_ref[...] = jnp.where(core == 0, norm[:, 0:slab], norm[:, slab:2 * slab])

    everything = columns_of(0)
    pltpu.make_async_copy(everything, everything, out_sem).wait()
    whole(columns_of(0), OUT, recv_sem.at[OUT]).wait()
    whole(gathered.at[:, pl.ds(0, (R - 1) * slab), :], AG, ag_recv.at[0]).wait_send()
    for kind in (O1, I1, O2, I2):
        whole(outer1.at[pl.ds(0, HALO)], kind, recv_sem.at[kind]).wait_send()
    whole(others.at[pl.ds(0, (X - 1) * HALO)], OT, recv_sem.at[OT]).wait_send()
    whole(image.at[pl.ds(0, X - 1), pl.ds(0, HALO)], IM, recv_sem.at[IM]).wait_send()
    for buf, kind in ((s1, S1), (s3, S3)):
        whole(buf.at[pl.ds(0, M - 1)], kind, recv_sem.at[kind]).wait_send()
    whole(s2.at[pl.ds(0, X - 1)], S2, recv_sem.at[S2]).wait_send()


def on_device(L, R, source, to_modes, from_modes, eigenvalue, shifts, weights, neighbors):
    slab, nodes = source.shape
    S = weights.shape[0]
    levels = to_modes.shape[0]
    T, X, K = CHUNKS, R // CORES, slab * CORES
    half = nodes // CORES
    NB = half // BLOCK
    CW = half // T
    E = NB + HALO
    A = -(-S // GROUP)
    M = L * CORES
    f32 = jnp.float32

    def window(count):
        return pltpu.VMEM((count * A * E, K, BLOCK), f32)

    dma = pltpu.SemaphoreType.DMA
    vmem = pl.BlockSpec(memory_space=pltpu.VMEM)
    hbm = pl.BlockSpec(memory_space=pltpu.HBM)
    smoothed, norm = pl.pallas_call(
        functools.partial(kernel, L, R, S),
        name="smoother",
        out_shape=(
            pltpu.VMEM((slab, nodes), f32),
            pltpu.VMEM((1, slab), f32),
        ),
        in_specs=[hbm] * 7,
        out_specs=(vmem, vmem),
        scratch_shapes=[
            pltpu.VMEM((T, levels, CW), f32),
            pltpu.VMEM((S, half), f32),
            pltpu.VMEM((NB, (A + 1) * GROUP, BLOCK), f32),
            window(1), window(1), window(1), window(1), window(X - 1),
            pltpu.VMEM((X, NB, K, BLOCK), f32),
            pltpu.VMEM((X, NB, K, BLOCK), f32),
            pltpu.VMEM((NB, K, BLOCK), f32),
            pltpu.VMEM((levels, levels), f32),
            pltpu.VMEM((X, 2, K, BLOCK), f32),
            pltpu.VMEM((T, 2, slab, CW), f32),
            pltpu.VMEM((NB, BLOCK), f32),
            pltpu.VMEM((M, 1, BLOCK), f32),
            pltpu.VMEM((X, 1, BLOCK), f32),
            pltpu.VMEM((M, 1, BLOCK), f32),
            pltpu.VMEM((levels, levels), f32),
            pltpu.VMEM((levels, levels), f32),
            pltpu.VMEM((1, levels), f32),
            pltpu.SMEM(neighbors.shape, jnp.int32),
            dma((5,)), dma(()), dma(()),
            dma((T,)), dma((T,)), dma((X - 1,)),
            dma((11,)), dma((11,)), dma(()), pltpu.SemaphoreType.REGULAR((2,)),
        ],
        compiler_params=pltpu.CompilerParams(
            collective_id=0, has_side_effects=True, vmem_limit_bytes=67043328 - 4 * slab * nodes - 4096
        ),
    )(
        source, weights, to_modes, from_modes, eigenvalue.reshape(1, levels),
        shifts.reshape(nodes // BLOCK, BLOCK), neighbors,
    )
    return smoothed, norm.reshape(slab)


def solution(mesh):
    return jax.shard_map(
        functools.partial(on_device, mesh.shape["lat"], mesh.shape["rad"]),
        mesh=mesh,
        in_specs=(P("rad", "lat"), P(), P(), P(), P("lat"), P(None, "lat"), P(None, "lat")),
        out_specs=(P("rad", "lat"), P("rad")),
        check_vma=False,
    )
```

```python
import functools
import math

import jax
import jax.numpy as jnp
from jax import lax
from jax.experimental import pallas as pl
from jax.experimental.pallas import tpu as pltpu
from jax.sharding import PartitionSpec as P

BLOCK = 128
HALO = 8
CHUNKS = 8
PARTS = 4
GROUP = 8
UNROLL = 8
STEP = 2
CORES = 2
HIGHEST = lax.Precision.HIGHEST
MESH = pl.DeviceIdType.MESH


def dot(a, b):
    return jnp.dot(a, b, precision=HIGHEST, preferred_element_type=jnp.float32)


def repeat(count, step, carry, most=UNROLL):
    width = math.gcd(count, most)

    def trip(n, carry):
        for j in range(width):
            carry = step(n * width + j, carry)
        return carry

    if count == width:
        return trip(0, carry)
    return lax.fori_loop(0, count // width, trip, carry)


def kernel(
    L, R, S,
    src, w_hbm, to_hbm, from_hbm, eig_hbm, shift_hbm, nbr_hbm,
    out, res_ref,
    gathered, wv, wr, outer1, inner1, outer2, inner2, others, modal, image, twice, eig_t, coef, acc, part,
    rows, s1, s2, s3, to_ref, from_ref, eig_ref, nbr_ref,
    in_sem, own_sem, w_sem, ag_recv, x_recv, send_sem, recv_sem, out_sem, passed,
):
    T = CHUNKS
    X = R // CORES
    M = L * CORES
    slab, nodes = src.shape
    K = slab * CORES
    half = nodes // CORES
    NB = half // BLOCK
    CB = NB // T
    HC = HALO // CB
    CW = CB * BLOCK
    E = NB + HALO
    A = -(-S // GROUP)
    lat = lax.axis_index("lat")
    rad = lax.axis_index("rad")
    core = lax.rem(rad, CORES)
    chip = lax.div(rad, CORES)
    partner = chip * CORES + (1 - core)
    me = lat * CORES + core
    other_lat = lax.rem(lat + (L - 1) * (1 - core) + core, L)

    def order(t, c):
        return t * (1 - c) + (T - 1 - t) * c

    def own_copy(q):
        return pltpu.make_async_copy(
            src.at[:, pl.ds(pl.multiple_of(core * half + q * CW, BLOCK), CW)],
            gathered.at[q, pl.ds(pl.multiple_of(rad * slab, 8), slab), :],
            own_sem,
        )

    w_copy = pltpu.make_async_copy(
        w_hbm.at[:, pl.ds(pl.multiple_of(core * half, BLOCK), half)], wv, w_sem
    )
    inputs = [
        pltpu.make_async_copy(a, b, in_sem.at[i])
        for i, (a, b) in enumerate([
            (to_hbm, to_ref), (from_hbm, from_ref), (eig_hbm, eig_ref), (nbr_hbm, nbr_ref),
            (shift_hbm.at[pl.ds(pl.multiple_of(core * NB, 8), NB), :], rows),
        ])
    ]

    def plane_peer(j):
        m = lax.rem(me + j, M)
        return m, lax.div(m, CORES), chip * CORES + lax.rem(m, CORES)

    barrier = pltpu.get_barrier_semaphore()
    up, down, met, near_in, all_in = [passed.at[i] for i in range(5)]
    gate = R - 1
    is_gate = rad == gate
    below, above = lat >= STEP, lat + STEP < L
    around = [(lat >= d, -d) for d in range(1, STEP + 1)] + [(lat + d < L, d) for d in range(1, STEP + 1)]

    def signal(sem, to_lat, to_rad):
        pl.semaphore_signal(
            sem, inc=1, device_id={"lat": to_lat, "rad": to_rad}, device_id_type=MESH
        )

    def signal_below(sem):
        pl.when(below)(lambda: signal(sem, lat - STEP, gate))

    def signal_above(sem):
        pl.when(above)(lambda: signal(sem, lat + STEP, gate))

    for j in range(1, R):
        r = lax.rem(rad + j, R)
        pl.when(r != gate)(functools.partial(signal, barrier, lat, r))
    w_copy.start()
    for copy in inputs:
        copy.start()
    for q in range(T):
        own_copy(q).start()

    @pl.when(jnp.logical_not(is_gate))
    def _():
        pl.semaphore_wait(barrier, R - 1)
        pl.when(partner == gate)(lambda: signal(met, lat, gate))

    @pl.when(is_gate)
    def _():
        pl.semaphore_wait(met, 1)
        for there, d in around:
            pl.when(there)(functools.partial(signal, barrier, lat + d, gate))

    AG, O1, I1, O2, I2, OT, IM, S1, S2, S3, OUT = range(11)

    def remote(src_ref, dst_ref, kind, recv, lat_to, rad_to):
        pltpu.make_async_remote_copy(
            src_ref=src_ref, dst_ref=dst_ref, send_sem=send_sem.at[kind], recv_sem=recv,
            device_id={"lat": lat_to, "rad": rad_to}, device_id_type=MESH,
        ).start()

    def whole(ref, kind, recv):
        return pltpu.make_async_remote_copy(
            src_ref=ref, dst_ref=ref, send_sem=send_sem.at[kind], recv_sem=recv,
            device_id={"lat": lat, "rad": partner}, device_id_type=MESH,
        )

    def arrived(ref, recv):
        whole(ref, AG, recv).wait_recv()

    def slot(q, r):
        return gathered.at[q, pl.ds(pl.multiple_of(r * slab, 8), slab), :]

    for t in range(T):
        for j in range(1, R):
            to = lax.rem(rad + j, R)
            to_core = lax.rem(to, CORES)
            q = order(t, to_core)
            remote(
                src.at[:, pl.ds(pl.multiple_of(to_core * half + q * CW, BLOCK), CW)],
                slot(q, rad), AG, ag_recv.at[q], lat, to,
            )

    w_copy.wait()
    for copy in inputs:
        copy.wait()
    row_id = lax.broadcasted_iota(jnp.int32, (A * GROUP, BLOCK), 0)

    def prepare(b, carry):
        wr[b, pl.ds((A - 1) * GROUP, GROUP), :] = jnp.zeros((GROUP, BLOCK), jnp.float32)
        wr[b, pl.ds(0, S), :] = wv[:, pl.ds(pl.multiple_of(b * BLOCK, BLOCK), BLOCK)]
        tile = wr[b, pl.ds(0, A * GROUP), :]
        placed = tile
        for c in range(1, GROUP):
            placed = jnp.where(lax.rem(row_id, GROUP) == c, pltpu.roll(tile, c, 1), placed)
        wr[b, pl.ds(0, A * GROUP), :] = placed
        diagonal = jnp.sum(tile, axis=0, keepdims=True) + rows[pl.ds(b, 1), :]
        wr[b, pl.ds(A * GROUP, GROUP), :] = jnp.broadcast_to(diagonal, (GROUP, BLOCK))
        return carry

    repeat(NB, prepare, 0)

    @pl.when(is_gate)
    def _():
        pl.semaphore_wait(barrier, sum(there.astype(jnp.int32) for there, _ in around))
        for r in range(R - 1):
            signal(near_in, lat, r)
        pl.when(jnp.logical_not(below))(lambda: signal_above(up))
        pl.when(jnp.logical_not(above))(lambda: signal_below(down))

        @pl.when(below)
        def _():
            pl.semaphore_wait(up, 1)
            signal_above(up)

        @pl.when(above)
        def _():
            pl.semaphore_wait(down, 1)
            signal_below(down)

        for r in range(R - 1):
            signal(all_in, lat, r)

    levels = to_ref.shape[0]
    eig_t[...] = jnp.transpose(jnp.broadcast_to(eig_ref[...], (levels, levels)))

    o_at = HALO * (1 - core)
    i_at = HALO * core

    def outer_dst(c, q):
        return (1 - c) * (NB + q * CB) + c * (q * CB - NB + HALO)

    def inner_dst(c, q):
        return c * (NB + q * CB) + (1 - c) * (q * CB - NB + HALO)

    outer_halo = core * NB
    inner_halo = (1 - core) * NB

    def outer_send(buf, t, kind):
        q = order(t, core)
        remote(
            buf.at[pl.ds(o_at + q * CB, CB)], buf.at[pl.ds(outer_dst(core, q), CB)],
            kind, recv_sem.at[kind], other_lat, partner,
        )

    def outer_wait(buf, kind):
        arrived(buf.at[pl.ds(outer_halo, HALO)], recv_sem.at[kind])

    def inner_send(buf, base, t, kind, recv):
        q = order(t, core)
        remote(
            buf.at[pl.ds(base + i_at + q * CB, CB)],
            buf.at[pl.ds(base + inner_dst(core, q), CB)],
            kind, recv, lat, partner,
        )

    def inner_wait(buf, base, recv):
        arrived(buf.at[pl.ds(base + inner_halo, HALO)], recv)

    def spread_at(targets, value):
        for a in range(1, A):
            moved = pltpu.roll(value, BLOCK - a * GROUP, 1)
            for buf, k in targets:
                buf[a * E + k] = moved

    def spread_halo(buf, base, at):
        def step(k, carry):
            spread_at([(buf, base + at + k)], buf[base + at + k])
            return carry

        repeat(HALO, step, 0, UNROLL)

    def own_rows(x):
        return to_ref[pl.ds(pl.multiple_of(x * K, 8), K), :]

    def project_others(t):
        q = order(t, core)
        for j in range(1, X):
            x = lax.rem(chip + j, X)
            base = (j - 1) * A * E
            product = dot(own_rows(x), gathered[q])
            for i in range(CB):
                value = product[:, i * BLOCK:(i + 1) * BLOCK]
                modal[x, q * CB + i] = value
                others[base + i_at + q * CB + i] = value
            if t >= T - HC:
                inner_send(others, base, t, OT, x_recv.at[j - 1])
            for i in range(CB):
                spread_at(
                    [(others, base + i_at + q * CB + i)], product[:, i * BLOCK:(i + 1) * BLOCK]
                )

    def operate(buf, base, x, b, field):
        total = None
        for c in range(GROUP):
            inner = None
            for a in range(A):
                s = a * GROUP + c
                if s < S:
                    n = nbr_ref[s, core * NB + b]
                    term = buf[base + a * E + b + n] * wr[b, pl.ds(s, 1), :]
                    inner = term if inner is None else inner + term
            if inner is not None:
                moved = inner if c == 0 else pltpu.roll(inner, BLOCK - c, 1)
                total = moved if total is None else total + moved
        eig = eig_t[pl.ds(pl.multiple_of(x * K, 8), K), :]
        return (wr[b, pl.ds(A * GROUP, 1), :] + eig) * field - total

    def first_pass(buf, at):
        def step(b, carry):
            field = modal[chip, b]
            value = operate(buf, at, chip, b, field)
            outer2[o_at + b] = value
            inner2[i_at + b] = value
            image[chip, b] = value
            return (carry[0] + field * field, carry[1] + value * value)

        return step

    zero = jnp.zeros((K, BLOCK), jnp.float32)

    def first(t, count, buf, at):
        start = order(t, core) * (1 - core) + order(t + count - 1, core) * core
        step = first_pass(buf, at)
        sums = repeat(count * CB, lambda i, carry: step(start * CB + i, carry), (acc[0], acc[1]))
        acc[0], acc[1] = sums
        for t in range(t, t + count):
            q = order(t, core)
            if t < HC:
                outer_send(outer2, t, O2)
                for j in range(1, X):
                    to = lax.rem(chip + j, X)
                    remote(
                        image.at[chip, pl.ds(q * CB, CB)], image.at[chip, pl.ds(q * CB, CB)],
                        IM, recv_sem.at[IM], lat, to * CORES + core,
                    )
            if t >= T - HC:
                inner_send(inner2, 0, t, I2, recv_sem.at[I2])

    def outer_first(count):
        outer_wait(outer1, O1)
        spread_halo(outer1, 0, outer_halo)
        first(0, count, outer1, o_at)

    EARLY, GROUPED = max(HC, T - 3), T // PARTS
    acc[0], acc[1] = zero, zero
    late = jnp.logical_and(lat == 0, core == 0)
    wraps = lat + 2 * core - 1 != other_lat
    prompt = jnp.logical_not(late)
    for t in range(T):
        q = order(t, core)
        if t == 0:
            mine_at = gathered.at[:, pl.ds(pl.multiple_of(rad * slab, 8), slab), :]
            pltpu.make_async_copy(mine_at, mine_at, own_sem).wait()
        arrived(gathered.at[q, pl.ds(0, (R - 1) * slab), :], ag_recv.at[q])
        product = dot(own_rows(chip), gathered[q])
        for i in range(CB):
            value = product[:, i * BLOCK:(i + 1) * BLOCK]
            b = q * CB + i
            outer1[o_at + b] = value
            inner1[i_at + b] = value
            modal[chip, b] = value
        if t == 0:
            pl.when(jnp.logical_not(is_gate))(lambda: pl.semaphore_wait(near_in, 1))
            pl.when(jnp.logical_and(jnp.logical_not(is_gate), wraps))(lambda: pl.semaphore_wait(all_in, 1))
        if t < HC:
            outer_send(outer1, t, O1)
        if t >= T - HC:
            inner_send(inner1, 0, t, I1, recv_sem.at[I1])
        for i in range(CB):
            b = q * CB + i
            spread_at(
                [(outer1, o_at + b), (inner1, i_at + b)], product[:, i * BLOCK:(i + 1) * BLOCK]
            )
        if t < T - 1:
            project_others(t)
        if t == EARLY:
            pl.when(prompt)(functools.partial(outer_first, t - HC + 1))
        if t > EARLY:
            pl.when(prompt)(functools.partial(first, t - HC, 1, outer1, o_at))
    pl.when(late)(functools.partial(outer_first, HC))
    inside = (NB // 2) * (1 - core)
    outside = (NB // 2) * core

    def spread_own(at):
        def step(i, carry):
            b = at + i
            spread_at([(outer2, o_at + b), (inner2, i_at + b)], image[chip, b])
            return carry

        repeat(NB // 2, step, 0, UNROLL)

    spread_own(outside)
    inner_wait(inner1, 0, recv_sem.at[I1])
    spread_halo(inner1, 0, inner_halo)
    for t in range(T - HC, T, GROUPED):
        first(t, GROUPED, inner1, i_at)

    ones = jnp.ones((8, BLOCK), jnp.float32)

    def lanes(values):
        line = lax.dot_general(
            ones, values, (((1,), (1,)), ((), ())), precision=HIGHEST,
            preferred_element_type=jnp.float32,
        )
        width = line.shape[1]
        if width < BLOCK:
            line = jnp.concatenate(
                [line, jnp.zeros((8, BLOCK - width), jnp.float32)], axis=1
            )
        return line[0:1]

    def plane_send(buf, kind):
        for j in range(1, M):
            m, to_lat, to_rad = plane_peer(j)
            remote(buf.at[me], buf.at[me], kind, recv_sem.at[kind], to_lat, to_rad)

    def plane_sum(buf, kind):
        arrived(buf.at[pl.ds(0, M - 1)], recv_sem.at[kind])
        total = buf[0]
        for m in range(1, M):
            total = total + buf[m]
        return total

    s1[me] = lanes(jnp.concatenate([acc[0], acc[1]], axis=0))
    pl.when(jnp.logical_not(jnp.logical_or(is_gate, wraps)))(lambda: pl.semaphore_wait(all_in, 1))
    plane_send(s1, S1)

    mine = jnp.concatenate(
        [
            from_ref[pl.ds(pl.multiple_of(rad * slab, 8), slab), :],
            from_ref[pl.ds(pl.multiple_of(partner * slab, 8), slab), :],
        ],
        axis=0,
    )

    FB = NB // PARTS

    def columns(f):
        return out.at[:, pl.ds(pl.multiple_of(core * half + f * FB * BLOCK, BLOCK), FB * BLOCK)]

    def columns_of(c):
        return out.at[:, pl.ds(c * half, half)]

    def finish(f):
        blocks = []
        for b in range(f * FB, (f + 1) * FB):
            blocks.append(
                jnp.concatenate(
                    [coef[x, 0] * modal[x, b] + coef[x, 1] * image[x, b] for x in range(X)], axis=0
                )
            )
        product = dot(mine, jnp.concatenate(blocks, axis=1))
        part[f, 0] = product[0:slab]
        part[f, 1] = product[slab:K]
        remote(part.at[f, 1], columns(f), OUT, recv_sem.at[OUT], lat, partner)
        pltpu.make_async_copy(part.at[f, 0], columns(f), out_sem).start()

    def second_pass(buf, at, first_block):
        def step(i, carry):
            b = first_block + i
            twice[b] = operate(buf, at, chip, b, image[chip, b])
            return carry

        repeat(NB // 2, step, 0)

    def residual(b, carry):
        final = modal[chip, b] - (coef[chip, 0] * image[chip, b] + coef[chip, 1] * twice[b])
        return carry + final * final

    def chebyshev(x):
        column = jnp.transpose(jnp.broadcast_to(s2[x], (BLOCK, BLOCK)))
        base, power = column[0:K], column[K:2 * K]
        upper = 1.5 * jnp.sqrt(power / (base + 1e-06))
        lower = upper * 0.125
        center = (upper + lower) * 0.5
        half_width = (upper - lower) * 0.5
        sigma = center / half_width
        rho_zero = 1.0 / sigma
        rho_one = 1.0 / (2.0 * sigma - rho_zero)
        second = 2.0 * rho_one / half_width
        coef[x, 0] = (1.0 + rho_one * rho_zero) / center + second
        coef[x, 1] = -second / center

    spread_own(inside)
    inner_wait(inner2, 0, recv_sem.at[I2])
    spread_halo(inner2, 0, inner_halo)
    second_pass(inner2, i_at, inside)
    project_others(T - 1)

    outer_wait(outer2, O2)
    spread_halo(outer2, 0, outer_halo)
    second_pass(outer2, o_at, outside)
    s2[chip] = plane_sum(s1, S1)
    for j in range(1, X):
        x = lax.rem(chip + j, X)
        remote(s2.at[chip], s2.at[chip], S2, recv_sem.at[S2], lat, x * CORES + core)
    chebyshev(chip)
    s3[me] = lanes(repeat(NB, residual, zero))
    plane_send(s3, S3)

    for j in range(1, X):
        x = lax.rem(chip + j, X)
        base = (j - 1) * A * E
        inner_wait(others, base, x_recv.at[j - 1])
        spread_halo(others, base, inner_halo)
    for j in range(1, X):
        x = lax.rem(chip + j, X)
        base = (j - 1) * A * E

        def others_pass(i, carry, x=x, base=base):
            b = inside + i
            image[x, b] = operate(others, base + i_at, x, b, modal[x, b])
            return carry

        repeat(NB // 2, others_pass, 0)

    arrived(s2.at[pl.ds(0, X - 1)], recv_sem.at[S2])
    for j in range(1, X):
        chebyshev(lax.rem(chip + j, X))
    arrived(image.at[pl.ds(0, X - 1), pl.ds(0, HALO)], recv_sem.at[IM])
    for f in range(PARTS):
        finish(f)

    norm = jnp.sqrt(plane_sum(s3, S3) / (s2[chip] + 1e-06))
    res_ref[...] = jnp.where(core == 0, norm[:, 0:slab], norm[:, slab:2 * slab])

    everything = columns_of(0)
    pltpu.make_async_copy(everything, everything, out_sem).wait()
    whole(columns_of(0), OUT, recv_sem.at[OUT]).wait()
    whole(gathered.at[:, pl.ds(0, (R - 1) * slab), :], AG, ag_recv.at[0]).wait_send()
    for kind in (O1, I1, O2, I2):
        whole(outer1.at[pl.ds(0, HALO)], kind, recv_sem.at[kind]).wait_send()
    whole(others.at[pl.ds(0, (X - 1) * HALO)], OT, recv_sem.at[OT]).wait_send()
    whole(image.at[pl.ds(0, X - 1), pl.ds(0, HALO)], IM, recv_sem.at[IM]).wait_send()
    for buf, kind in ((s1, S1), (s3, S3)):
        whole(buf.at[pl.ds(0, M - 1)], kind, recv_sem.at[kind]).wait_send()
    whole(s2.at[pl.ds(0, X - 1)], S2, recv_sem.at[S2]).wait_send()


def on_device(L, R, source, to_modes, from_modes, eigenvalue, shifts, weights, neighbors):
    slab, nodes = source.shape
    S = weights.shape[0]
    levels = to_modes.shape[0]
    T, X, K = CHUNKS, R // CORES, slab * CORES
    half = nodes // CORES
    NB = half // BLOCK
    CW = half // T
    E = NB + HALO
    A = -(-S // GROUP)
    M = L * CORES
    f32 = jnp.float32

    def window(count):
        return pltpu.VMEM((count * A * E, K, BLOCK), f32)

    dma = pltpu.SemaphoreType.DMA
    vmem = pl.BlockSpec(memory_space=pltpu.VMEM)
    hbm = pl.BlockSpec(memory_space=pltpu.HBM)
    smoothed, norm = pl.pallas_call(
        functools.partial(kernel, L, R, S),
        name="smoother",
        out_shape=(
            pltpu.VMEM((slab, nodes), f32),
            pltpu.VMEM((1, slab), f32),
        ),
        in_specs=[hbm] * 7,
        out_specs=(vmem, vmem),
        scratch_shapes=[
            pltpu.VMEM((T, levels, CW), f32),
            pltpu.VMEM((S, half), f32),
            pltpu.VMEM((NB, (A + 1) * GROUP, BLOCK), f32),
            window(1), window(1), window(1), window(1), window(X - 1),
            pltpu.VMEM((X, NB, K, BLOCK), f32),
            pltpu.VMEM((X, NB, K, BLOCK), f32),
            pltpu.VMEM((NB, K, BLOCK), f32),
            pltpu.VMEM((levels, levels), f32),
            pltpu.VMEM((X, 2, K, BLOCK), f32),
            pltpu.VMEM((2, K, BLOCK), f32),
            pltpu.VMEM((PARTS, 2, slab, half // PARTS), f32),
            pltpu.VMEM((NB, BLOCK), f32),
            pltpu.VMEM((M, 1, BLOCK), f32),
            pltpu.VMEM((X, 1, BLOCK), f32),
            pltpu.VMEM((M, 1, BLOCK), f32),
            pltpu.VMEM((levels, levels), f32),
            pltpu.VMEM((levels, levels), f32),
            pltpu.VMEM((1, levels), f32),
            pltpu.SMEM(neighbors.shape, jnp.int32),
            dma((5,)), dma(()), dma(()),
            dma((T,)), dma((X - 1,)),
            dma((11,)), dma((11,)), dma(()), pltpu.SemaphoreType.REGULAR((5,)),
        ],
        compiler_params=pltpu.CompilerParams(
            collective_id=0, has_side_effects=True, vmem_limit_bytes=67043328 - 4 * slab * nodes - 4096
        ),
    )(
        source, weights, to_modes, from_modes, eigenvalue.reshape(1, levels),
        shifts.reshape(nodes // BLOCK, BLOCK), neighbors,
    )
    return smoothed, norm.reshape(slab)


def solution(mesh):
    return jax.shard_map(
        functools.partial(on_device, mesh.shape["lat"], mesh.shape["rad"]),
        mesh=mesh,
        in_specs=(P("rad", "lat"), P(), P(), P(), P("lat"), P(None, "lat"), P(None, "lat")),
        out_specs=(P("rad", "lat"), P("rad")),
        check_vma=False,
    )
```

```python
import functools
import math

import jax
import jax.numpy as jnp
from jax import lax
from jax.experimental import pallas as pl
from jax.experimental.pallas import tpu as pltpu
from jax.sharding import PartitionSpec as P

BLOCK = 128
HALO = 8
CHUNKS = 8
PARTS = 4
NEAR = 2
GROUP = 8
UNROLL = 8
STEP = 2
CORES = 2
HIGHEST = lax.Precision.HIGHEST
MESH = pl.DeviceIdType.MESH


def dot(a, b):
    return jnp.dot(a, b, precision=HIGHEST, preferred_element_type=jnp.float32)


def repeat(count, step, carry, most=UNROLL):
    width = math.gcd(count, most)

    def trip(n, carry):
        for j in range(width):
            carry = step(n * width + j, carry)
        return carry

    if count == width:
        return trip(0, carry)
    return lax.fori_loop(0, count // width, trip, carry)


def kernel(
    L, R, S,
    src, w_hbm, to_hbm, from_hbm, eig_hbm, shift_hbm, nbr_hbm,
    out, res_ref,
    gathered, wv, wr, far_wv, far_wr, far, outer1, inner1, outer2, inner2, others, modal, image, twice, eig_t, coef, acc, part,
    rows, far_rows, s1, s2, s3, to_ref, from_ref, eig_ref, nbr_ref, far_nbr,
    in_sem, own_sem, w_sem, ag_recv, x_recv, send_sem, recv_sem, out_sem, passed,
):
    T = CHUNKS
    X = R // CORES
    M = L * CORES
    slab, nodes = src.shape
    K = slab * CORES
    half = nodes // CORES
    NB = half // BLOCK
    CB = NB // T
    HC = HALO // CB
    CW = CB * BLOCK
    E = NB + HALO
    F = NEAR + 2 * HALO
    NC = NEAR // CB
    A = -(-S // GROUP)
    lat = lax.axis_index("lat")
    rad = lax.axis_index("rad")
    core = lax.rem(rad, CORES)
    chip = lax.div(rad, CORES)
    partner = chip * CORES + (1 - core)
    me = lat * CORES + core
    other_lat = lax.rem(lat + (L - 1) * (1 - core) + core, L)
    wraps = lat + 2 * core - 1 != other_lat

    def order(t, c):
        return t * (1 - c) + (T - 1 - t) * c

    def own_copy(q):
        return pltpu.make_async_copy(
            src.at[:, pl.ds(pl.multiple_of(core * half + q * CW, BLOCK), CW)],
            gathered.at[q, pl.ds(pl.multiple_of(rad * slab, 8), slab), :],
            own_sem,
        )

    w_copy = pltpu.make_async_copy(
        w_hbm.at[:, pl.ds(pl.multiple_of(core * half, BLOCK), half)], wv, w_sem
    )
    inputs = [
        pltpu.make_async_copy(a, b, in_sem.at[i])
        for i, (a, b) in enumerate([
            (to_hbm, to_ref), (from_hbm, from_ref), (eig_hbm, eig_ref), (nbr_hbm, nbr_ref),
            (shift_hbm.at[pl.ds(pl.multiple_of(core * NB, 8), NB), :], rows),
        ])
    ]

    def plane_peer(j):
        m = lax.rem(me + j, M)
        return m, lax.div(m, CORES), chip * CORES + lax.rem(m, CORES)

    barrier = pltpu.get_barrier_semaphore()
    up, down, met, near_in, all_in = [passed.at[i] for i in range(5)]
    gate = R - 1
    is_gate = rad == gate
    below, above = lat >= STEP, lat + STEP < L
    around = [(lat >= d, -d) for d in range(1, STEP + 1)] + [(lat + d < L, d) for d in range(1, STEP + 1)]

    def signal(sem, to_lat, to_rad):
        pl.semaphore_signal(
            sem, inc=1, device_id={"lat": to_lat, "rad": to_rad}, device_id_type=MESH
        )

    def signal_below(sem):
        pl.when(below)(lambda: signal(sem, lat - STEP, gate))

    def signal_above(sem):
        pl.when(above)(lambda: signal(sem, lat + STEP, gate))

    for j in range(1, R):
        r = lax.rem(rad + j, R)
        pl.when(r != gate)(functools.partial(signal, barrier, lat, r))
    w_copy.start()
    for copy in inputs:
        copy.start()
    for q in range(T):
        own_copy(q).start()

    @pl.when(jnp.logical_not(is_gate))
    def _():
        pl.semaphore_wait(barrier, R - 1)
        pl.when(partner == gate)(lambda: signal(met, lat, gate))

    @pl.when(is_gate)
    def _():
        pl.semaphore_wait(met, 1)
        for there, d in around:
            pl.when(there)(functools.partial(signal, barrier, lat + d, gate))

    AG, O1, I1, O2, I2, OT, IM, S1, S2, S3, OUT, FAR, FAR_W, FAR_ROWS, FAR_NBR = range(15)

    def remote(src_ref, dst_ref, kind, recv, lat_to, rad_to):
        pltpu.make_async_remote_copy(
            src_ref=src_ref, dst_ref=dst_ref, send_sem=send_sem.at[kind], recv_sem=recv,
            device_id={"lat": lat_to, "rad": rad_to}, device_id_type=MESH,
        ).start()

    def whole(ref, kind, recv):
        return pltpu.make_async_remote_copy(
            src_ref=ref, dst_ref=ref, send_sem=send_sem.at[kind], recv_sem=recv,
            device_id={"lat": lat, "rad": partner}, device_id_type=MESH,
        )

    def arrived(ref, recv):
        whole(ref, AG, recv).wait_recv()

    def slot(q, r):
        return gathered.at[q, pl.ds(pl.multiple_of(r * slab, 8), slab), :]

    for t in range(T):
        for j in range(1, R):
            to = lax.rem(rad + j, R)
            to_core = lax.rem(to, CORES)
            q = order(t, to_core)
            remote(
                src.at[:, pl.ds(pl.multiple_of(to_core * half + q * CW, BLOCK), CW)],
                slot(q, rad), AG, ag_recv.at[q], lat, to,
            )

    w_copy.wait()
    for copy in inputs:
        copy.wait()
    row_id = lax.broadcasted_iota(jnp.int32, (A * GROUP, BLOCK), 0)

    def prepare_from(raw, shift, row_at, ready, b):
        ready[b, pl.ds((A - 1) * GROUP, GROUP), :] = jnp.zeros((GROUP, BLOCK), jnp.float32)
        ready[b, pl.ds(0, S), :] = raw[:, pl.ds(pl.multiple_of(b * BLOCK, BLOCK), BLOCK)]
        tile = ready[b, pl.ds(0, A * GROUP), :]
        placed = tile
        for c in range(1, GROUP):
            placed = jnp.where(lax.rem(row_id, GROUP) == c, pltpu.roll(tile, c, 1), placed)
        ready[b, pl.ds(0, A * GROUP), :] = placed
        diagonal = jnp.sum(tile, axis=0, keepdims=True) + shift[pl.ds(row_at + b, 1), :]
        ready[b, pl.ds(A * GROUP, GROUP), :] = jnp.broadcast_to(diagonal, (GROUP, BLOCK))

    def prepare(b, carry):
        prepare_from(wv, rows, 0, wr, b)
        return carry

    row_tile = far_rows.shape[0]

    def prepare_far(b, carry):
        prepare_from(far_wv, far_rows, (row_tile - NEAR) * (1 - core), far_wr, b)
        return carry

    far_inputs = ((far_wv, FAR_W), (far_rows, FAR_ROWS), (far_nbr, FAR_NBR))

    def far_start():
        parts = (
            w_hbm.at[:, pl.ds(pl.multiple_of(core * (nodes - NEAR * BLOCK), BLOCK), NEAR * BLOCK)],
            shift_hbm.at[pl.ds(pl.multiple_of(core * (nodes // BLOCK - row_tile), 8), row_tile), :],
            nbr_hbm,
        )
        for part_ref, (ref, kind) in zip(parts, far_inputs):
            remote(part_ref, ref, kind, recv_sem.at[kind], other_lat, partner)

    def far_ready():
        for ref, kind in far_inputs:
            arrived(ref, recv_sem.at[kind])
        repeat(NEAR, prepare_far, 0)

    repeat(NB, prepare, 0)

    @pl.when(is_gate)
    def _():
        pl.semaphore_wait(barrier, sum(there.astype(jnp.int32) for there, _ in around))
        for r in range(R - 1):
            signal(near_in, lat, r)
        pl.when(jnp.logical_not(wraps))(far_start)
        pl.when(jnp.logical_not(below))(lambda: signal_above(up))
        pl.when(jnp.logical_not(above))(lambda: signal_below(down))

        @pl.when(below)
        def _():
            pl.semaphore_wait(up, 1)
            signal_above(up)

        @pl.when(above)
        def _():
            pl.semaphore_wait(down, 1)
            signal_below(down)

        for r in range(R - 1):
            signal(all_in, lat, r)

    @pl.when(jnp.logical_not(is_gate))
    def _():
        pl.semaphore_wait(near_in, 1)
        pl.when(jnp.logical_not(wraps))(far_start)

    levels = to_ref.shape[0]
    eig_t[...] = jnp.transpose(jnp.broadcast_to(eig_ref[...], (levels, levels)))

    o_at = HALO * (1 - core)
    i_at = HALO * core

    def outer_dst(c, q):
        return (1 - c) * (NB + q * CB) + c * (q * CB - NB + HALO)

    def inner_dst(c, q):
        return c * (NB + q * CB) + (1 - c) * (q * CB - NB + HALO)

    outer_halo = core * NB
    inner_halo = (1 - core) * NB

    def outer_send(buf, t, kind):
        q = order(t, core)
        remote(
            buf.at[pl.ds(o_at + q * CB, CB)], buf.at[pl.ds(outer_dst(core, q), CB)],
            kind, recv_sem.at[kind], other_lat, partner,
        )

    def outer_wait(buf, skip, kind):
        arrived(buf.at[pl.ds(outer_halo + core * skip, HALO - skip)], recv_sem.at[kind])

    def inner_send(buf, base, t, kind, recv):
        q = order(t, core)
        remote(
            buf.at[pl.ds(base + i_at + q * CB, CB)],
            buf.at[pl.ds(base + inner_dst(core, q), CB)],
            kind, recv, lat, partner,
        )

    def inner_wait(buf, base, recv):
        arrived(buf.at[pl.ds(base + inner_halo, HALO)], recv)

    def spread_at(targets, value):
        for a in range(1, A):
            moved = pltpu.roll(value, BLOCK - a * GROUP, 1)
            for buf, stride, k in targets:
                buf[a * stride + k] = moved

    def spread_halo(buf, base, at, count=HALO):
        def step(k, carry):
            spread_at([(buf, E, base + at + k)], buf[base + at + k])
            return carry

        repeat(count, step, 0)

    far_own = (NEAR + HALO) * (1 - core) - (NB - HALO) * core
    far_halo = NEAR * (1 - core) + HALO * core
    far_more = 2 * HALO * core

    def far_at(b):
        return b + HALO * (1 - core) - (NB - NEAR - HALO) * core

    def far_send(t):
        q = order(t, core)
        remote(
            outer1.at[pl.ds(o_at + q * CB, CB)], far.at[pl.ds(far_at(q * CB), CB)],
            FAR, recv_sem.at[FAR], other_lat, partner,
        )

    def spread_outer_halo():
        def step(k, carry):
            value = outer1[outer_halo + k]
            far[far_halo + k] = value
            spread_at([(outer1, E, outer_halo + k), (far, F, far_halo + k)], value)
            return carry

        repeat(HALO, step, 0)

    def far_pass():
        arrived(far.at[pl.ds(far_more, NEAR)], recv_sem.at[FAR])

        def spread_more(k, carry):
            spread_at([(far, F, far_more + k)], far[far_more + k])
            return carry

        def step(i, carry):
            at = HALO + i
            column = (nodes // BLOCK - NEAR) * (1 - core) + i
            value = operate(far, F, at, far_wr, i, far_nbr, column, chip, far[at])
            k = outer_halo + (HALO - NEAR) * (1 - core) + i
            outer2[k] = value
            spread_at([(outer2, E, k)], value)
            return carry

        repeat(NEAR, spread_more, 0)
        repeat(NEAR, step, 0)

    def own_rows(x):
        return to_ref[pl.ds(pl.multiple_of(x * K, 8), K), :]

    def project_others(t):
        q = order(t, core)
        for j in range(1, X):
            x = lax.rem(chip + j, X)
            base = (j - 1) * A * E
            product = dot(own_rows(x), gathered[q])
            for i in range(CB):
                value = product[:, i * BLOCK:(i + 1) * BLOCK]
                modal[x, q * CB + i] = value
                others[base + i_at + q * CB + i] = value
            if t >= T - HC:
                inner_send(others, base, t, OT, x_recv.at[j - 1])
            for i in range(CB):
                spread_at(
                    [(others, E, base + i_at + q * CB + i)], product[:, i * BLOCK:(i + 1) * BLOCK]
                )

    def operate(buf, stride, at, weight, b, table, column, x, field):
        total = None
        for c in range(GROUP):
            inner = None
            for a in range(A):
                s = a * GROUP + c
                if s < S:
                    n = table[s, column]
                    term = buf[a * stride + at + n] * weight[b, pl.ds(s, 1), :]
                    inner = term if inner is None else inner + term
            if inner is not None:
                moved = inner if c == 0 else pltpu.roll(inner, BLOCK - c, 1)
                total = moved if total is None else total + moved
        eig = eig_t[pl.ds(pl.multiple_of(x * K, 8), K), :]
        return (weight[b, pl.ds(A * GROUP, 1), :] + eig) * field - total

    def operate_own(buf, base, x, b, field):
        return operate(buf, E, base + b, wr, b, nbr_ref, core * NB + b, x, field)

    def first_pass(buf, at):
        def step(b, carry):
            field = modal[chip, b]
            value = operate_own(buf, at, chip, b, field)
            outer2[o_at + b] = value
            inner2[i_at + b] = value
            image[chip, b] = value
            return (carry[0] + field * field, carry[1] + value * value)

        return step

    zero = jnp.zeros((K, BLOCK), jnp.float32)

    def image_send(t):
        q = order(t, core)
        for j in range(1, X):
            to = lax.rem(chip + j, X)
            remote(
                image.at[chip, pl.ds(q * CB, CB)], image.at[chip, pl.ds(q * CB, CB)],
                IM, recv_sem.at[IM], lat, to * CORES + core,
            )

    def first(t, count, buf, at):
        start = order(t, core) * (1 - core) + order(t + count - 1, core) * core
        step = first_pass(buf, at)
        sums = repeat(count * CB, lambda i, carry: step(start * CB + i, carry), (acc[0], acc[1]))
        acc[0], acc[1] = sums
        for t in range(t, t + count):
            q = order(t, core)
            if NC <= t < HC:
                outer_send(outer2, t, O2)
            if t < HC // 2:
                image_send(t)
            if t >= T - HC:
                inner_send(inner2, 0, t, I2, recv_sem.at[I2])

    def outer_first(count):
        outer_wait(outer1, 0, O1)
        spread_outer_halo()
        first(0, count, outer1, o_at)

    EARLY, GROUPED, READY = max(HC, T - 3), T // PARTS, HC - 1
    acc[0], acc[1] = zero, zero
    late = jnp.logical_and(lat == 0, core == 0)
    prompt = jnp.logical_not(late)
    for t in range(T):
        q = order(t, core)
        if t == 0:
            mine_at = gathered.at[:, pl.ds(pl.multiple_of(rad * slab, 8), slab), :]
            pltpu.make_async_copy(mine_at, mine_at, own_sem).wait()
        arrived(gathered.at[q, pl.ds(0, (R - 1) * slab), :], ag_recv.at[q])
        product = dot(own_rows(chip), gathered[q])
        for i in range(CB):
            value = product[:, i * BLOCK:(i + 1) * BLOCK]
            b = q * CB + i
            outer1[o_at + b] = value
            inner1[i_at + b] = value
            modal[chip, b] = value
            if t < HC:
                far[far_own + b] = value
        if t == 0:
            pl.when(jnp.logical_and(jnp.logical_not(is_gate), wraps))(lambda: pl.semaphore_wait(all_in, 1))
        if t < HC:
            outer_send(outer1, t, O1)
        elif t < HC + NC:
            pl.when(prompt)(functools.partial(far_send, t))
        if t >= T - HC:
            inner_send(inner1, 0, t, I1, recv_sem.at[I1])
        for i in range(CB):
            b = q * CB + i
            spread_at(
                [(outer1, E, o_at + b), (inner1, E, i_at + b)]
                + ([(far, F, far_own + b)] if t < HC else []),
                product[:, i * BLOCK:(i + 1) * BLOCK],
            )
        if t < T - 1:
            project_others(t)
        if t == READY:
            pl.when(jnp.logical_not(wraps))(far_ready)
        if t == HC + NC - 1:
            pl.when(jnp.logical_and(prompt, wraps))(far_start)
        if t == EARLY:

            @pl.when(late)
            def _():
                for n in range(HC, HC + NC):
                    far_send(n)
                far_start()

            pl.when(prompt)(functools.partial(outer_first, t - HC + 1))
        if t > EARLY:
            pl.when(prompt)(functools.partial(first, t - HC, 1, outer1, o_at))

    pl.when(late)(functools.partial(outer_first, HC))
    inside = (NB // 2) * (1 - core)
    outside = (NB // 2) * core

    def spread_own(at):
        def step(i, carry):
            b = at + i
            spread_at([(outer2, E, o_at + b), (inner2, E, i_at + b)], image[chip, b])
            return carry

        repeat(NB // 2, step, 0, UNROLL)

    spread_own(outside)
    inner_wait(inner1, 0, recv_sem.at[I1])
    spread_halo(inner1, 0, inner_halo)
    for t in range(T - HC, T, GROUPED):
        first(t, GROUPED, inner1, i_at)

    ones = jnp.ones((8, BLOCK), jnp.float32)

    def lanes(values):
        line = lax.dot_general(
            ones, values, (((1,), (1,)), ((), ())), precision=HIGHEST,
            preferred_element_type=jnp.float32,
        )
        width = line.shape[1]
        if width < BLOCK:
            line = jnp.concatenate(
                [line, jnp.zeros((8, BLOCK - width), jnp.float32)], axis=1
            )
        return line[0:1]

    def plane_send(ref, kind):
        for j in range(1, M):
            m, to_lat, to_rad = plane_peer(j)
            remote(ref, ref, kind, recv_sem.at[kind], to_lat, to_rad)

    def plane_sum(buf):
        total = buf[0]
        for m in range(1, M):
            total = total + buf[m]
        return total

    def cross_send():
        def step(n, carry):
            to = lax.rem(chip + 1 + lax.div(n, M), X)
            m = lax.rem(me + lax.rem(n, M), M)
            remote(
                s1.at[chip, me], s1.at[chip, me], S2, recv_sem.at[S2],
                lax.div(m, CORES), to * CORES + lax.rem(m, CORES),
            )
            return carry

        lax.fori_loop(0, (X - 1) * M, step, 0)

    s1[chip, me] = lanes(jnp.concatenate([acc[0], acc[1]], axis=0))
    pl.when(jnp.logical_not(jnp.logical_or(is_gate, wraps)))(lambda: pl.semaphore_wait(all_in, 1))
    plane_send(s1.at[chip, me], S1)
    cross_send()
    for t in range(HC // 2, HC):
        image_send(t)

    mine = jnp.concatenate(
        [
            from_ref[pl.ds(pl.multiple_of(rad * slab, 8), slab), :],
            from_ref[pl.ds(pl.multiple_of(partner * slab, 8), slab), :],
        ],
        axis=0,
    )

    FB = NB // PARTS

    def columns(f):
        return out.at[:, pl.ds(pl.multiple_of(core * half + f * FB * BLOCK, BLOCK), FB * BLOCK)]

    def columns_of(c):
        return out.at[:, pl.ds(c * half, half)]

    def finish(f):
        blocks = []
        for b in range(f * FB, (f + 1) * FB):
            blocks.append(
                jnp.concatenate(
                    [coef[x, 0] * modal[x, b] + coef[x, 1] * image[x, b] for x in range(X)], axis=0
                )
            )
        product = dot(mine, jnp.concatenate(blocks, axis=1))
        part[f, 0] = product[0:slab]
        part[f, 1] = product[slab:K]
        remote(part.at[f, 1], columns(f), OUT, recv_sem.at[OUT], lat, partner)
        pltpu.make_async_copy(part.at[f, 0], columns(f), out_sem).start()

    def second_pass(buf, at, first_block):
        def step(i, carry):
            b = first_block + i
            twice[b] = operate_own(buf, at, chip, b, image[chip, b])
            return carry

        repeat(NB // 2, step, 0)

    def residual(b, carry):
        final = modal[chip, b] - (coef[chip, 0] * image[chip, b] + coef[chip, 1] * twice[b])
        return carry + final * final

    def chebyshev(x):
        s2[x] = plane_sum(s1.at[x])
        column = jnp.transpose(jnp.broadcast_to(s2[x], (BLOCK, BLOCK)))
        base, power = column[0:K], column[K:2 * K]
        upper = 1.5 * jnp.sqrt(power / (base + 1e-06))
        lower = upper * 0.125
        center = (upper + lower) * 0.5
        half_width = (upper - lower) * 0.5
        sigma = center / half_width
        rho_zero = 1.0 / sigma
        rho_one = 1.0 / (2.0 * sigma - rho_zero)
        second = 2.0 * rho_one / half_width
        coef[x, 0] = (1.0 + rho_one * rho_zero) / center + second
        coef[x, 1] = -second / center

    spread_own(inside)
    inner_wait(inner2, 0, recv_sem.at[I2])
    spread_halo(inner2, 0, inner_halo)
    second_pass(inner2, i_at, inside)
    project_others(T - 1)

    pl.when(wraps)(far_ready)
    far_pass()
    outer_wait(outer2, NEAR, O2)
    spread_halo(outer2, 0, outer_halo + core * NEAR, HALO - NEAR)
    second_pass(outer2, o_at, outside)
    arrived(s1.at[0, pl.ds(0, M - 1)], recv_sem.at[S1])
    chebyshev(chip)
    s3[me] = lanes(repeat(NB, residual, zero))
    plane_send(s3.at[me], S3)

    for j in range(1, X):
        x = lax.rem(chip + j, X)
        base = (j - 1) * A * E
        inner_wait(others, base, x_recv.at[j - 1])
        spread_halo(others, base, inner_halo)
    for j in range(1, X):
        x = lax.rem(chip + j, X)
        base = (j - 1) * A * E

        def others_pass(i, carry, x=x, base=base):
            b = inside + i
            image[x, b] = operate_own(others, base + i_at, x, b, modal[x, b])
            return carry

        repeat(NB // 2, others_pass, 0)

    arrived(s1.at[pl.ds(0, X - 1)], recv_sem.at[S2])
    for j in range(1, X):
        chebyshev(lax.rem(chip + j, X))
    arrived(image.at[pl.ds(0, X - 1), pl.ds(0, HALO)], recv_sem.at[IM])
    for f in range(PARTS):
        finish(f)

    arrived(s3.at[pl.ds(0, M - 1)], recv_sem.at[S3])
    norm = jnp.sqrt(plane_sum(s3) / (s2[chip] + 1e-06))
    res_ref[...] = jnp.where(core == 0, norm[:, 0:slab], norm[:, slab:2 * slab])

    everything = columns_of(0)
    pltpu.make_async_copy(everything, everything, out_sem).wait()
    whole(columns_of(0), OUT, recv_sem.at[OUT]).wait()
    whole(gathered.at[:, pl.ds(0, (R - 1) * slab), :], AG, ag_recv.at[0]).wait_send()
    for kind in (O1, I1, I2):
        whole(outer1.at[pl.ds(0, HALO)], kind, recv_sem.at[kind]).wait_send()
    whole(outer1.at[pl.ds(0, HALO - NEAR)], O2, recv_sem.at[O2]).wait_send()
    whole(outer1.at[pl.ds(0, NEAR)], FAR, recv_sem.at[FAR]).wait_send()
    for ref, kind in far_inputs:
        whole(ref, kind, recv_sem.at[kind]).wait_send()
    whole(others.at[pl.ds(0, (X - 1) * HALO)], OT, recv_sem.at[OT]).wait_send()
    whole(image.at[pl.ds(0, X - 1), pl.ds(0, HALO)], IM, recv_sem.at[IM]).wait_send()
    for kind in (S1, S3):
        whole(s3.at[pl.ds(0, M - 1)], kind, recv_sem.at[kind]).wait_send()
    whole(s1.at[pl.ds(0, X - 1)], S2, recv_sem.at[S2]).wait_send()


def on_device(L, R, source, to_modes, from_modes, eigenvalue, shifts, weights, neighbors):
    slab, nodes = source.shape
    S = weights.shape[0]
    levels = to_modes.shape[0]
    T, X, K = CHUNKS, R // CORES, slab * CORES
    half = nodes // CORES
    NB = half // BLOCK
    CW = half // T
    E = NB + HALO
    A = -(-S // GROUP)
    M = L * CORES
    f32 = jnp.float32

    def window(count):
        return pltpu.VMEM((count * A * E, K, BLOCK), f32)

    dma = pltpu.SemaphoreType.DMA
    vmem = pl.BlockSpec(memory_space=pltpu.VMEM)
    hbm = pl.BlockSpec(memory_space=pltpu.HBM)
    smoothed, norm = pl.pallas_call(
        functools.partial(kernel, L, R, S),
        name="smoother",
        out_shape=(
            pltpu.VMEM((slab, nodes), f32),
            pltpu.VMEM((1, slab), f32),
        ),
        in_specs=[hbm] * 7,
        out_specs=(vmem, vmem),
        scratch_shapes=[
            pltpu.VMEM((T, levels, CW), f32),
            pltpu.VMEM((S, half), f32),
            pltpu.VMEM((NB, (A + 1) * GROUP, BLOCK), f32),
            pltpu.VMEM((S, NEAR * BLOCK), f32),
            pltpu.VMEM((NEAR, (A + 1) * GROUP, BLOCK), f32),
            pltpu.VMEM((A * (NEAR + 2 * HALO), K, BLOCK), f32),
            window(1), window(1), window(1), window(1), window(X - 1),
            pltpu.VMEM((X, NB, K, BLOCK), f32),
            pltpu.VMEM((X, NB, K, BLOCK), f32),
            pltpu.VMEM((NB, K, BLOCK), f32),
            pltpu.VMEM((levels, levels), f32),
            pltpu.VMEM((X, 2, K, BLOCK), f32),
            pltpu.VMEM((2, K, BLOCK), f32),
            pltpu.VMEM((PARTS, 2, slab, half // PARTS), f32),
            pltpu.VMEM((NB, BLOCK), f32),
            pltpu.VMEM((GROUP, BLOCK), f32),
            pltpu.VMEM((X, M, 1, BLOCK), f32),
            pltpu.VMEM((X, 1, BLOCK), f32),
            pltpu.VMEM((M, 1, BLOCK), f32),
            pltpu.VMEM((levels, levels), f32),
            pltpu.VMEM((levels, levels), f32),
            pltpu.VMEM((1, levels), f32),
            pltpu.SMEM(neighbors.shape, jnp.int32),
            pltpu.SMEM(neighbors.shape, jnp.int32),
            dma((5,)), dma(()), dma(()),
            dma((T,)), dma((X - 1,)),
            dma((15,)), dma((15,)), dma(()), pltpu.SemaphoreType.REGULAR((5,)),
        ],
        compiler_params=pltpu.CompilerParams(
            collective_id=0, has_side_effects=True, vmem_limit_bytes=67043328 - 4 * slab * nodes - 4096
        ),
    )(
        source, weights, to_modes, from_modes, eigenvalue.reshape(1, levels),
        shifts.reshape(nodes // BLOCK, BLOCK), neighbors,
    )
    return smoothed, norm.reshape(slab)


def solution(mesh):
    return jax.shard_map(
        functools.partial(on_device, mesh.shape["lat"], mesh.shape["rad"]),
        mesh=mesh,
        in_specs=(P("rad", "lat"), P(), P(), P(), P("lat"), P(None, "lat"), P(None, "lat")),
        out_specs=(P("rad", "lat"), P("rad")),
        check_vma=False,
    )
```

```python
import functools

import jax
import jax.numpy as jnp
from jax import lax
from jax.experimental import pallas as pl
from jax.experimental.pallas import tpu as pltpu
from jax.sharding import PartitionSpec as P

BLOCK = 128
HALO = 8
CHUNKS = 8
PARTS = 4
NEAR = 2
GROUP = 8
UNROLL = 8
STEP = 2
CORES = 2
HIGHEST = lax.Precision.HIGHEST
MESH = pl.DeviceIdType.MESH


def halves(v):
    high = v.astype(jnp.bfloat16)
    return high, (v - high.astype(jnp.float32)).astype(jnp.bfloat16)


def dot(a, b):
    (a_high, a_low), (b_high, b_low) = halves(a), halves(b)
    left = jnp.concatenate([a_high, a_high], axis=1)
    right = jnp.concatenate([b_high, b_low], axis=0)
    return jnp.dot(left, right, preferred_element_type=jnp.float32) + jnp.dot(
        a_low, b_high, preferred_element_type=jnp.float32
    )


def repeat(count, step, carry, most=UNROLL):
    width = max(n for n in range(1, min(count, most) + 1) if count % n == 0)

    def trip(n, carry):
        for j in range(width):
            carry = step(n * width + j, carry)
        return carry

    if count == width:
        return trip(0, carry)
    return lax.fori_loop(0, count // width, trip, carry)


def kernel(
    L, R, S,
    src, w_hbm, to_hbm, from_hbm, eig_hbm, shift_hbm, nbr_hbm,
    out, res_ref,
    gathered, wv, wr, far_wv, far_wr, far, outer1, inner1, outer2, inner2, others, modal, image, twice, eig_t, coef, acc, part,
    rows, far_rows, s1, s2, s3, to_ref, from_ref, eig_ref, nbr_ref, far_nbr,
    in_sem, own_sem, w_sem, ag_recv, x_recv, send_sem, recv_sem, out_sem, passed,
):
    T = CHUNKS
    X = R // CORES
    M = L * CORES
    slab, nodes = src.shape
    K = slab * CORES
    half = nodes // CORES
    NB = half // BLOCK
    CB = NB // T
    HC = HALO // CB
    CW = CB * BLOCK
    E = NB + HALO
    F = NEAR + 2 * HALO
    NC = NEAR // CB
    A = -(-S // GROUP)
    lat = lax.axis_index("lat")
    rad = lax.axis_index("rad")
    core = lax.rem(rad, CORES)
    chip = lax.div(rad, CORES)
    partner = chip * CORES + (1 - core)
    me = lat * CORES + core
    other_lat = lax.rem(lat + (L - 1) * (1 - core) + core, L)
    wraps = lat + 2 * core - 1 != other_lat

    def order(t, c):
        return t * (1 - c) + (T - 1 - t) * c

    def own_copy(q):
        return pltpu.make_async_copy(
            src.at[:, pl.ds(pl.multiple_of(core * half + q * CW, BLOCK), CW)],
            gathered.at[q, pl.ds(pl.multiple_of(rad * slab, 8), slab), :],
            own_sem,
        )

    w_copy = pltpu.make_async_copy(
        w_hbm.at[:, pl.ds(pl.multiple_of(core * half, BLOCK), half)], wv, w_sem
    )
    inputs = [
        pltpu.make_async_copy(a, b, in_sem.at[i])
        for i, (a, b) in enumerate([
            (to_hbm, to_ref), (from_hbm, from_ref), (eig_hbm, eig_ref), (nbr_hbm, nbr_ref),
            (shift_hbm.at[pl.ds(pl.multiple_of(core * NB, 8), NB), :], rows),
        ])
    ]

    def plane_peer(j):
        m = lax.rem(me + j, M)
        return m, lax.div(m, CORES), chip * CORES + lax.rem(m, CORES)

    barrier = pltpu.get_barrier_semaphore()
    up, down, met, near_in, all_in = [passed.at[i] for i in range(5)]
    gate = R - 1
    is_gate = rad == gate
    below, above = lat >= STEP, lat + STEP < L
    around = [(lat >= d, -d) for d in range(1, STEP + 1)] + [(lat + d < L, d) for d in range(1, STEP + 1)]

    def signal(sem, to_lat, to_rad):
        pl.semaphore_signal(
            sem, inc=1, device_id={"lat": to_lat, "rad": to_rad}, device_id_type=MESH
        )

    def signal_below(sem):
        pl.when(below)(lambda: signal(sem, lat - STEP, gate))

    def signal_above(sem):
        pl.when(above)(lambda: signal(sem, lat + STEP, gate))

    for j in range(1, R):
        r = lax.rem(rad + j, R)
        pl.when(r != gate)(functools.partial(signal, barrier, lat, r))
    w_copy.start()
    for copy in inputs:
        copy.start()
    for q in range(T):
        own_copy(q).start()

    @pl.when(jnp.logical_not(is_gate))
    def _():
        pl.semaphore_wait(barrier, R - 1)
        pl.when(partner == gate)(lambda: signal(met, lat, gate))

    @pl.when(is_gate)
    def _():
        pl.semaphore_wait(met, 1)
        for there, d in around:
            pl.when(there)(functools.partial(signal, barrier, lat + d, gate))

    AG, O1, I1, O2, I2, OT, IM, S1, S2, S3, OUT, FAR, FAR_W, FAR_ROWS, FAR_NBR = range(15)

    def remote(src_ref, dst_ref, kind, recv, lat_to, rad_to):
        pltpu.make_async_remote_copy(
            src_ref=src_ref, dst_ref=dst_ref, send_sem=send_sem.at[kind], recv_sem=recv,
            device_id={"lat": lat_to, "rad": rad_to}, device_id_type=MESH,
        ).start()

    def whole(ref, kind, recv):
        return pltpu.make_async_remote_copy(
            src_ref=ref, dst_ref=ref, send_sem=send_sem.at[kind], recv_sem=recv,
            device_id={"lat": lat, "rad": partner}, device_id_type=MESH,
        )

    def arrived(ref, recv):
        whole(ref, AG, recv).wait_recv()

    def slot(q, r):
        return gathered.at[q, pl.ds(pl.multiple_of(r * slab, 8), slab), :]

    for t in range(T):
        for j in range(1, R):
            to = lax.rem(rad + j, R)
            to_core = lax.rem(to, CORES)
            q = order(t, to_core)
            remote(
                src.at[:, pl.ds(pl.multiple_of(to_core * half + q * CW, BLOCK), CW)],
                slot(q, rad), AG, ag_recv.at[q], lat, to,
            )

    w_copy.wait()
    for copy in inputs:
        copy.wait()
    row_id = lax.broadcasted_iota(jnp.int32, (A * GROUP, BLOCK), 0)

    def prepare_from(raw, shift, row_at, ready, b):
        ready[b, pl.ds((A - 1) * GROUP, GROUP), :] = jnp.zeros((GROUP, BLOCK), jnp.float32)
        ready[b, pl.ds(0, S), :] = raw[:, pl.ds(pl.multiple_of(b * BLOCK, BLOCK), BLOCK)]
        tile = ready[b, pl.ds(0, A * GROUP), :]
        placed = tile
        for c in range(1, GROUP):
            placed = jnp.where(lax.rem(row_id, GROUP) == c, pltpu.roll(tile, c, 1), placed)
        ready[b, pl.ds(0, A * GROUP), :] = placed
        diagonal = jnp.sum(tile, axis=0, keepdims=True) + shift[pl.ds(row_at + b, 1), :]
        ready[b, pl.ds(A * GROUP, GROUP), :] = jnp.broadcast_to(diagonal, (GROUP, BLOCK))

    def prepare(b, carry):
        prepare_from(wv, rows, 0, wr, b)
        return carry

    row_tile = far_rows.shape[0]

    def prepare_far(b, carry):
        prepare_from(far_wv, far_rows, (row_tile - NEAR) * (1 - core), far_wr, b)
        return carry

    far_inputs = ((far_wv, FAR_W), (far_rows, FAR_ROWS), (far_nbr, FAR_NBR))

    def far_start():
        parts = (
            w_hbm.at[:, pl.ds(pl.multiple_of(core * (nodes - NEAR * BLOCK), BLOCK), NEAR * BLOCK)],
            shift_hbm.at[pl.ds(pl.multiple_of(core * (nodes // BLOCK - row_tile), 8), row_tile), :],
            nbr_hbm,
        )
        for part_ref, (ref, kind) in zip(parts, far_inputs):
            remote(part_ref, ref, kind, recv_sem.at[kind], other_lat, partner)

    def far_ready():
        for ref, kind in far_inputs:
            arrived(ref, recv_sem.at[kind])
        repeat(NEAR, prepare_far, 0)

    repeat(NB, prepare, 0)

    @pl.when(is_gate)
    def _():
        pl.semaphore_wait(barrier, sum(there.astype(jnp.int32) for there, _ in around))
        for r in range(R - 1):
            signal(near_in, lat, r)
        pl.when(jnp.logical_not(wraps))(far_start)
        pl.when(jnp.logical_not(below))(lambda: signal_above(up))
        pl.when(jnp.logical_not(above))(lambda: signal_below(down))

        @pl.when(below)
        def _():
            pl.semaphore_wait(up, 1)
            signal_above(up)

        @pl.when(above)
        def _():
            pl.semaphore_wait(down, 1)
            signal_below(down)

        for r in range(R - 1):
            signal(all_in, lat, r)

    @pl.when(jnp.logical_not(is_gate))
    def _():
        pl.semaphore_wait(near_in, 1)
        pl.when(jnp.logical_not(wraps))(far_start)

    levels = to_ref.shape[0]
    eig_t[...] = jnp.transpose(jnp.broadcast_to(eig_ref[...], (levels, levels)))

    o_at = HALO * (1 - core)
    i_at = HALO * core

    def outer_dst(c, q):
        return (1 - c) * (NB + q * CB) + c * (q * CB - NB + HALO)

    def inner_dst(c, q):
        return c * (NB + q * CB) + (1 - c) * (q * CB - NB + HALO)

    outer_halo = core * NB
    inner_halo = (1 - core) * NB

    def outer_send(buf, t, kind):
        q = order(t, core)
        remote(
            buf.at[pl.ds(o_at + q * CB, CB)], buf.at[pl.ds(outer_dst(core, q), CB)],
            kind, recv_sem.at[kind], other_lat, partner,
        )

    def outer_wait(buf, skip, kind):
        arrived(buf.at[pl.ds(outer_halo + core * skip, HALO - skip)], recv_sem.at[kind])

    def inner_send(buf, base, t, kind, recv):
        q = order(t, core)
        remote(
            buf.at[pl.ds(base + i_at + q * CB, CB)],
            buf.at[pl.ds(base + inner_dst(core, q), CB)],
            kind, recv, lat, partner,
        )

    def inner_wait(buf, base, recv):
        arrived(buf.at[pl.ds(base + inner_halo, HALO)], recv)

    def spread_at(targets, value):
        for a in range(1, A):
            moved = pltpu.roll(value, BLOCK - a * GROUP, 1)
            for buf, stride, k in targets:
                buf[a * stride + k] = moved

    def spread_halo(buf, base, at, count=HALO):
        def step(k, carry):
            spread_at([(buf, E, base + at + k)], buf[base + at + k])
            return carry

        repeat(count, step, 0)

    far_own = (NEAR + HALO) * (1 - core) - (NB - HALO) * core
    far_halo = NEAR * (1 - core) + HALO * core
    far_more = 2 * HALO * core

    def far_at(b):
        return b + HALO * (1 - core) - (NB - NEAR - HALO) * core

    def far_send(t):
        q = order(t, core)
        remote(
            outer1.at[pl.ds(o_at + q * CB, CB)], far.at[pl.ds(far_at(q * CB), CB)],
            FAR, recv_sem.at[FAR], other_lat, partner,
        )

    def spread_outer_halo():
        def step(k, carry):
            value = outer1[outer_halo + k]
            far[far_halo + k] = value
            spread_at([(outer1, E, outer_halo + k), (far, F, far_halo + k)], value)
            return carry

        repeat(HALO, step, 0)

    def far_pass():
        arrived(far.at[pl.ds(far_more, NEAR)], recv_sem.at[FAR])

        def spread_more(k, carry):
            spread_at([(far, F, far_more + k)], far[far_more + k])
            return carry

        def step(i, carry):
            at = HALO + i
            column = (nodes // BLOCK - NEAR) * (1 - core) + i
            value = operate(far, F, at, far_wr, i, far_nbr, column, chip, far[at])
            k = outer_halo + (HALO - NEAR) * (1 - core) + i
            outer2[k] = value
            spread_at([(outer2, E, k)], value)
            return carry

        repeat(NEAR, spread_more, 0)
        repeat(NEAR, step, 0)

    def own_rows(x):
        return to_ref[pl.ds(pl.multiple_of(x * K, 8), K), :]

    def project_others(t):
        q = order(t, core)
        for j in range(1, X):
            x = lax.rem(chip + j, X)
            base = (j - 1) * A * E
            product = dot(own_rows(x), gathered[q])
            for i in range(CB):
                value = product[:, i * BLOCK:(i + 1) * BLOCK]
                modal[x, q * CB + i] = value
                others[base + i_at + q * CB + i] = value
            if t >= T - HC:
                inner_send(others, base, t, OT, x_recv.at[j - 1])
            for i in range(CB):
                spread_at(
                    [(others, E, base + i_at + q * CB + i)], product[:, i * BLOCK:(i + 1) * BLOCK]
                )

    def operate(buf, stride, at, weight, b, table, column, x, field):
        total = None
        for c in range(GROUP):
            inner = None
            for a in range(A):
                s = a * GROUP + c
                if s < S:
                    n = table[s, column]
                    term = buf[a * stride + at + n] * weight[b, pl.ds(s, 1), :]
                    inner = term if inner is None else inner + term
            if inner is not None:
                moved = inner if c == 0 else pltpu.roll(inner, BLOCK - c, 1)
                total = moved if total is None else total + moved
        eig = eig_t[pl.ds(pl.multiple_of(x * K, 8), K), :]
        return (weight[b, pl.ds(A * GROUP, 1), :] + eig) * field - total

    def operate_own(buf, base, x, b, field):
        return operate(buf, E, base + b, wr, b, nbr_ref, core * NB + b, x, field)

    def first_pass(buf, at):
        def step(b, carry):
            field = modal[chip, b]
            value = operate_own(buf, at, chip, b, field)
            outer2[o_at + b] = value
            inner2[i_at + b] = value
            image[chip, b] = value
            return (carry[0] + field * field, carry[1] + value * value)

        return step

    zero = jnp.zeros((K, BLOCK), jnp.float32)

    def image_send(t):
        q = order(t, core)
        for j in range(1, X):
            to = lax.rem(chip + j, X)
            remote(
                image.at[chip, pl.ds(q * CB, CB)], image.at[chip, pl.ds(q * CB, CB)],
                IM, recv_sem.at[IM], lat, to * CORES + core,
            )

    def first(t, count, buf, at):
        start = order(t, core) * (1 - core) + order(t + count - 1, core) * core
        step = first_pass(buf, at)
        sums = repeat(count * CB, lambda i, carry: step(start * CB + i, carry), (acc[0], acc[1]))
        acc[0], acc[1] = sums
        for t in range(t, t + count):
            q = order(t, core)
            if NC <= t < HC:
                outer_send(outer2, t, O2)
            if t < HC // 2:
                image_send(t)
            if t >= T - HC:
                inner_send(inner2, 0, t, I2, recv_sem.at[I2])

    def outer_first(count):
        outer_wait(outer1, 0, O1)
        spread_outer_halo()
        for t in range(NC, count):
            first(t, 1, outer1, o_at)
        if count == HC:
            first(0, NC, outer1, o_at)

    LAST = 2
    EARLY, GROUPED, READY = max(HC, T - 3), T // PARTS, HC - 1
    acc[0], acc[1] = zero, zero
    late = jnp.logical_and(lat == 0, core == 0)
    prompt = jnp.logical_not(late)
    for t in range(T):
        q = order(t, core)
        if t == 0:
            mine_at = gathered.at[:, pl.ds(pl.multiple_of(rad * slab, 8), slab), :]
            pltpu.make_async_copy(mine_at, mine_at, own_sem).wait()
        arrived(gathered.at[q, pl.ds(0, (R - 1) * slab), :], ag_recv.at[q])
        product = dot(own_rows(chip), gathered[q])
        for i in range(CB):
            value = product[:, i * BLOCK:(i + 1) * BLOCK]
            b = q * CB + i
            outer1[o_at + b] = value
            inner1[i_at + b] = value
            modal[chip, b] = value
            if t < HC:
                far[far_own + b] = value
        if t == 0:
            pl.when(jnp.logical_and(jnp.logical_not(is_gate), wraps))(lambda: pl.semaphore_wait(all_in, 1))
        if t < HC:
            outer_send(outer1, t, O1)
        elif t < HC + NC:
            pl.when(prompt)(functools.partial(far_send, t))
        if t >= T - HC:
            inner_send(inner1, 0, t, I1, recv_sem.at[I1])
        for i in range(CB):
            b = q * CB + i
            spread_at(
                [(outer1, E, o_at + b), (inner1, E, i_at + b)]
                + ([(far, F, far_own + b)] if t < HC else []),
                product[:, i * BLOCK:(i + 1) * BLOCK],
            )
        if t < T - LAST:
            project_others(t)
        if t == READY:
            pl.when(jnp.logical_not(wraps))(far_ready)
        if t == HC + NC - 1:
            pl.when(jnp.logical_and(prompt, wraps))(far_start)
        if t == EARLY:

            @pl.when(late)
            def _():
                for n in range(HC, HC + NC):
                    far_send(n)
                far_start()

            pl.when(prompt)(functools.partial(outer_first, t - HC + 1))
        if t > EARLY:
            pl.when(prompt)(functools.partial(first, t - HC, 1, outer1, o_at))
        if t == T - 1:
            pl.when(prompt)(functools.partial(first, 0, NC, outer1, o_at))

    pl.when(late)(functools.partial(outer_first, HC))
    inside = (NB // 2) * (1 - core)
    outside = (NB // 2) * core

    def spread_own(at):
        def step(i, carry):
            b = at + i
            spread_at([(outer2, E, o_at + b), (inner2, E, i_at + b)], image[chip, b])
            return carry

        repeat(NB // 2, step, 0, UNROLL)

    spread_own(outside)
    inner_wait(inner1, 0, recv_sem.at[I1])
    spread_halo(inner1, 0, inner_halo)
    for t in range(T - HC, T, GROUPED):
        first(t, GROUPED, inner1, i_at)

    ones = jnp.ones((8, 2 * BLOCK), jnp.bfloat16)

    def lanes(values):
        line = lax.dot_general(
            ones, jnp.concatenate(halves(values), axis=1), (((1,), (1,)), ((), ())),
            preferred_element_type=jnp.float32,
        )
        width = line.shape[1]
        if width < BLOCK:
            line = jnp.concatenate(
                [line, jnp.zeros((8, BLOCK - width), jnp.float32)], axis=1
            )
        return line[0:1]

    def plane_send(ref, kind):
        for j in range(1, M):
            m, to_lat, to_rad = plane_peer(j)
            remote(ref, ref, kind, recv_sem.at[kind], to_lat, to_rad)

    def plane_sum(buf):
        total = buf[0]
        for m in range(1, M):
            total = total + buf[m]
        return total

    def cross_send():
        def step(n, carry):
            to = lax.rem(chip + 1 + lax.div(n, M), X)
            m = lax.rem(me + lax.rem(n, M), M)
            remote(
                s1.at[chip, me], s1.at[chip, me], S2, recv_sem.at[S2],
                lax.div(m, CORES), to * CORES + lax.rem(m, CORES),
            )
            return carry

        lax.fori_loop(0, (X - 1) * M, step, 0)

    s1[chip, me] = lanes(jnp.concatenate([acc[0], acc[1]], axis=0))
    pl.when(jnp.logical_not(jnp.logical_or(is_gate, wraps)))(lambda: pl.semaphore_wait(all_in, 1))
    plane_send(s1.at[chip, me], S1)
    cross_send()
    for t in range(HC // 2, HC):
        image_send(t)

    mine = jnp.concatenate(
        [
            from_ref[pl.ds(pl.multiple_of(rad * slab, 8), slab), :],
            from_ref[pl.ds(pl.multiple_of(partner * slab, 8), slab), :],
        ],
        axis=0,
    )

    FB = NB // PARTS

    def columns(f):
        return out.at[:, pl.ds(pl.multiple_of(core * half + f * FB * BLOCK, BLOCK), FB * BLOCK)]

    def columns_of(c):
        return out.at[:, pl.ds(c * half, half)]

    def finish(f):
        blocks = []
        for i in range(FB):
            b = f * FB + i
            blocks.append(
                jnp.concatenate(
                    [coef[x, 0] * modal[x, b] + coef[x, 1] * image[x, b] for x in range(X)], axis=0
                )
            )
        product = dot(mine, jnp.concatenate(blocks, axis=1))
        part[f, 0] = product[0:slab]
        part[f, 1] = product[slab:K]
        remote(part.at[f, 1], columns(f), OUT, recv_sem.at[OUT], lat, partner)
        pltpu.make_async_copy(part.at[f, 0], columns(f), out_sem).start()

    def second_pass(buf, at, first_block):
        def step(i, carry):
            b = first_block + i
            twice[b] = operate_own(buf, at, chip, b, image[chip, b])
            return carry

        repeat(NB // 2, step, 0)

    def residual(b, carry):
        final = modal[chip, b] - (coef[chip, 0] * image[chip, b] + coef[chip, 1] * twice[b])
        return carry + final * final

    def chebyshev(x):
        s2[x] = plane_sum(s1.at[x])
        column = jnp.transpose(jnp.broadcast_to(s2[x], (BLOCK, BLOCK)))
        base, power = column[0:K], column[K:2 * K]
        upper = 1.5 * jnp.sqrt(power / (base + 1e-06))
        lower = upper * 0.125
        center = (upper + lower) * 0.5
        half_width = (upper - lower) * 0.5
        sigma = center / half_width
        rho_zero = 1.0 / sigma
        rho_one = 1.0 / (2.0 * sigma - rho_zero)
        second = 2.0 * rho_one / half_width
        coef[x, 0] = (1.0 + rho_one * rho_zero) / center + second
        coef[x, 1] = -second / center

    spread_own(inside)
    inner_wait(inner2, 0, recv_sem.at[I2])
    spread_halo(inner2, 0, inner_halo)
    second_pass(inner2, i_at, inside)
    def others_image():
        for t in range(T - LAST, T):
            project_others(t)
        for j in range(1, X):
            x = lax.rem(chip + j, X)
            base = (j - 1) * A * E
            inner_wait(others, base, x_recv.at[j - 1])
            spread_halo(others, base, inner_halo)
        for j in range(1, X):
            x = lax.rem(chip + j, X)
            base = (j - 1) * A * E

            def others_pass(i, carry, x=x, base=base):
                b = inside + i
                image[x, b] = operate_own(others, base + i_at, x, b, modal[x, b])
                return carry

            repeat(NB // 2, others_pass, 0)

    pl.when(wraps)(far_ready)
    far_pass()
    pl.when(lat == 0)(others_image)
    outer_wait(outer2, NEAR, O2)
    spread_halo(outer2, 0, outer_halo + core * NEAR, HALO - NEAR)
    second_pass(outer2, o_at, outside)
    arrived(s1.at[0, pl.ds(0, M - 1)], recv_sem.at[S1])
    chebyshev(chip)
    s3[me] = lanes(repeat(NB, residual, zero))
    plane_send(s3.at[me], S3)

    arrived(s1.at[pl.ds(0, X - 1)], recv_sem.at[S2])
    for j in range(1, X):
        chebyshev(lax.rem(chip + j, X))
    arrived(image.at[pl.ds(0, X - 1), pl.ds(0, HALO)], recv_sem.at[IM])
    for f in range(PARTS // 2):
        finish(f + (PARTS // 2) * core)
    pl.when(lat != 0)(others_image)
    for f in range(PARTS // 2):
        finish(f + (PARTS // 2) * (1 - core))

    arrived(s3.at[pl.ds(0, M - 1)], recv_sem.at[S3])
    norm = jnp.sqrt(plane_sum(s3) / (s2[chip] + 1e-06))
    res_ref[...] = jnp.where(core == 0, norm[:, 0:slab], norm[:, slab:2 * slab])

    everything = columns_of(0)
    pltpu.make_async_copy(everything, everything, out_sem).wait()
    whole(columns_of(0), OUT, recv_sem.at[OUT]).wait()
    whole(gathered.at[:, pl.ds(0, (R - 1) * slab), :], AG, ag_recv.at[0]).wait_send()
    for kind in (O1, I1, I2):
        whole(outer1.at[pl.ds(0, HALO)], kind, recv_sem.at[kind]).wait_send()
    whole(outer1.at[pl.ds(0, HALO - NEAR)], O2, recv_sem.at[O2]).wait_send()
    whole(outer1.at[pl.ds(0, NEAR)], FAR, recv_sem.at[FAR]).wait_send()
    for ref, kind in far_inputs:
        whole(ref, kind, recv_sem.at[kind]).wait_send()
    whole(others.at[pl.ds(0, (X - 1) * HALO)], OT, recv_sem.at[OT]).wait_send()
    whole(image.at[pl.ds(0, X - 1), pl.ds(0, HALO)], IM, recv_sem.at[IM]).wait_send()
    for kind in (S1, S3):
        whole(s3.at[pl.ds(0, M - 1)], kind, recv_sem.at[kind]).wait_send()
    whole(s1.at[pl.ds(0, X - 1)], S2, recv_sem.at[S2]).wait_send()


def on_device(L, R, source, to_modes, from_modes, eigenvalue, shifts, weights, neighbors):
    slab, nodes = source.shape
    S = weights.shape[0]
    levels = to_modes.shape[0]
    T, X, K = CHUNKS, R // CORES, slab * CORES
    half = nodes // CORES
    NB = half // BLOCK
    CW = half // T
    E = NB + HALO
    A = -(-S // GROUP)
    M = L * CORES
    f32 = jnp.float32

    def window(count):
        return pltpu.VMEM((count * A * E, K, BLOCK), f32)

    dma = pltpu.SemaphoreType.DMA
    vmem = pl.BlockSpec(memory_space=pltpu.VMEM)
    hbm = pl.BlockSpec(memory_space=pltpu.HBM)
    smoothed, norm = pl.pallas_call(
        functools.partial(kernel, L, R, S),
        name="smoother",
        out_shape=(
            pltpu.VMEM((slab, nodes), f32),
            pltpu.VMEM((1, slab), f32),
        ),
        in_specs=[hbm] * 7,
        out_specs=(vmem, vmem),
        scratch_shapes=[
            pltpu.VMEM((T, levels, CW), f32),
            pltpu.VMEM((S, half), f32),
            pltpu.VMEM((NB, (A + 1) * GROUP, BLOCK), f32),
            pltpu.VMEM((S, NEAR * BLOCK), f32),
            pltpu.VMEM((NEAR, (A + 1) * GROUP, BLOCK), f32),
            pltpu.VMEM((A * (NEAR + 2 * HALO), K, BLOCK), f32),
            window(1), window(1), window(1), window(1), window(X - 1),
            pltpu.VMEM((X, NB, K, BLOCK), f32),
            pltpu.VMEM((X, NB, K, BLOCK), f32),
            pltpu.VMEM((NB, K, BLOCK), f32),
            pltpu.VMEM((levels, levels), f32),
            pltpu.VMEM((X, 2, K, BLOCK), f32),
            pltpu.VMEM((2, K, BLOCK), f32),
            pltpu.VMEM((PARTS, 2, slab, half // PARTS), f32),
            pltpu.VMEM((NB, BLOCK), f32),
            pltpu.VMEM((GROUP, BLOCK), f32),
            pltpu.VMEM((X, M, 1, BLOCK), f32),
            pltpu.VMEM((X, 1, BLOCK), f32),
            pltpu.VMEM((M, 1, BLOCK), f32),
            pltpu.VMEM((levels, levels), f32),
            pltpu.VMEM((levels, levels), f32),
            pltpu.VMEM((1, levels), f32),
            pltpu.SMEM(neighbors.shape, jnp.int32),
            pltpu.SMEM(neighbors.shape, jnp.int32),
            dma((5,)), dma(()), dma(()),
            dma((T,)), dma((X - 1,)),
            dma((15,)), dma((15,)), dma(()), pltpu.SemaphoreType.REGULAR((5,)),
        ],
        compiler_params=pltpu.CompilerParams(
            collective_id=0, has_side_effects=True, vmem_limit_bytes=67043328 - 4 * slab * nodes - 4096
        ),
    )(
        source, weights, to_modes, from_modes, eigenvalue.reshape(1, levels),
        shifts.reshape(nodes // BLOCK, BLOCK), neighbors,
    )
    return smoothed, norm.reshape(slab)


def solution(mesh):
    return jax.shard_map(
        functools.partial(on_device, mesh.shape["lat"], mesh.shape["rad"]),
        mesh=mesh,
        in_specs=(P("rad", "lat"), P(), P(), P(), P("lat"), P(None, "lat"), P(None, "lat")),
        out_specs=(P("rad", "lat"), P("rad")),
        check_vma=False,
    )
```

```python
import functools

import jax
import jax.numpy as jnp
from jax import lax
from jax.experimental import pallas as pl
from jax.experimental.pallas import tpu as pltpu
from jax.sharding import PartitionSpec as P

BLOCK = 128
HALO = 8
CHUNKS = 8
PARTS = 4
NEAR = 2
GROUP = 8
UNROLL = 8
STEP = 2
CORES = 2
HIGHEST = lax.Precision.HIGHEST
MESH = pl.DeviceIdType.MESH


def halves(v):
    high = v.astype(jnp.bfloat16)
    return high, (v - high.astype(jnp.float32)).astype(jnp.bfloat16)


def dot(a, b):
    (a_high, a_low), (b_high, b_low) = halves(a), halves(b)
    left = jnp.concatenate([a_high, a_high], axis=1)
    right = jnp.concatenate([b_high, b_low], axis=0)
    return jnp.dot(left, right, preferred_element_type=jnp.float32) + jnp.dot(
        a_low, b_high, preferred_element_type=jnp.float32
    )


def repeat(count, step, carry, most=UNROLL):
    width = max(n for n in range(1, min(count, most) + 1) if count % n == 0)

    def trip(n, carry):
        for j in range(width):
            carry = step(n * width + j, carry)
        return carry

    if count == width:
        return trip(0, carry)
    return lax.fori_loop(0, count // width, trip, carry)


def kernel(
    L, R, S,
    src, w_hbm, to_hbm, from_hbm, eig_hbm, shift_hbm, nbr_hbm,
    out, res_ref,
    gathered, wv, wr, far_wv, far_wr, far, outer1, inner1, outer2, inner2, others, modal, image, twice, eig_t, coef, acc, part,
    rows, far_rows, s1, s2, s3, to_ref, from_ref, eig_ref, nbr_ref, far_nbr,
    in_sem, own_sem, w_sem, ag_recv, x_recv, send_sem, recv_sem, out_sem, passed,
):
    T = CHUNKS
    X = R // CORES
    M = L * CORES
    slab, nodes = src.shape
    K = slab * CORES
    half = nodes // CORES
    NB = half // BLOCK
    CB = NB // T
    HC = HALO // CB
    CW = CB * BLOCK
    E = NB + HALO
    F = NEAR + 2 * HALO
    NC = NEAR // CB
    A = -(-S // GROUP)
    lat = lax.axis_index("lat")
    rad = lax.axis_index("rad")
    core = lax.rem(rad, CORES)
    chip = lax.div(rad, CORES)
    partner = chip * CORES + (1 - core)
    me = lat * CORES + core
    other_lat = lax.rem(lat + (L - 1) * (1 - core) + core, L)
    wraps = lat + 2 * core - 1 != other_lat

    def order(t, c):
        return t * (1 - c) + (T - 1 - t) * c

    def own_copy(q):
        return pltpu.make_async_copy(
            src.at[:, pl.ds(pl.multiple_of(core * half + q * CW, BLOCK), CW)],
            gathered.at[q, pl.ds(pl.multiple_of(rad * slab, 8), slab), :],
            own_sem,
        )

    w_copy = pltpu.make_async_copy(
        w_hbm.at[:, pl.ds(pl.multiple_of(core * half, BLOCK), half)], wv, w_sem
    )
    inputs = [
        pltpu.make_async_copy(a, b, in_sem.at[i])
        for i, (a, b) in enumerate([
            (to_hbm, to_ref), (from_hbm, from_ref), (eig_hbm, eig_ref), (nbr_hbm, nbr_ref),
            (shift_hbm.at[pl.ds(pl.multiple_of(core * NB, 8), NB), :], rows),
        ])
    ]

    def plane_peer(j):
        m = lax.rem(me + j, M)
        return m, lax.div(m, CORES), chip * CORES + lax.rem(m, CORES)

    barrier = pltpu.get_barrier_semaphore()
    up, down, met, near_in, all_in = [passed.at[i] for i in range(5)]
    gate = R - 1
    is_gate = rad == gate
    below, above = lat >= STEP, lat + STEP < L
    around = [(lat >= d, -d) for d in range(1, STEP + 1)] + [(lat + d < L, d) for d in range(1, STEP + 1)]

    def signal(sem, to_lat, to_rad):
        pl.semaphore_signal(
            sem, inc=1, device_id={"lat": to_lat, "rad": to_rad}, device_id_type=MESH
        )

    def signal_below(sem):
        pl.when(below)(lambda: signal(sem, lat - STEP, gate))

    def signal_above(sem):
        pl.when(above)(lambda: signal(sem, lat + STEP, gate))

    for j in range(1, R):
        r = lax.rem(rad + j, R)
        pl.when(r != gate)(functools.partial(signal, barrier, lat, r))
    w_copy.start()
    for copy in inputs:
        copy.start()
    for q in range(T):
        own_copy(q).start()

    @pl.when(jnp.logical_not(is_gate))
    def _():
        pl.semaphore_wait(barrier, R - 1)
        pl.when(partner == gate)(lambda: signal(met, lat, gate))

    @pl.when(is_gate)
    def _():
        pl.semaphore_wait(met, 1)
        for there, d in around:
            pl.when(there)(functools.partial(signal, barrier, lat + d, gate))

    AG, O1, I1, O2, I2, OT, IM, S1, S2, S3, OUT, FAR, FAR_W, FAR_ROWS, FAR_NBR = range(15)

    def remote(src_ref, dst_ref, kind, recv, lat_to, rad_to):
        pltpu.make_async_remote_copy(
            src_ref=src_ref, dst_ref=dst_ref, send_sem=send_sem.at[kind], recv_sem=recv,
            device_id={"lat": lat_to, "rad": rad_to}, device_id_type=MESH,
        ).start()

    def whole(ref, kind, recv):
        return pltpu.make_async_remote_copy(
            src_ref=ref, dst_ref=ref, send_sem=send_sem.at[kind], recv_sem=recv,
            device_id={"lat": lat, "rad": partner}, device_id_type=MESH,
        )

    def arrived(ref, recv):
        whole(ref, AG, recv).wait_recv()

    def slot(q, r):
        return gathered.at[q, pl.ds(pl.multiple_of(r * slab, 8), slab), :]

    for t in range(T):
        for j in range(1, R):
            to = lax.rem(rad + j, R)
            to_core = lax.rem(to, CORES)
            q = order(t, to_core)
            remote(
                src.at[:, pl.ds(pl.multiple_of(to_core * half + q * CW, BLOCK), CW)],
                slot(q, rad), AG, ag_recv.at[q], lat, to,
            )

    w_copy.wait()
    for copy in inputs:
        copy.wait()
    row_id = lax.broadcasted_iota(jnp.int32, (A * GROUP, BLOCK), 0)

    def prepare_from(raw, shift, row_at, ready, b):
        ready[b, pl.ds((A - 1) * GROUP, GROUP), :] = jnp.zeros((GROUP, BLOCK), jnp.float32)
        ready[b, pl.ds(0, S), :] = raw[:, pl.ds(pl.multiple_of(b * BLOCK, BLOCK), BLOCK)]
        tile = ready[b, pl.ds(0, A * GROUP), :]
        placed = tile
        for c in range(1, GROUP):
            placed = jnp.where(lax.rem(row_id, GROUP) == c, pltpu.roll(tile, c, 1), placed)
        ready[b, pl.ds(0, A * GROUP), :] = placed
        diagonal = jnp.sum(tile, axis=0, keepdims=True) + shift[pl.ds(row_at + b, 1), :]
        ready[b, pl.ds(A * GROUP, GROUP), :] = jnp.broadcast_to(diagonal, (GROUP, BLOCK))

    def prepare(b, carry):
        prepare_from(wv, rows, 0, wr, b)
        return carry

    row_tile = far_rows.shape[0]

    def prepare_far(b, carry):
        prepare_from(far_wv, far_rows, (row_tile - NEAR) * (1 - core), far_wr, b)
        return carry

    far_inputs = ((far_wv, FAR_W), (far_rows, FAR_ROWS), (far_nbr, FAR_NBR))

    def far_start():
        parts = (
            w_hbm.at[:, pl.ds(pl.multiple_of(core * (nodes - NEAR * BLOCK), BLOCK), NEAR * BLOCK)],
            shift_hbm.at[pl.ds(pl.multiple_of(core * (nodes // BLOCK - row_tile), 8), row_tile), :],
            nbr_hbm,
        )
        for part_ref, (ref, kind) in zip(parts, far_inputs):
            remote(part_ref, ref, kind, recv_sem.at[kind], other_lat, partner)

    def far_ready():
        for ref, kind in far_inputs:
            arrived(ref, recv_sem.at[kind])
        repeat(NEAR, prepare_far, 0)

    repeat(NB, prepare, 0)

    @pl.when(is_gate)
    def _():
        pl.semaphore_wait(barrier, sum(there.astype(jnp.int32) for there, _ in around))
        for r in range(R - 1):
            signal(near_in, lat, r)
        pl.when(jnp.logical_not(wraps))(far_start)
        pl.when(jnp.logical_not(below))(lambda: signal_above(up))
        pl.when(jnp.logical_not(above))(lambda: signal_below(down))

        @pl.when(below)
        def _():
            pl.semaphore_wait(up, 1)
            signal_above(up)

        @pl.when(above)
        def _():
            pl.semaphore_wait(down, 1)
            signal_below(down)

        for r in range(R - 1):
            signal(all_in, lat, r)

    @pl.when(jnp.logical_not(is_gate))
    def _():
        pl.semaphore_wait(near_in, 1)
        pl.when(jnp.logical_not(wraps))(far_start)

    levels = to_ref.shape[0]
    eig_t[...] = jnp.transpose(jnp.broadcast_to(eig_ref[...], (levels, levels)))

    o_at = HALO * (1 - core)
    i_at = HALO * core

    def outer_dst(c, q):
        return (1 - c) * (NB + q * CB) + c * (q * CB - NB + HALO)

    def inner_dst(c, q):
        return c * (NB + q * CB) + (1 - c) * (q * CB - NB + HALO)

    outer_halo = core * NB
    inner_halo = (1 - core) * NB

    def outer_send(buf, t, kind):
        q = order(t, core)
        remote(
            buf.at[pl.ds(o_at + q * CB, CB)], buf.at[pl.ds(outer_dst(core, q), CB)],
            kind, recv_sem.at[kind], other_lat, partner,
        )

    def outer_wait(buf, skip, kind):
        arrived(buf.at[pl.ds(outer_halo + core * skip, HALO - skip)], recv_sem.at[kind])

    def inner_send(buf, base, t, kind, recv):
        q = order(t, core)
        remote(
            buf.at[pl.ds(base + i_at + q * CB, CB)],
            buf.at[pl.ds(base + inner_dst(core, q), CB)],
            kind, recv, lat, partner,
        )

    def inner_wait(buf, base, recv):
        arrived(buf.at[pl.ds(base + inner_halo, HALO)], recv)

    def spread_at(targets, value):
        for a in range(1, A):
            moved = pltpu.roll(value, BLOCK - a * GROUP, 1)
            for buf, stride, k in targets:
                buf[a * stride + k] = moved

    def spread_halo(buf, base, at, count=HALO):
        def step(k, carry):
            spread_at([(buf, E, base + at + k)], buf[base + at + k])
            return carry

        repeat(count, step, 0)

    far_own = (NEAR + HALO) * (1 - core) - (NB - HALO) * core
    far_halo = NEAR * (1 - core) + HALO * core
    far_more = 2 * HALO * core

    def far_at(b):
        return b + HALO * (1 - core) - (NB - NEAR - HALO) * core

    def far_send(t):
        q = order(t, core)
        remote(
            outer1.at[pl.ds(o_at + q * CB, CB)], far.at[pl.ds(far_at(q * CB), CB)],
            FAR, recv_sem.at[FAR], other_lat, partner,
        )

    def spread_outer_halo():
        def step(k, carry):
            value = outer1[outer_halo + k]
            far[far_halo + k] = value
            spread_at([(outer1, E, outer_halo + k), (far, F, far_halo + k)], value)
            return carry

        repeat(HALO, step, 0)

    def far_pass():
        arrived(far.at[pl.ds(far_more, NEAR)], recv_sem.at[FAR])

        def spread_more(k, carry):
            spread_at([(far, F, far_more + k)], far[far_more + k])
            return carry

        def step(i, carry):
            at = HALO + i
            column = (nodes // BLOCK - NEAR) * (1 - core) + i
            value = operate(far, F, at, far_wr, i, far_nbr, column, chip, far[at])
            k = outer_halo + (HALO - NEAR) * (1 - core) + i
            outer2[k] = value
            spread_at([(outer2, E, k)], value)
            return carry

        repeat(NEAR, spread_more, 0)
        repeat(NEAR, step, 0)

    def own_rows(x):
        return to_ref[pl.ds(pl.multiple_of(x * K, 8), K), :]

    def project_others(t):
        q = order(t, core)
        for j in range(1, X):
            x = lax.rem(chip + j, X)
            base = (j - 1) * A * E
            product = dot(own_rows(x), gathered[q])
            for i in range(CB):
                value = product[:, i * BLOCK:(i + 1) * BLOCK]
                modal[x, q * CB + i] = value
                others[base + i_at + q * CB + i] = value
            if t >= T - HC:
                inner_send(others, base, t, OT, x_recv.at[j - 1])
            for i in range(CB):
                spread_at(
                    [(others, E, base + i_at + q * CB + i)], product[:, i * BLOCK:(i + 1) * BLOCK]
                )

    def operate(buf, stride, at, weight, b, table, column, x, field):
        total = None
        for c in range(GROUP):
            inner = None
            for a in range(A):
                s = a * GROUP + c
                if s < S:
                    n = table[s, column]
                    term = buf[a * stride + at + n] * weight[b, pl.ds(s, 1), :]
                    inner = term if inner is None else inner + term
            if inner is not None:
                moved = inner if c == 0 else pltpu.roll(inner, BLOCK - c, 1)
                total = moved if total is None else total + moved
        eig = eig_t[pl.ds(pl.multiple_of(x * K, 8), K), :]
        return (weight[b, pl.ds(A * GROUP, 1), :] + eig) * field - total

    def operate_own(buf, base, x, b, field):
        return operate(buf, E, base + b, wr, b, nbr_ref, core * NB + b, x, field)

    def first_pass(buf, at):
        def step(b, carry):
            field = modal[chip, b]
            value = operate_own(buf, at, chip, b, field)
            outer2[o_at + b] = value
            inner2[i_at + b] = value
            image[chip, b] = value
            return (carry[0] + field * field, carry[1] + value * value)

        return step

    zero = jnp.zeros((K, BLOCK), jnp.float32)

    def image_send(t):
        q = order(t, core)
        for j in range(1, X):
            to = lax.rem(chip + j, X)
            remote(
                image.at[chip, pl.ds(q * CB, CB)], image.at[chip, pl.ds(q * CB, CB)],
                IM, recv_sem.at[IM], lat, to * CORES + core,
            )

    def first(t, count, buf, at):
        start = order(t, core) * (1 - core) + order(t + count - 1, core) * core
        step = first_pass(buf, at)
        sums = repeat(count * CB, lambda i, carry: step(start * CB + i, carry), (acc[0], acc[1]))
        acc[0], acc[1] = sums
        for t in range(t, t + count):
            q = order(t, core)
            if NC <= t < HC:
                outer_send(outer2, t, O2)
            if t < HC // 2:
                image_send(t)
            if t >= T - HC:
                inner_send(inner2, 0, t, I2, recv_sem.at[I2])

    def outer_first(count):
        outer_wait(outer1, 0, O1)
        spread_outer_halo()
        for t in range(NC, count):
            first(t, 1, outer1, o_at)
        if count == HC:
            first(0, NC, outer1, o_at)

    LAST, EARLY, GROUPED, READY = T // 4, T * 11 // 16, T // PARTS, HC - 1
    acc[0], acc[1] = zero, zero
    late = jnp.logical_and(lat == 0, core == 0)
    prompt = jnp.logical_not(late)
    for t in range(T):
        q = order(t, core)
        if t == 0:
            mine_at = gathered.at[:, pl.ds(pl.multiple_of(rad * slab, 8), slab), :]
            pltpu.make_async_copy(mine_at, mine_at, own_sem).wait()
        arrived(gathered.at[q, pl.ds(0, (R - 1) * slab), :], ag_recv.at[q])
        product = dot(own_rows(chip), gathered[q])
        for i in range(CB):
            value = product[:, i * BLOCK:(i + 1) * BLOCK]
            b = q * CB + i
            outer1[o_at + b] = value
            inner1[i_at + b] = value
            modal[chip, b] = value
            if t < HC:
                far[far_own + b] = value
        if t == 0:
            pl.when(jnp.logical_and(jnp.logical_not(is_gate), wraps))(lambda: pl.semaphore_wait(all_in, 1))
        if t < HC:
            outer_send(outer1, t, O1)
        elif t < HC + NC:
            pl.when(prompt)(functools.partial(far_send, t))
        if t >= T - HC:
            inner_send(inner1, 0, t, I1, recv_sem.at[I1])
        for i in range(CB):
            b = q * CB + i
            spread_at(
                [(outer1, E, o_at + b), (inner1, E, i_at + b)]
                + ([(far, F, far_own + b)] if t < HC else []),
                product[:, i * BLOCK:(i + 1) * BLOCK],
            )
        if t < T - LAST:
            project_others(t)
        if t == READY:
            pl.when(jnp.logical_not(wraps))(far_ready)
        if t == HC + NC - 1:
            pl.when(jnp.logical_and(prompt, wraps))(far_start)
        if t == EARLY:

            @pl.when(late)
            def _():
                for n in range(HC, HC + NC):
                    far_send(n)
                far_start()

            pl.when(prompt)(functools.partial(outer_first, t - HC + 1))
        if t > EARLY:
            pl.when(prompt)(functools.partial(first, t - HC, 1, outer1, o_at))
        if t == T - 1:
            pl.when(prompt)(functools.partial(first, 0, NC, outer1, o_at))

    pl.when(late)(functools.partial(outer_first, HC))
    inside = (NB // 2) * (1 - core)
    outside = (NB // 2) * core

    def spread_own(at):
        def step(i, carry):
            b = at + i
            spread_at([(outer2, E, o_at + b), (inner2, E, i_at + b)], image[chip, b])
            return carry

        repeat(NB // 2, step, 0, UNROLL)

    spread_own(outside)
    inner_wait(inner1, 0, recv_sem.at[I1])
    spread_halo(inner1, 0, inner_halo)
    for t in range(T - HC, T, GROUPED):
        first(t, GROUPED, inner1, i_at)

    ones = jnp.ones((8, 2 * BLOCK), jnp.bfloat16)

    def lanes(values):
        line = lax.dot_general(
            ones, jnp.concatenate(halves(values), axis=1), (((1,), (1,)), ((), ())),
            preferred_element_type=jnp.float32,
        )
        width = line.shape[1]
        if width < BLOCK:
            line = jnp.concatenate(
                [line, jnp.zeros((8, BLOCK - width), jnp.float32)], axis=1
            )
        return line[0:1]

    def plane_send(ref, kind):
        for j in range(1, M):
            m, to_lat, to_rad = plane_peer(j)
            remote(ref, ref, kind, recv_sem.at[kind], to_lat, to_rad)

    def plane_sum(buf):
        total = buf[0]
        for m in range(1, M):
            total = total + buf[m]
        return total

    def cross_send():
        def step(n, carry):
            to = lax.rem(chip + 1 + lax.div(n, M), X)
            m = lax.rem(me + lax.rem(n, M), M)
            remote(
                s1.at[chip, me], s1.at[chip, me], S2, recv_sem.at[S2],
                lax.div(m, CORES), to * CORES + lax.rem(m, CORES),
            )
            return carry

        lax.fori_loop(0, (X - 1) * M, step, 0)

    s1[chip, me] = lanes(jnp.concatenate([acc[0], acc[1]], axis=0))
    pl.when(jnp.logical_not(jnp.logical_or(is_gate, wraps)))(lambda: pl.semaphore_wait(all_in, 1))
    plane_send(s1.at[chip, me], S1)
    cross_send()
    for t in range(HC // 2, HC):
        image_send(t)

    mine = jnp.concatenate(
        [
            from_ref[pl.ds(pl.multiple_of(rad * slab, 8), slab), :],
            from_ref[pl.ds(pl.multiple_of(partner * slab, 8), slab), :],
        ],
        axis=0,
    )

    FB = NB // PARTS

    def columns(f):
        return out.at[:, pl.ds(pl.multiple_of(core * half + f * FB * BLOCK, BLOCK), FB * BLOCK)]

    def columns_of(c):
        return out.at[:, pl.ds(c * half, half)]

    def finish(f):
        blocks = []
        for i in range(FB):
            b = f * FB + i
            blocks.append(
                jnp.concatenate(
                    [coef[x, 0] * modal[x, b] + coef[x, 1] * image[x, b] for x in range(X)], axis=0
                )
            )
        product = dot(mine, jnp.concatenate(blocks, axis=1))
        part[f, 0] = product[0:slab]
        part[f, 1] = product[slab:K]
        remote(part.at[f, 1], columns(f), OUT, recv_sem.at[OUT], lat, partner)
        pltpu.make_async_copy(part.at[f, 0], columns(f), out_sem).start()

    def second_pass(buf, at, first_block):
        def step(i, carry):
            b = first_block + i
            twice[b] = operate_own(buf, at, chip, b, image[chip, b])
            return carry

        repeat(NB // 2, step, 0)

    def residual(b, carry):
        final = modal[chip, b] - (coef[chip, 0] * image[chip, b] + coef[chip, 1] * twice[b])
        return carry + final * final

    def chebyshev(x):
        s2[x] = plane_sum(s1.at[x])
        column = jnp.transpose(jnp.broadcast_to(s2[x], (BLOCK, BLOCK)))
        base, power = column[0:K], column[K:2 * K]
        upper = 1.5 * jnp.sqrt(power / (base + 1e-06))
        lower = upper * 0.125
        center = (upper + lower) * 0.5
        half_width = (upper - lower) * 0.5
        sigma = center / half_width
        rho_zero = 1.0 / sigma
        rho_one = 1.0 / (2.0 * sigma - rho_zero)
        second = 2.0 * rho_one / half_width
        coef[x, 0] = (1.0 + rho_one * rho_zero) / center + second
        coef[x, 1] = -second / center

    spread_own(inside)

    def project_last():
        for t in range(T - LAST, T):
            project_others(t)

    pl.when(lat == 0)(project_last)
    pl.when(wraps)(far_ready)
    far_pass()
    inner_wait(inner2, 0, recv_sem.at[I2])
    spread_halo(inner2, 0, inner_halo)
    second_pass(inner2, i_at, inside)
    def others_image():
        for j in range(1, X):
            x = lax.rem(chip + j, X)
            base = (j - 1) * A * E
            inner_wait(others, base, x_recv.at[j - 1])
            spread_halo(others, base, inner_halo)
        for j in range(1, X):
            x = lax.rem(chip + j, X)
            base = (j - 1) * A * E

            def others_pass(i, carry, x=x, base=base):
                b = inside + i
                image[x, b] = operate_own(others, base + i_at, x, b, modal[x, b])
                return carry

            repeat(NB // 2, others_pass, 0)

    pl.when(lat == 0)(others_image)
    outer_wait(outer2, NEAR, O2)
    spread_halo(outer2, 0, outer_halo + core * NEAR, HALO - NEAR)
    second_pass(outer2, o_at, outside)
    arrived(s1.at[0, pl.ds(0, M - 1)], recv_sem.at[S1])
    chebyshev(chip)
    s3[me] = lanes(repeat(NB, residual, zero))
    plane_send(s3.at[me], S3)

    @pl.when(lat != 0)
    def _():
        project_last()
        others_image()

    arrived(s1.at[pl.ds(0, X - 1)], recv_sem.at[S2])
    for j in range(1, X):
        chebyshev(lax.rem(chip + j, X))
    arrived(image.at[pl.ds(0, X - 1), pl.ds(0, HALO)], recv_sem.at[IM])
    for f in range(PARTS):
        finish(f)

    arrived(s3.at[pl.ds(0, M - 1)], recv_sem.at[S3])
    norm = jnp.sqrt(plane_sum(s3) / (s2[chip] + 1e-06))
    res_ref[...] = jnp.where(core == 0, norm[:, 0:slab], norm[:, slab:2 * slab])

    everything = columns_of(0)
    pltpu.make_async_copy(everything, everything, out_sem).wait()
    whole(columns_of(0), OUT, recv_sem.at[OUT]).wait()
    whole(gathered.at[:, pl.ds(0, (R - 1) * slab), :], AG, ag_recv.at[0]).wait_send()
    for kind in (O1, I1, I2):
        whole(outer1.at[pl.ds(0, HALO)], kind, recv_sem.at[kind]).wait_send()
    whole(outer1.at[pl.ds(0, HALO - NEAR)], O2, recv_sem.at[O2]).wait_send()
    whole(outer1.at[pl.ds(0, NEAR)], FAR, recv_sem.at[FAR]).wait_send()
    for ref, kind in far_inputs:
        whole(ref, kind, recv_sem.at[kind]).wait_send()
    whole(others.at[pl.ds(0, (X - 1) * HALO)], OT, recv_sem.at[OT]).wait_send()
    whole(image.at[pl.ds(0, X - 1), pl.ds(0, HALO)], IM, recv_sem.at[IM]).wait_send()
    for kind in (S1, S3):
        whole(s3.at[pl.ds(0, M - 1)], kind, recv_sem.at[kind]).wait_send()
    whole(s1.at[pl.ds(0, X - 1)], S2, recv_sem.at[S2]).wait_send()


def deliver(smoothed, norm, out, res, sem):
    copies = [
        pltpu.make_async_copy(a, b, sem.at[i]) for i, (a, b) in enumerate([(smoothed, out), (norm, res)])
    ]
    for copy in copies:
        copy.start()
    for copy in copies:
        copy.wait()


def on_device(L, R, source, to_modes, from_modes, eigenvalue, shifts, weights, neighbors):
    slab, nodes = source.shape
    S = weights.shape[0]
    levels = to_modes.shape[0]
    T, X, K = CHUNKS, R // CORES, slab * CORES
    half = nodes // CORES
    NB = half // BLOCK
    CW = half // T
    E = NB + HALO
    A = -(-S // GROUP)
    M = L * CORES
    f32 = jnp.float32

    def window(count):
        return pltpu.VMEM((count * A * E, K, BLOCK), f32)

    dma = pltpu.SemaphoreType.DMA
    vmem = pl.BlockSpec(memory_space=pltpu.VMEM)
    hbm = pl.BlockSpec(memory_space=pltpu.HBM)
    smoothed, norm = pl.pallas_call(
        functools.partial(kernel, L, R, S),
        name="smoother",
        out_shape=(
            pltpu.VMEM((slab, nodes), f32),
            pltpu.VMEM((1, slab), f32),
        ),
        in_specs=[hbm] * 7,
        out_specs=(vmem, vmem),
        scratch_shapes=[
            pltpu.VMEM((T, levels, CW), f32),
            pltpu.VMEM((S, half), f32),
            pltpu.VMEM((NB, (A + 1) * GROUP, BLOCK), f32),
            pltpu.VMEM((S, NEAR * BLOCK), f32),
            pltpu.VMEM((NEAR, (A + 1) * GROUP, BLOCK), f32),
            pltpu.VMEM((A * (NEAR + 2 * HALO), K, BLOCK), f32),
            window(1), window(1), window(1), window(1), window(X - 1),
            pltpu.VMEM((X, NB, K, BLOCK), f32),
            pltpu.VMEM((X, NB, K, BLOCK), f32),
            pltpu.VMEM((NB, K, BLOCK), f32),
            pltpu.VMEM((levels, levels), f32),
            pltpu.VMEM((X, 2, K, BLOCK), f32),
            pltpu.VMEM((2, K, BLOCK), f32),
            pltpu.VMEM((PARTS, 2, slab, half // PARTS), f32),
            pltpu.VMEM((NB, BLOCK), f32),
            pltpu.VMEM((GROUP, BLOCK), f32),
            pltpu.VMEM((X, M, 1, BLOCK), f32),
            pltpu.VMEM((X, 1, BLOCK), f32),
            pltpu.VMEM((M, 1, BLOCK), f32),
            pltpu.VMEM((levels, levels), f32),
            pltpu.VMEM((levels, levels), f32),
            pltpu.VMEM((1, levels), f32),
            pltpu.SMEM(neighbors.shape, jnp.int32),
            pltpu.SMEM(neighbors.shape, jnp.int32),
            dma((5,)), dma(()), dma(()),
            dma((T,)), dma((X - 1,)),
            dma((15,)), dma((15,)), dma(()), pltpu.SemaphoreType.REGULAR((5,)),
        ],
        compiler_params=pltpu.CompilerParams(
            collective_id=0, has_side_effects=True, vmem_limit_bytes=67043328 - 4 * slab * nodes - 4096
        ),
    )(
        source, weights, to_modes, from_modes, eigenvalue.reshape(1, levels),
        shifts.reshape(nodes // BLOCK, BLOCK), neighbors,
    )
    smoothed, norm = pl.pallas_call(
        deliver,
        name="deliver",
        out_shape=(
            jax.ShapeDtypeStruct((slab, nodes), f32), jax.ShapeDtypeStruct((1, slab), f32)
        ),
        in_specs=[vmem, vmem],
        out_specs=(hbm, hbm),
        scratch_shapes=[dma((2,))],
    )(
        pltpu.with_memory_space_constraint(smoothed, pltpu.VMEM),
        pltpu.with_memory_space_constraint(norm, pltpu.VMEM),
    )
    return smoothed, norm.reshape(slab)


def solution(mesh):
    return jax.shard_map(
        functools.partial(on_device, mesh.shape["lat"], mesh.shape["rad"]),
        mesh=mesh,
        in_specs=(P("rad", "lat"), P(), P(), P(), P("lat"), P(None, "lat"), P(None, "lat")),
        out_specs=(P("rad", "lat"), P("rad")),
        check_vma=False,
    )
```

```python
import functools

import jax
import jax.numpy as jnp
from jax import lax
from jax.experimental import pallas as pl
from jax.experimental.pallas import tpu as pltpu
from jax.sharding import PartitionSpec as P

BLOCK = 128
HALO = 8
CHUNKS = 8
PARTS = 4
NEAR = 2
GROUP = 8
UNROLL = 8
STEP = 2
CORES = 2
HIGHEST = lax.Precision.HIGHEST
MESH = pl.DeviceIdType.MESH


def halves(v):
    high = v.astype(jnp.bfloat16)
    return high, (v - high.astype(jnp.float32)).astype(jnp.bfloat16)


def dot(a, b):
    (a_high, a_low), (b_high, b_low) = halves(a), halves(b)
    left = jnp.concatenate([a_high, a_high], axis=1)
    right = jnp.concatenate([b_high, b_low], axis=0)
    return jnp.dot(left, right, preferred_element_type=jnp.float32) + jnp.dot(
        a_low, b_high, preferred_element_type=jnp.float32
    )


def repeat(count, step, carry, most=UNROLL):
    width = max(n for n in range(1, min(count, most) + 1) if count % n == 0)

    def trip(n, carry):
        for j in range(width):
            carry = step(n * width + j, carry)
        return carry

    if count == width:
        return trip(0, carry)
    return lax.fori_loop(0, count // width, trip, carry)


def kernel(
    L, R, S,
    src, w_hbm, to_hbm, from_hbm, eig_hbm, shift_hbm, nbr_hbm,
    out, res_ref,
    gathered, wv, wr, far_wv, far_wr, far, outer1, inner1, outer2, inner2, others, modal, image, twice, eig_t, coef, acc, part,
    rows, far_rows, s1, s2, s3, to_ref, from_ref, eig_ref, nbr_ref, far_nbr,
    in_sem, own_sem, w_sem, ag_recv, x_recv, send_sem, recv_sem, out_sem, passed,
):
    T = CHUNKS
    X = R // CORES
    M = L * CORES
    slab, nodes = src.shape
    K = slab * CORES
    half = nodes // CORES
    NB = half // BLOCK
    CB = NB // T
    HC = HALO // CB
    CW = CB * BLOCK
    E = NB + HALO
    F = NEAR + 2 * HALO
    NC = NEAR // CB
    A = -(-S // GROUP)
    lat = lax.axis_index("lat")
    rad = lax.axis_index("rad")
    core = lax.rem(rad, CORES)
    chip = lax.div(rad, CORES)
    partner = chip * CORES + (1 - core)
    me = lat * CORES + core
    other_lat = lax.rem(lat + (L - 1) * (1 - core) + core, L)
    wraps = lat + 2 * core - 1 != other_lat

    def order(t, c):
        return t * (1 - c) + (T - 1 - t) * c

    def own_copy(q):
        return pltpu.make_async_copy(
            src.at[:, pl.ds(pl.multiple_of(core * half + q * CW, BLOCK), CW)],
            gathered.at[q, pl.ds(pl.multiple_of(rad * slab, 8), slab), :],
            own_sem,
        )

    w_copy = pltpu.make_async_copy(
        w_hbm.at[:, pl.ds(pl.multiple_of(core * half, BLOCK), half)], wv, w_sem
    )
    inputs = [
        pltpu.make_async_copy(a, b, in_sem.at[i])
        for i, (a, b) in enumerate([
            (to_hbm, to_ref), (from_hbm, from_ref), (eig_hbm, eig_ref), (nbr_hbm, nbr_ref),
            (shift_hbm.at[pl.ds(pl.multiple_of(core * NB, 8), NB), :], rows),
        ])
    ]

    def plane_peer(j):
        m = lax.rem(me + j, M)
        return m, lax.div(m, CORES), chip * CORES + lax.rem(m, CORES)

    barrier = pltpu.get_barrier_semaphore()
    up, down, met, near_in, all_in = [passed.at[i] for i in range(5)]
    gate = R - 1
    is_gate = rad == gate
    below, above = lat >= STEP, lat + STEP < L
    around = [(lat >= d, -d) for d in range(1, STEP + 1)] + [(lat + d < L, d) for d in range(1, STEP + 1)]

    def signal(sem, to_lat, to_rad):
        pl.semaphore_signal(
            sem, inc=1, device_id={"lat": to_lat, "rad": to_rad}, device_id_type=MESH
        )

    def signal_below(sem):
        pl.when(below)(lambda: signal(sem, lat - STEP, gate))

    def signal_above(sem):
        pl.when(above)(lambda: signal(sem, lat + STEP, gate))

    for j in range(1, R):
        r = lax.rem(rad + j, R)
        pl.when(r != gate)(functools.partial(signal, barrier, lat, r))
    w_copy.start()
    for copy in inputs:
        copy.start()
    for q in range(T):
        own_copy(q).start()

    @pl.when(jnp.logical_not(is_gate))
    def _():
        pl.semaphore_wait(barrier, R - 1)
        pl.when(partner == gate)(lambda: signal(met, lat, gate))

    @pl.when(is_gate)
    def _():
        pl.semaphore_wait(met, 1)
        for there, d in around:
            pl.when(there)(functools.partial(signal, barrier, lat + d, gate))

    AG, O1, I1, O2, I2, OT, IM, S1, S2, S3, OUT, FAR, FAR_W, FAR_ROWS, FAR_NBR = range(15)

    def remote(src_ref, dst_ref, kind, recv, lat_to, rad_to):
        pltpu.make_async_remote_copy(
            src_ref=src_ref, dst_ref=dst_ref, send_sem=send_sem.at[kind], recv_sem=recv,
            device_id={"lat": lat_to, "rad": rad_to}, device_id_type=MESH,
        ).start()

    def whole(ref, kind, recv):
        return pltpu.make_async_remote_copy(
            src_ref=ref, dst_ref=ref, send_sem=send_sem.at[kind], recv_sem=recv,
            device_id={"lat": lat, "rad": partner}, device_id_type=MESH,
        )

    def arrived(ref, recv):
        whole(ref, AG, recv).wait_recv()

    def slot(q, r):
        return gathered.at[q, pl.ds(pl.multiple_of(r * slab, 8), slab), :]

    for t in range(T):
        for j in range(1, R):
            to = lax.rem(rad + j, R)
            to_core = lax.rem(to, CORES)
            q = order(t, to_core)
            remote(
                src.at[:, pl.ds(pl.multiple_of(to_core * half + q * CW, BLOCK), CW)],
                slot(q, rad), AG, ag_recv.at[q], lat, to,
            )

    w_copy.wait()
    for copy in inputs:
        copy.wait()
    row_id = lax.broadcasted_iota(jnp.int32, (A * GROUP, BLOCK), 0)

    def prepare_from(raw, shift, row_at, ready, b):
        ready[b, pl.ds((A - 1) * GROUP, GROUP), :] = jnp.zeros((GROUP, BLOCK), jnp.float32)
        ready[b, pl.ds(0, S), :] = raw[:, pl.ds(pl.multiple_of(b * BLOCK, BLOCK), BLOCK)]
        tile = ready[b, pl.ds(0, A * GROUP), :]
        placed = tile
        for c in range(1, GROUP):
            placed = jnp.where(lax.rem(row_id, GROUP) == c, pltpu.roll(tile, c, 1), placed)
        ready[b, pl.ds(0, A * GROUP), :] = placed
        diagonal = jnp.sum(tile, axis=0, keepdims=True) + shift[pl.ds(row_at + b, 1), :]
        ready[b, pl.ds(A * GROUP, GROUP), :] = jnp.broadcast_to(diagonal, (GROUP, BLOCK))

    def prepare(b, carry):
        prepare_from(wv, rows, 0, wr, b)
        return carry

    row_tile = far_rows.shape[0]

    def prepare_far(b, carry):
        prepare_from(far_wv, far_rows, (row_tile - NEAR) * (1 - core), far_wr, b)
        return carry

    far_inputs = ((far_wv, FAR_W), (far_rows, FAR_ROWS), (far_nbr, FAR_NBR))

    def far_start():
        parts = (
            w_hbm.at[:, pl.ds(pl.multiple_of(core * (nodes - NEAR * BLOCK), BLOCK), NEAR * BLOCK)],
            shift_hbm.at[pl.ds(pl.multiple_of(core * (nodes // BLOCK - row_tile), 8), row_tile), :],
            nbr_hbm,
        )
        for part_ref, (ref, kind) in zip(parts, far_inputs):
            remote(part_ref, ref, kind, recv_sem.at[kind], other_lat, partner)

    def far_ready():
        for ref, kind in far_inputs:
            arrived(ref, recv_sem.at[kind])
        repeat(NEAR, prepare_far, 0)

    repeat(NB, prepare, 0)

    @pl.when(is_gate)
    def _():
        pl.semaphore_wait(barrier, sum(there.astype(jnp.int32) for there, _ in around))
        for r in range(R - 1):
            signal(near_in, lat, r)
        pl.when(jnp.logical_not(wraps))(far_start)
        pl.when(jnp.logical_not(below))(lambda: signal_above(up))
        pl.when(jnp.logical_not(above))(lambda: signal_below(down))

        @pl.when(below)
        def _():
            pl.semaphore_wait(up, 1)
            signal_above(up)

        @pl.when(above)
        def _():
            pl.semaphore_wait(down, 1)
            signal_below(down)

        for r in range(R - 1):
            signal(all_in, lat, r)

    @pl.when(jnp.logical_not(is_gate))
    def _():
        pl.semaphore_wait(near_in, 1)
        pl.when(jnp.logical_not(wraps))(far_start)

    levels = to_ref.shape[0]
    eig_t[...] = jnp.transpose(jnp.broadcast_to(eig_ref[...], (levels, levels)))

    o_at = HALO * (1 - core)
    i_at = HALO * core

    def outer_dst(c, q):
        return (1 - c) * (NB + q * CB) + c * (q * CB - NB + HALO)

    def inner_dst(c, q):
        return c * (NB + q * CB) + (1 - c) * (q * CB - NB + HALO)

    outer_halo = core * NB
    inner_halo = (1 - core) * NB

    def outer_send(buf, t, kind):
        q = order(t, core)
        remote(
            buf.at[pl.ds(o_at + q * CB, CB)], buf.at[pl.ds(outer_dst(core, q), CB)],
            kind, recv_sem.at[kind], other_lat, partner,
        )

    def outer_wait(buf, skip, kind):
        arrived(buf.at[pl.ds(outer_halo + core * skip, HALO - skip)], recv_sem.at[kind])

    def inner_send(buf, base, t, kind, recv):
        q = order(t, core)
        remote(
            buf.at[pl.ds(base + i_at + q * CB, CB)],
            buf.at[pl.ds(base + inner_dst(core, q), CB)],
            kind, recv, lat, partner,
        )

    def inner_wait(buf, base, recv):
        arrived(buf.at[pl.ds(base + inner_halo, HALO)], recv)

    def spread_at(targets, value):
        for a in range(1, A):
            moved = pltpu.roll(value, BLOCK - a * GROUP, 1)
            for buf, stride, k in targets:
                buf[a * stride + k] = moved

    def spread_halo(buf, base, at, count=HALO):
        def step(k, carry):
            spread_at([(buf, E, base + at + k)], buf[base + at + k])
            return carry

        repeat(count, step, 0)

    far_own = (NEAR + HALO) * (1 - core) - (NB - HALO) * core
    far_halo = NEAR * (1 - core) + HALO * core
    far_more = 2 * HALO * core

    def far_at(b):
        return b + HALO * (1 - core) - (NB - NEAR - HALO) * core

    def far_send(t):
        q = order(t, core)
        remote(
            outer1.at[pl.ds(o_at + q * CB, CB)], far.at[pl.ds(far_at(q * CB), CB)],
            FAR, recv_sem.at[FAR], other_lat, partner,
        )

    def spread_outer_halo():
        def step(k, carry):
            value = outer1[outer_halo + k]
            far[far_halo + k] = value
            spread_at([(outer1, E, outer_halo + k), (far, F, far_halo + k)], value)
            return carry

        repeat(HALO, step, 0)

    def far_pass():
        arrived(far.at[pl.ds(far_more, NEAR)], recv_sem.at[FAR])

        def spread_more(k, carry):
            spread_at([(far, F, far_more + k)], far[far_more + k])
            return carry

        def step(i, carry):
            at = HALO + i
            column = (nodes // BLOCK - NEAR) * (1 - core) + i
            value = operate(far, F, at, far_wr, i, far_nbr, column, chip, far[at])
            k = outer_halo + (HALO - NEAR) * (1 - core) + i
            outer2[k] = value
            spread_at([(outer2, E, k)], value)
            return carry

        repeat(NEAR, spread_more, 0)
        repeat(NEAR, step, 0)

    def own_rows(x):
        return to_ref[pl.ds(pl.multiple_of(x * K, 8), K), :]

    def project_others(t):
        q = order(t, core)
        for j in range(1, X):
            x = lax.rem(chip + j, X)
            base = (j - 1) * A * E
            product = dot(own_rows(x), gathered[q])
            for i in range(CB):
                value = product[:, i * BLOCK:(i + 1) * BLOCK]
                modal[x, q * CB + i] = value
                others[base + i_at + q * CB + i] = value
            if t >= T - HC:
                inner_send(others, base, t, OT, x_recv.at[j - 1])
            for i in range(CB):
                spread_at(
                    [(others, E, base + i_at + q * CB + i)], product[:, i * BLOCK:(i + 1) * BLOCK]
                )

    def operate(buf, stride, at, weight, b, table, column, x, field):
        total = None
        for c in range(GROUP):
            inner = None
            for a in range(A):
                s = a * GROUP + c
                if s < S:
                    n = table[s, column]
                    term = buf[a * stride + at + n] * weight[b, pl.ds(s, 1), :]
                    inner = term if inner is None else inner + term
            if inner is not None:
                moved = inner if c == 0 else pltpu.roll(inner, BLOCK - c, 1)
                total = moved if total is None else total + moved
        eig = eig_t[pl.ds(pl.multiple_of(x * K, 8), K), :]
        return (weight[b, pl.ds(A * GROUP, 1), :] + eig) * field - total

    def operate_own(buf, base, x, b, field):
        return operate(buf, E, base + b, wr, b, nbr_ref, core * NB + b, x, field)

    def first_pass(buf, at):
        def step(b, carry):
            field = modal[chip, b]
            value = operate_own(buf, at, chip, b, field)
            outer2[o_at + b] = value
            inner2[i_at + b] = value
            image[chip, b] = value
            return (carry[0] + field * field, carry[1] + value * value)

        return step

    zero = jnp.zeros((K, BLOCK), jnp.float32)

    def image_send(t):
        q = order(t, core)
        for j in range(1, X):
            to = lax.rem(chip + j, X)
            remote(
                image.at[chip, pl.ds(q * CB, CB)], image.at[chip, pl.ds(q * CB, CB)],
                IM, recv_sem.at[IM], lat, to * CORES + core,
            )

    def first(t, count, buf, at):
        start = order(t, core) * (1 - core) + order(t + count - 1, core) * core
        step = first_pass(buf, at)
        sums = repeat(count * CB, lambda i, carry: step(start * CB + i, carry), (acc[0], acc[1]))
        acc[0], acc[1] = sums
        for t in range(t, t + count):
            q = order(t, core)
            if NC <= t < HC:
                outer_send(outer2, t, O2)
            if t < HC // 2:
                image_send(t)
            if t >= T - HC:
                inner_send(inner2, 0, t, I2, recv_sem.at[I2])

    def outer_first(count):
        outer_wait(outer1, 0, O1)
        spread_outer_halo()
        for t in range(NC, count):
            first(t, 1, outer1, o_at)
        if count == HC:
            first(0, NC, outer1, o_at)

    LAST, EARLY, GROUPED, READY = T // 4, T * 11 // 16, T // PARTS, HC - 1
    acc[0], acc[1] = zero, zero
    late = jnp.logical_and(lat == 0, core == 0)
    prompt = jnp.logical_not(late)
    for t in range(T):
        q = order(t, core)
        if t == 0:
            mine_at = gathered.at[:, pl.ds(pl.multiple_of(rad * slab, 8), slab), :]
            pltpu.make_async_copy(mine_at, mine_at, own_sem).wait()
        arrived(gathered.at[q, pl.ds(0, (R - 1) * slab), :], ag_recv.at[q])
        product = dot(own_rows(chip), gathered[q])
        for i in range(CB):
            value = product[:, i * BLOCK:(i + 1) * BLOCK]
            b = q * CB + i
            outer1[o_at + b] = value
            inner1[i_at + b] = value
            modal[chip, b] = value
            if t < HC:
                far[far_own + b] = value
        if t == 0:
            pl.when(jnp.logical_and(jnp.logical_not(is_gate), wraps))(lambda: pl.semaphore_wait(all_in, 1))
        if t < HC:
            outer_send(outer1, t, O1)
        elif t < HC + NC:
            pl.when(prompt)(functools.partial(far_send, t))
        if t >= T - HC:
            inner_send(inner1, 0, t, I1, recv_sem.at[I1])
        for i in range(CB):
            b = q * CB + i
            spread_at(
                [(outer1, E, o_at + b), (inner1, E, i_at + b)]
                + ([(far, F, far_own + b)] if t < HC else []),
                product[:, i * BLOCK:(i + 1) * BLOCK],
            )
        if t < T - LAST:
            project_others(t)
        if t == READY:
            pl.when(jnp.logical_not(wraps))(far_ready)
        if t == HC + NC - 1:
            pl.when(jnp.logical_and(prompt, wraps))(far_start)
        if t == EARLY:

            @pl.when(late)
            def _():
                for n in range(HC, HC + NC):
                    far_send(n)
                far_start()

            pl.when(prompt)(functools.partial(outer_first, t - HC + 1))
        if t > EARLY:
            pl.when(prompt)(functools.partial(first, t - HC, 1, outer1, o_at))
        if t == T - 1:
            pl.when(prompt)(functools.partial(first, 0, NC, outer1, o_at))

    pl.when(late)(functools.partial(outer_first, HC))
    inside = (NB // 2) * (1 - core)
    outside = (NB // 2) * core

    def spread_own(at):
        def step(i, carry):
            b = at + i
            spread_at([(outer2, E, o_at + b), (inner2, E, i_at + b)], image[chip, b])
            return carry

        repeat(NB // 2, step, 0, UNROLL)

    pl.when(prompt)(functools.partial(spread_own, outside))
    inner_wait(inner1, 0, recv_sem.at[I1])
    spread_halo(inner1, 0, inner_halo)
    for t in range(T - HC, T, GROUPED):
        first(t, GROUPED, inner1, i_at)

    ones = jnp.ones((8, 2 * BLOCK), jnp.bfloat16)

    def lanes(values):
        line = lax.dot_general(
            ones, jnp.concatenate(halves(values), axis=1), (((1,), (1,)), ((), ())),
            preferred_element_type=jnp.float32,
        )
        width = line.shape[1]
        if width < BLOCK:
            line = jnp.concatenate(
                [line, jnp.zeros((8, BLOCK - width), jnp.float32)], axis=1
            )
        return line[0:1]

    def plane_send(ref, kind):
        for j in range(1, M):
            m, to_lat, to_rad = plane_peer(j)
            remote(ref, ref, kind, recv_sem.at[kind], to_lat, to_rad)

    def plane_sum(buf):
        total = buf[0]
        for m in range(1, M):
            total = total + buf[m]
        return total

    def cross_send():
        def step(n, carry):
            to = lax.rem(chip + 1 + lax.div(n, M), X)
            m = lax.rem(me + lax.rem(n, M), M)
            remote(
                s1.at[chip, me], s1.at[chip, me], S2, recv_sem.at[S2],
                lax.div(m, CORES), to * CORES + lax.rem(m, CORES),
            )
            return carry

        lax.fori_loop(0, (X - 1) * M, step, 0)

    s1[chip, me] = lanes(jnp.concatenate([acc[0], acc[1]], axis=0))
    pl.when(jnp.logical_not(jnp.logical_or(is_gate, wraps)))(lambda: pl.semaphore_wait(all_in, 1))
    plane_send(s1.at[chip, me], S1)
    cross_send()
    for t in range(HC // 2, HC):
        image_send(t)

    mine = jnp.concatenate(
        [
            from_ref[pl.ds(pl.multiple_of(rad * slab, 8), slab), :],
            from_ref[pl.ds(pl.multiple_of(partner * slab, 8), slab), :],
        ],
        axis=0,
    )

    FB = NB // PARTS

    def columns(f):
        return out.at[:, pl.ds(pl.multiple_of(core * half + f * FB * BLOCK, BLOCK), FB * BLOCK)]

    def columns_of(c):
        return out.at[:, pl.ds(c * half, half)]

    def finish(f):
        blocks = []
        for i in range(FB):
            b = f * FB + i
            blocks.append(
                jnp.concatenate(
                    [coef[x, 0] * modal[x, b] + coef[x, 1] * image[x, b] for x in range(X)], axis=0
                )
            )
        product = dot(mine, jnp.concatenate(blocks, axis=1))
        part[f, 0] = product[0:slab]
        part[f, 1] = product[slab:K]
        remote(part.at[f, 1], columns(f), OUT, recv_sem.at[OUT], lat, partner)
        pltpu.make_async_copy(part.at[f, 0], columns(f), out_sem).start()

    def second_pass(buf, at, first_block):
        def step(i, carry):
            b = first_block + i
            twice[b] = operate_own(buf, at, chip, b, image[chip, b])
            return carry

        repeat(NB // 2, step, 0)

    def residual(b, carry):
        final = modal[chip, b] - (coef[chip, 0] * image[chip, b] + coef[chip, 1] * twice[b])
        return carry + final * final

    def chebyshev(x):
        s2[x] = plane_sum(s1.at[x])
        column = jnp.transpose(jnp.broadcast_to(s2[x], (BLOCK, BLOCK)))
        base, power = column[0:K], column[K:2 * K]
        upper = 1.5 * jnp.sqrt(power / (base + 1e-06))
        lower = upper * 0.125
        center = (upper + lower) * 0.5
        half_width = (upper - lower) * 0.5
        sigma = center / half_width
        rho_zero = 1.0 / sigma
        rho_one = 1.0 / (2.0 * sigma - rho_zero)
        second = 2.0 * rho_one / half_width
        coef[x, 0] = (1.0 + rho_one * rho_zero) / center + second
        coef[x, 1] = -second / center

    pl.when(late)(functools.partial(spread_own, outside))
    spread_own(inside)

    def project_last():
        for t in range(T - LAST, T):
            project_others(t)

    pl.when(lat == 0)(project_last)
    pl.when(wraps)(far_ready)
    far_pass()
    inner_wait(inner2, 0, recv_sem.at[I2])
    spread_halo(inner2, 0, inner_halo)
    second_pass(inner2, i_at, inside)
    def others_image():
        for j in range(1, X):
            x = lax.rem(chip + j, X)
            base = (j - 1) * A * E
            inner_wait(others, base, x_recv.at[j - 1])
            spread_halo(others, base, inner_halo)
        for j in range(1, X):
            x = lax.rem(chip + j, X)
            base = (j - 1) * A * E

            def others_pass(i, carry, x=x, base=base):
                b = inside + i
                image[x, b] = operate_own(others, base + i_at, x, b, modal[x, b])
                return carry

            repeat(NB // 2, others_pass, 0)

    pl.when(lat == 0)(others_image)
    outer_wait(outer2, NEAR, O2)
    spread_halo(outer2, 0, outer_halo + core * NEAR, HALO - NEAR)
    second_pass(outer2, o_at, outside)
    arrived(s1.at[0, pl.ds(0, M - 1)], recv_sem.at[S1])
    chebyshev(chip)
    s3[me] = lanes(repeat(NB, residual, zero))
    plane_send(s3.at[me], S3)

    @pl.when(lat != 0)
    def _():
        project_last()
        others_image()

    arrived(s1.at[pl.ds(0, X - 1)], recv_sem.at[S2])
    for j in range(1, X):
        chebyshev(lax.rem(chip + j, X))
    arrived(image.at[pl.ds(0, X - 1), pl.ds(0, HALO)], recv_sem.at[IM])
    for f in range(PARTS):
        finish(f)

    arrived(s3.at[pl.ds(0, M - 1)], recv_sem.at[S3])
    norm = jnp.sqrt(plane_sum(s3) / (s2[chip] + 1e-06))
    res_ref[...] = jnp.where(core == 0, norm[:, 0:slab], norm[:, slab:2 * slab])

    everything = columns_of(0)
    pltpu.make_async_copy(everything, everything, out_sem).wait()
    whole(columns_of(0), OUT, recv_sem.at[OUT]).wait()
    whole(gathered.at[:, pl.ds(0, (R - 1) * slab), :], AG, ag_recv.at[0]).wait_send()
    for kind in (O1, I1, I2):
        whole(outer1.at[pl.ds(0, HALO)], kind, recv_sem.at[kind]).wait_send()
    whole(outer1.at[pl.ds(0, HALO - NEAR)], O2, recv_sem.at[O2]).wait_send()
    whole(outer1.at[pl.ds(0, NEAR)], FAR, recv_sem.at[FAR]).wait_send()
    for ref, kind in far_inputs:
        whole(ref, kind, recv_sem.at[kind]).wait_send()
    whole(others.at[pl.ds(0, (X - 1) * HALO)], OT, recv_sem.at[OT]).wait_send()
    whole(image.at[pl.ds(0, X - 1), pl.ds(0, HALO)], IM, recv_sem.at[IM]).wait_send()
    for kind in (S1, S3):
        whole(s3.at[pl.ds(0, M - 1)], kind, recv_sem.at[kind]).wait_send()
    whole(s1.at[pl.ds(0, X - 1)], S2, recv_sem.at[S2]).wait_send()


def deliver(smoothed, norm, out, res, sem):
    copies = [
        pltpu.make_async_copy(a, b, sem.at[i]) for i, (a, b) in enumerate([(smoothed, out), (norm, res)])
    ]
    for copy in copies:
        copy.start()
    for copy in copies:
        copy.wait()


def on_device(L, R, source, to_modes, from_modes, eigenvalue, shifts, weights, neighbors):
    slab, nodes = source.shape
    S = weights.shape[0]
    levels = to_modes.shape[0]
    T, X, K = CHUNKS, R // CORES, slab * CORES
    half = nodes // CORES
    NB = half // BLOCK
    CW = half // T
    E = NB + HALO
    A = -(-S // GROUP)
    M = L * CORES
    f32 = jnp.float32

    def window(count):
        return pltpu.VMEM((count * A * E, K, BLOCK), f32)

    dma = pltpu.SemaphoreType.DMA
    vmem = pl.BlockSpec(memory_space=pltpu.VMEM)
    hbm = pl.BlockSpec(memory_space=pltpu.HBM)
    smoothed, norm = pl.pallas_call(
        functools.partial(kernel, L, R, S),
        name="smoother",
        out_shape=(
            pltpu.VMEM((slab, nodes), f32),
            pltpu.VMEM((1, slab), f32),
        ),
        in_specs=[hbm] * 7,
        out_specs=(vmem, vmem),
        scratch_shapes=[
            pltpu.VMEM((T, levels, CW), f32),
            pltpu.VMEM((S, half), f32),
            pltpu.VMEM((NB, (A + 1) * GROUP, BLOCK), f32),
            pltpu.VMEM((S, NEAR * BLOCK), f32),
            pltpu.VMEM((NEAR, (A + 1) * GROUP, BLOCK), f32),
            pltpu.VMEM((A * (NEAR + 2 * HALO), K, BLOCK), f32),
            window(1), window(1), window(1), window(1), window(X - 1),
            pltpu.VMEM((X, NB, K, BLOCK), f32),
            pltpu.VMEM((X, NB, K, BLOCK), f32),
            pltpu.VMEM((NB, K, BLOCK), f32),
            pltpu.VMEM((levels, levels), f32),
            pltpu.VMEM((X, 2, K, BLOCK), f32),
            pltpu.VMEM((2, K, BLOCK), f32),
            pltpu.VMEM((PARTS, 2, slab, half // PARTS), f32),
            pltpu.VMEM((NB, BLOCK), f32),
            pltpu.VMEM((GROUP, BLOCK), f32),
            pltpu.VMEM((X, M, 1, BLOCK), f32),
            pltpu.VMEM((X, 1, BLOCK), f32),
            pltpu.VMEM((M, 1, BLOCK), f32),
            pltpu.VMEM((levels, levels), f32),
            pltpu.VMEM((levels, levels), f32),
            pltpu.VMEM((1, levels), f32),
            pltpu.SMEM(neighbors.shape, jnp.int32),
            pltpu.SMEM(neighbors.shape, jnp.int32),
            dma((5,)), dma(()), dma(()),
            dma((T,)), dma((X - 1,)),
            dma((15,)), dma((15,)), dma(()), pltpu.SemaphoreType.REGULAR((5,)),
        ],
        compiler_params=pltpu.CompilerParams(
            collective_id=0, has_side_effects=True, vmem_limit_bytes=67043328 - 4 * slab * nodes - 4096
        ),
    )(
        source, weights, to_modes, from_modes, eigenvalue.reshape(1, levels),
        shifts.reshape(nodes // BLOCK, BLOCK), neighbors,
    )
    smoothed, norm = pl.pallas_call(
        deliver,
        name="deliver",
        out_shape=(
            jax.ShapeDtypeStruct((slab, nodes), f32), jax.ShapeDtypeStruct((1, slab), f32)
        ),
        in_specs=[vmem, vmem],
        out_specs=(hbm, hbm),
        scratch_shapes=[dma((2,))],
    )(
        pltpu.with_memory_space_constraint(smoothed, pltpu.VMEM),
        pltpu.with_memory_space_constraint(norm, pltpu.VMEM),
    )
    return smoothed, norm.reshape(slab)


def solution(mesh):
    return jax.shard_map(
        functools.partial(on_device, mesh.shape["lat"], mesh.shape["rad"]),
        mesh=mesh,
        in_specs=(P("rad", "lat"), P(), P(), P(), P("lat"), P(None, "lat"), P(None, "lat")),
        out_specs=(P("rad", "lat"), P("rad")),
        check_vma=False,
    )
```

```python
import functools

import jax
import jax.numpy as jnp
from jax import lax
from jax.experimental import pallas as pl
from jax.experimental.pallas import tpu as pltpu
from jax.sharding import PartitionSpec as P

BLOCK = 128
HALO = 8
CHUNKS = 8
PARTS = 4
NEAR = 2
GROUP = 8
UNROLL = 8
STEP = 2
CORES = 2
HIGHEST = lax.Precision.HIGHEST
MESH = pl.DeviceIdType.MESH


def halves(v):
    high = v.astype(jnp.bfloat16)
    return high, (v - high.astype(jnp.float32)).astype(jnp.bfloat16)


def dot(a, b):
    (a_high, a_low), (b_high, b_low) = halves(a), halves(b)
    left = jnp.concatenate([a_high, a_high], axis=1)
    right = jnp.concatenate([b_high, b_low], axis=0)
    return jnp.dot(left, right, preferred_element_type=jnp.float32) + jnp.dot(
        a_low, b_high, preferred_element_type=jnp.float32
    )


def repeat(count, step, carry, most=UNROLL):
    width = max(n for n in range(1, min(count, most) + 1) if count % n == 0)

    def trip(n, carry):
        for j in range(width):
            carry = step(n * width + j, carry)
        return carry

    if count == width:
        return trip(0, carry)
    return lax.fori_loop(0, count // width, trip, carry)


def kernel(
    L, R, S,
    src, w_hbm, to_hbm, from_hbm, eig_hbm, shift_hbm, nbr_hbm,
    out, res_ref,
    gathered, wv, wr, far_wv, far_wr, far, outer1, inner1, outer2, inner2, others, modal, image, twice, eig_t, coef, acc, part,
    rows, far_rows, s1, s2, s3, to_ref, from_ref, eig_ref, nbr_ref, far_nbr,
    in_sem, own_sem, w_sem, ag_recv, x_recv, send_sem, recv_sem, out_sem, passed,
):
    T = CHUNKS
    X = R // CORES
    M = L * CORES
    slab, nodes = src.shape
    K = slab * CORES
    half = nodes // CORES
    NB = half // BLOCK
    CB = NB // T
    HC = HALO // CB
    CW = CB * BLOCK
    E = NB + HALO
    F = NEAR + 2 * HALO
    NC = NEAR // CB
    A = -(-S // GROUP)
    lat = lax.axis_index("lat")
    rad = lax.axis_index("rad")
    core = lax.rem(rad, CORES)
    chip = lax.div(rad, CORES)
    partner = chip * CORES + (1 - core)
    me = lat * CORES + core
    other_lat = lax.rem(lat + (L - 1) * (1 - core) + core, L)
    wraps = lat + 2 * core - 1 != other_lat

    def order(t, c):
        return t * (1 - c) + (T - 1 - t) * c

    def own_copy(q):
        return pltpu.make_async_copy(
            src.at[:, pl.ds(pl.multiple_of(core * half + q * CW, BLOCK), CW)],
            gathered.at[q, pl.ds(pl.multiple_of(rad * slab, 8), slab), :],
            own_sem,
        )

    w_copy = pltpu.make_async_copy(
        w_hbm.at[:, pl.ds(pl.multiple_of(core * half, BLOCK), half)], wv, w_sem
    )
    inputs = [
        pltpu.make_async_copy(a, b, in_sem.at[i])
        for i, (a, b) in enumerate([
            (to_hbm, to_ref), (from_hbm, from_ref), (eig_hbm, eig_ref), (nbr_hbm, nbr_ref),
            (shift_hbm.at[pl.ds(pl.multiple_of(core * NB, 8), NB), :], rows),
        ])
    ]

    def plane_peer(j):
        m = lax.rem(me + j, M)
        return m, lax.div(m, CORES), chip * CORES + lax.rem(m, CORES)

    barrier = pltpu.get_barrier_semaphore()
    up, down, met, near_in, all_in = [passed.at[i] for i in range(5)]
    gate = R - 1
    is_gate = rad == gate
    below, above = lat >= STEP, lat + STEP < L
    around = [(lat >= d, -d) for d in range(1, STEP + 1)] + [(lat + d < L, d) for d in range(1, STEP + 1)]

    def signal(sem, to_lat, to_rad):
        pl.semaphore_signal(
            sem, inc=1, device_id={"lat": to_lat, "rad": to_rad}, device_id_type=MESH
        )

    def signal_below(sem):
        pl.when(below)(lambda: signal(sem, lat - STEP, gate))

    def signal_above(sem):
        pl.when(above)(lambda: signal(sem, lat + STEP, gate))

    for j in range(1, R):
        r = lax.rem(rad + j, R)
        pl.when(r != gate)(functools.partial(signal, barrier, lat, r))
    w_copy.start()
    for copy in inputs:
        copy.start()
    for q in range(T):
        own_copy(q).start()

    @pl.when(jnp.logical_not(is_gate))
    def _():
        pl.semaphore_wait(barrier, R - 1)
        pl.when(partner == gate)(lambda: signal(met, lat, gate))

    @pl.when(is_gate)
    def _():
        pl.semaphore_wait(met, 1)
        for there, d in around:
            pl.when(there)(functools.partial(signal, barrier, lat + d, gate))

    AG, O1, I1, O2, I2, OT, IM, S1, S2, S3, OUT, FAR, FAR_W, FAR_ROWS, FAR_NBR = range(15)

    def remote(src_ref, dst_ref, kind, recv, lat_to, rad_to):
        pltpu.make_async_remote_copy(
            src_ref=src_ref, dst_ref=dst_ref, send_sem=send_sem.at[kind], recv_sem=recv,
            device_id={"lat": lat_to, "rad": rad_to}, device_id_type=MESH,
        ).start()

    def whole(ref, kind, recv):
        return pltpu.make_async_remote_copy(
            src_ref=ref, dst_ref=ref, send_sem=send_sem.at[kind], recv_sem=recv,
            device_id={"lat": lat, "rad": partner}, device_id_type=MESH,
        )

    def arrived(ref, recv):
        whole(ref, AG, recv).wait_recv()

    def slot(q, r):
        return gathered.at[q, pl.ds(pl.multiple_of(r * slab, 8), slab), :]

    for t in range(T):
        for j in range(1, R):
            to = lax.rem(rad + j, R)
            to_core = lax.rem(to, CORES)
            q = order(t, to_core)
            remote(
                src.at[:, pl.ds(pl.multiple_of(to_core * half + q * CW, BLOCK), CW)],
                slot(q, rad), AG, ag_recv.at[q], lat, to,
            )

    w_copy.wait()
    for copy in inputs:
        copy.wait()
    row_id = lax.broadcasted_iota(jnp.int32, (A * GROUP, BLOCK), 0)

    def prepare_from(raw, shift, row_at, ready, b):
        ready[b, pl.ds((A - 1) * GROUP, GROUP), :] = jnp.zeros((GROUP, BLOCK), jnp.float32)
        ready[b, pl.ds(0, S), :] = raw[:, pl.ds(pl.multiple_of(b * BLOCK, BLOCK), BLOCK)]
        tile = ready[b, pl.ds(0, A * GROUP), :]
        placed = tile
        for c in range(1, GROUP):
            placed = jnp.where(lax.rem(row_id, GROUP) == c, pltpu.roll(tile, c, 1), placed)
        ready[b, pl.ds(0, A * GROUP), :] = placed
        diagonal = jnp.sum(tile, axis=0, keepdims=True) + shift[pl.ds(row_at + b, 1), :]
        ready[b, pl.ds(A * GROUP, GROUP), :] = jnp.broadcast_to(diagonal, (GROUP, BLOCK))

    def prepare(b, carry):
        prepare_from(wv, rows, 0, wr, b)
        return carry

    row_tile = far_rows.shape[0]

    def prepare_far(b, carry):
        prepare_from(far_wv, far_rows, (row_tile - NEAR) * (1 - core), far_wr, b)
        return carry

    far_inputs = ((far_wv, FAR_W), (far_rows, FAR_ROWS), (far_nbr, FAR_NBR))

    def far_start():
        parts = (
            w_hbm.at[:, pl.ds(pl.multiple_of(core * (nodes - NEAR * BLOCK), BLOCK), NEAR * BLOCK)],
            shift_hbm.at[pl.ds(pl.multiple_of(core * (nodes // BLOCK - row_tile), 8), row_tile), :],
            nbr_hbm,
        )
        for part_ref, (ref, kind) in zip(parts, far_inputs):
            remote(part_ref, ref, kind, recv_sem.at[kind], other_lat, partner)

    def far_ready():
        for ref, kind in far_inputs:
            arrived(ref, recv_sem.at[kind])
        repeat(NEAR, prepare_far, 0)

    repeat(NB, prepare, 0)

    @pl.when(is_gate)
    def _():
        pl.semaphore_wait(barrier, sum(there.astype(jnp.int32) for there, _ in around))
        for r in range(R - 1):
            signal(near_in, lat, r)
        pl.when(jnp.logical_not(wraps))(far_start)
        pl.when(jnp.logical_not(below))(lambda: signal_above(up))
        pl.when(jnp.logical_not(above))(lambda: signal_below(down))

        @pl.when(below)
        def _():
            pl.semaphore_wait(up, 1)
            signal_above(up)

        @pl.when(above)
        def _():
            pl.semaphore_wait(down, 1)
            signal_below(down)

        for r in range(R - 1):
            signal(all_in, lat, r)

    @pl.when(jnp.logical_not(is_gate))
    def _():
        pl.semaphore_wait(near_in, 1)
        pl.when(jnp.logical_not(wraps))(far_start)

    levels = to_ref.shape[0]
    eig_t[...] = jnp.transpose(jnp.broadcast_to(eig_ref[...], (levels, levels)))

    o_at = HALO * (1 - core)
    i_at = HALO * core

    def outer_dst(c, q):
        return (1 - c) * (NB + q * CB) + c * (q * CB - NB + HALO)

    def inner_dst(c, q):
        return c * (NB + q * CB) + (1 - c) * (q * CB - NB + HALO)

    outer_halo = core * NB
    inner_halo = (1 - core) * NB

    def outer_send(buf, t, kind):
        q = order(t, core)
        remote(
            buf.at[pl.ds(o_at + q * CB, CB)], buf.at[pl.ds(outer_dst(core, q), CB)],
            kind, recv_sem.at[kind], other_lat, partner,
        )

    def outer_wait(buf, skip, kind):
        arrived(buf.at[pl.ds(outer_halo + core * skip, HALO - skip)], recv_sem.at[kind])

    def inner_send(buf, base, t, kind, recv):
        q = order(t, core)
        remote(
            buf.at[pl.ds(base + i_at + q * CB, CB)],
            buf.at[pl.ds(base + inner_dst(core, q), CB)],
            kind, recv, lat, partner,
        )

    def inner_wait(buf, base, recv):
        arrived(buf.at[pl.ds(base + inner_halo, HALO)], recv)

    def spread_at(targets, value):
        for a in range(1, A):
            moved = pltpu.roll(value, BLOCK - a * GROUP, 1)
            for buf, stride, k in targets:
                buf[a * stride + k] = moved

    def spread_halo(buf, base, at, count=HALO):
        def step(k, carry):
            spread_at([(buf, E, base + at + k)], buf[base + at + k])
            return carry

        repeat(count, step, 0)

    far_own = (NEAR + HALO) * (1 - core) - (NB - HALO) * core
    far_halo = NEAR * (1 - core) + HALO * core
    far_more = 2 * HALO * core

    def far_at(b):
        return b + HALO * (1 - core) - (NB - NEAR - HALO) * core

    def far_send(t):
        q = order(t, core)
        remote(
            outer1.at[pl.ds(o_at + q * CB, CB)], far.at[pl.ds(far_at(q * CB), CB)],
            FAR, recv_sem.at[FAR], other_lat, partner,
        )

    def spread_outer_halo():
        def step(k, carry):
            value = outer1[outer_halo + k]
            far[far_halo + k] = value
            spread_at([(outer1, E, outer_halo + k), (far, F, far_halo + k)], value)
            return carry

        repeat(HALO, step, 0)

    def far_pass():
        arrived(far.at[pl.ds(far_more, NEAR)], recv_sem.at[FAR])

        def spread_more(k, carry):
            spread_at([(far, F, far_more + k)], far[far_more + k])
            return carry

        def step(i, carry):
            at = HALO + i
            column = (nodes // BLOCK - NEAR) * (1 - core) + i
            value = operate(far, F, at, far_wr, i, far_nbr, column, chip, far[at])
            k = outer_halo + (HALO - NEAR) * (1 - core) + i
            outer2[k] = value
            spread_at([(outer2, E, k)], value)
            return carry

        repeat(NEAR, spread_more, 0)
        repeat(NEAR, step, 0)

    def own_rows(x):
        return to_ref[pl.ds(pl.multiple_of(x * K, 8), K), :]

    def project_others(t):
        q = order(t, core)
        for j in range(1, X):
            x = lax.rem(chip + j, X)
            base = (j - 1) * A * E
            product = dot(own_rows(x), gathered[q])
            for i in range(CB):
                value = product[:, i * BLOCK:(i + 1) * BLOCK]
                modal[x, q * CB + i] = value
                others[base + i_at + q * CB + i] = value
            if t >= T - HC:
                inner_send(others, base, t, OT, x_recv.at[j - 1])
            for i in range(CB):
                spread_at(
                    [(others, E, base + i_at + q * CB + i)], product[:, i * BLOCK:(i + 1) * BLOCK]
                )

    def operate(buf, stride, at, weight, b, table, column, x, field):
        total = None
        for c in range(GROUP):
            inner = None
            for a in range(A):
                s = a * GROUP + c
                if s < S:
                    n = table[s, column]
                    term = buf[a * stride + at + n] * weight[b, pl.ds(s, 1), :]
                    inner = term if inner is None else inner + term
            if inner is not None:
                moved = inner if c == 0 else pltpu.roll(inner, BLOCK - c, 1)
                total = moved if total is None else total + moved
        eig = eig_t[pl.ds(pl.multiple_of(x * K, 8), K), :]
        return (weight[b, pl.ds(A * GROUP, 1), :] + eig) * field - total

    def operate_own(buf, base, x, b, field):
        return operate(buf, E, base + b, wr, b, nbr_ref, core * NB + b, x, field)

    def first_pass(buf, at):
        def step(b, carry):
            field = modal[chip, b]
            value = operate_own(buf, at, chip, b, field)
            outer2[o_at + b] = value
            inner2[i_at + b] = value
            image[chip, b] = value
            return (carry[0] + field * field, carry[1] + value * value)

        return step

    zero = jnp.zeros((K, BLOCK), jnp.float32)

    def image_send(t):
        q = order(t, core)
        for j in range(1, X):
            to = lax.rem(chip + j, X)
            remote(
                image.at[chip, pl.ds(q * CB, CB)], image.at[chip, pl.ds(q * CB, CB)],
                IM, recv_sem.at[IM], lat, to * CORES + core,
            )

    def first(t, count, buf, at):
        start = order(t, core) * (1 - core) + order(t + count - 1, core) * core
        step = first_pass(buf, at)
        sums = repeat(count * CB, lambda i, carry: step(start * CB + i, carry), (acc[0], acc[1]))
        acc[0], acc[1] = sums
        for t in range(t, t + count):
            q = order(t, core)
            if NC <= t < HC:
                outer_send(outer2, t, O2)
            if t < HC // 2:
                image_send(t)
            if t >= T - HC:
                inner_send(inner2, 0, t, I2, recv_sem.at[I2])

    def outer_first(count):
        outer_wait(outer1, 0, O1)
        spread_outer_halo()
        for t in range(NC, count):
            first(t, 1, outer1, o_at)
        if count == HC:
            first(0, NC, outer1, o_at)

    LAST, EARLY, GROUPED, READY = T // 4, T * 11 // 16, T // PARTS, HC - 1
    acc[0], acc[1] = zero, zero
    late = jnp.logical_and(lat == 0, core == 0)
    prompt = jnp.logical_not(late)
    for t in range(T):
        q = order(t, core)
        if t == 0:
            mine_at = gathered.at[:, pl.ds(pl.multiple_of(rad * slab, 8), slab), :]
            pltpu.make_async_copy(mine_at, mine_at, own_sem).wait()
        arrived(gathered.at[q, pl.ds(0, (R - 1) * slab), :], ag_recv.at[q])
        product = dot(own_rows(chip), gathered[q])
        for i in range(CB):
            value = product[:, i * BLOCK:(i + 1) * BLOCK]
            b = q * CB + i
            outer1[o_at + b] = value
            inner1[i_at + b] = value
            modal[chip, b] = value
            if t < HC:
                far[far_own + b] = value
        if t == 0:
            pl.when(jnp.logical_and(jnp.logical_not(is_gate), wraps))(lambda: pl.semaphore_wait(all_in, 1))
        if t < HC:
            outer_send(outer1, t, O1)
        elif t < HC + NC:
            pl.when(prompt)(functools.partial(far_send, t))
        if t >= T - HC:
            inner_send(inner1, 0, t, I1, recv_sem.at[I1])
        for i in range(CB):
            b = q * CB + i
            spread_at(
                [(outer1, E, o_at + b), (inner1, E, i_at + b)]
                + ([(far, F, far_own + b)] if t < HC else []),
                product[:, i * BLOCK:(i + 1) * BLOCK],
            )
        if t < T - LAST:
            project_others(t)
        if t == READY:
            pl.when(jnp.logical_not(wraps))(far_ready)
        if t == HC + NC - 1:
            pl.when(jnp.logical_and(prompt, wraps))(far_start)
        if t == EARLY:

            @pl.when(late)
            def _():
                for n in range(HC, HC + NC):
                    far_send(n)
                far_start()

            pl.when(prompt)(functools.partial(outer_first, t - HC + 1))
        if t > EARLY:
            pl.when(prompt)(functools.partial(first, t - HC, 1, outer1, o_at))
        if t == T - 1:
            pl.when(prompt)(functools.partial(first, 0, NC, outer1, o_at))

    pl.when(late)(functools.partial(outer_first, HC))
    inside = (NB // 2) * (1 - core)
    outside = (NB // 2) * core

    def spread_own(at):
        def step(i, carry):
            b = at + i
            spread_at([(outer2, E, o_at + b), (inner2, E, i_at + b)], image[chip, b])
            return carry

        repeat(NB // 2, step, 0, UNROLL)

    spread_own(outside)
    inner_wait(inner1, 0, recv_sem.at[I1])
    spread_halo(inner1, 0, inner_halo)
    for t in range(T - HC, T, GROUPED):
        first(t, GROUPED, inner1, i_at)

    ones = jnp.ones((8, 2 * BLOCK), jnp.bfloat16)

    def lanes(values):
        line = lax.dot_general(
            ones, jnp.concatenate(halves(values), axis=1), (((1,), (1,)), ((), ())),
            preferred_element_type=jnp.float32,
        )
        width = line.shape[1]
        if width < BLOCK:
            line = jnp.concatenate(
                [line, jnp.zeros((8, BLOCK - width), jnp.float32)], axis=1
            )
        return line[0:1]

    def plane_send(ref, kind):
        for j in range(1, M):
            m, to_lat, to_rad = plane_peer(j)
            remote(ref, ref, kind, recv_sem.at[kind], to_lat, to_rad)

    def plane_sum(buf):
        total = buf[0]
        for m in range(1, M):
            total = total + buf[m]
        return total

    def cross_send():
        def step(n, carry):
            to = lax.rem(chip + 1 + lax.div(n, M), X)
            m = lax.rem(me + lax.rem(n, M), M)
            remote(
                s1.at[chip, me], s1.at[chip, me], S2, recv_sem.at[S2],
                lax.div(m, CORES), to * CORES + lax.rem(m, CORES),
            )
            return carry

        lax.fori_loop(0, (X - 1) * M, step, 0)

    s1[chip, me] = lanes(jnp.concatenate([acc[0], acc[1]], axis=0))
    pl.when(jnp.logical_not(jnp.logical_or(is_gate, wraps)))(lambda: pl.semaphore_wait(all_in, 1))
    plane_send(s1.at[chip, me], S1)
    cross_send()
    for t in range(HC // 2, HC):
        image_send(t)

    mine = jnp.concatenate(
        [
            from_ref[pl.ds(pl.multiple_of(rad * slab, 8), slab), :],
            from_ref[pl.ds(pl.multiple_of(partner * slab, 8), slab), :],
        ],
        axis=0,
    )

    FB = NB // PARTS

    def columns(f):
        return out.at[:, pl.ds(pl.multiple_of(core * half + f * FB * BLOCK, BLOCK), FB * BLOCK)]

    def columns_of(c):
        return out.at[:, pl.ds(c * half, half)]

    def finish(f):
        blocks = []
        for i in range(FB):
            b = f * FB + i
            blocks.append(
                jnp.concatenate(
                    [coef[x, 0] * modal[x, b] + coef[x, 1] * image[x, b] for x in range(X)], axis=0
                )
            )
        product = dot(mine, jnp.concatenate(blocks, axis=1))
        part[f, 0] = product[0:slab]
        part[f, 1] = product[slab:K]
        remote(part.at[f, 1], columns(f), OUT, recv_sem.at[OUT], lat, partner)
        pltpu.make_async_copy(part.at[f, 0], columns(f), out_sem).start()

    def second_pass(buf, at, first_block):
        def step(i, carry):
            b = first_block + i
            twice[b] = operate_own(buf, at, chip, b, image[chip, b])
            return carry

        repeat(NB // 2, step, 0)

    def residual(b, carry):
        final = modal[chip, b] - (coef[chip, 0] * image[chip, b] + coef[chip, 1] * twice[b])
        return carry + final * final

    def chebyshev(x):
        s2[x] = plane_sum(s1.at[x])
        column = jnp.transpose(jnp.broadcast_to(s2[x], (BLOCK, BLOCK)))
        base, power = column[0:K], column[K:2 * K]
        upper = 1.5 * jnp.sqrt(power / (base + 1e-06))
        lower = upper * 0.125
        center = (upper + lower) * 0.5
        half_width = (upper - lower) * 0.5
        sigma = center / half_width
        rho_zero = 1.0 / sigma
        rho_one = 1.0 / (2.0 * sigma - rho_zero)
        second = 2.0 * rho_one / half_width
        coef[x, 0] = (1.0 + rho_one * rho_zero) / center + second
        coef[x, 1] = -second / center

    spread_own(inside)

    def project_last():
        for t in range(T - LAST, T):
            project_others(t)

    pl.when(lat == 0)(project_last)
    pl.when(wraps)(far_ready)
    far_pass()
    inner_wait(inner2, 0, recv_sem.at[I2])
    spread_halo(inner2, 0, inner_halo)
    second_pass(inner2, i_at, inside)
    def others_image():
        for j in range(1, X):
            x = lax.rem(chip + j, X)
            base = (j - 1) * A * E
            inner_wait(others, base, x_recv.at[j - 1])
            spread_halo(others, base, inner_halo)
        for j in range(1, X):
            x = lax.rem(chip + j, X)
            base = (j - 1) * A * E

            def others_pass(i, carry, x=x, base=base):
                b = inside + i
                image[x, b] = operate_own(others, base + i_at, x, b, modal[x, b])
                return carry

            repeat(NB // 2, others_pass, 0)

    pl.when(lat == 0)(others_image)
    outer_wait(outer2, NEAR, O2)
    spread_halo(outer2, 0, outer_halo + core * NEAR, HALO - NEAR)
    second_pass(outer2, o_at, outside)
    arrived(s1.at[0, pl.ds(0, M - 1)], recv_sem.at[S1])
    chebyshev(chip)
    s3[me] = lanes(repeat(NB, residual, zero))
    plane_send(s3.at[me], S3)

    @pl.when(lat != 0)
    def _():
        project_last()
        others_image()

    arrived(s1.at[pl.ds(0, X - 1)], recv_sem.at[S2])
    for j in range(1, X):
        chebyshev(lax.rem(chip + j, X))
    arrived(image.at[pl.ds(0, X - 1), pl.ds(0, HALO)], recv_sem.at[IM])
    for f in range(PARTS):
        finish(f)

    arrived(s3.at[pl.ds(0, M - 1)], recv_sem.at[S3])
    norm = jnp.sqrt(plane_sum(s3) / (s2[chip] + 1e-06))
    res_ref[...] = jnp.where(core == 0, norm[:, 0:slab], norm[:, slab:2 * slab])

    everything = columns_of(0)
    pltpu.make_async_copy(everything, everything, out_sem).wait()
    whole(columns_of(0), OUT, recv_sem.at[OUT]).wait()
    whole(gathered.at[:, pl.ds(0, (R - 1) * slab), :], AG, ag_recv.at[0]).wait_send()
    for kind in (O1, I1, I2):
        whole(outer1.at[pl.ds(0, HALO)], kind, recv_sem.at[kind]).wait_send()
    whole(outer1.at[pl.ds(0, HALO - NEAR)], O2, recv_sem.at[O2]).wait_send()
    whole(outer1.at[pl.ds(0, NEAR)], FAR, recv_sem.at[FAR]).wait_send()
    for ref, kind in far_inputs:
        whole(ref, kind, recv_sem.at[kind]).wait_send()
    whole(others.at[pl.ds(0, (X - 1) * HALO)], OT, recv_sem.at[OT]).wait_send()
    whole(image.at[pl.ds(0, X - 1), pl.ds(0, HALO)], IM, recv_sem.at[IM]).wait_send()
    for kind in (S1, S3):
        whole(s3.at[pl.ds(0, M - 1)], kind, recv_sem.at[kind]).wait_send()
    whole(s1.at[pl.ds(0, X - 1)], S2, recv_sem.at[S2]).wait_send()


def deliver(smoothed, norm, out, res, sem):
    width = smoothed.shape[1] // (sem.shape[0] - 1)
    pairs = [(norm, res)] + [
        (smoothed.at[:, pl.ds(i * width, width)], out.at[:, pl.ds(i * width, width)])
        for i in range(sem.shape[0] - 1)
    ]
    copies = [pltpu.make_async_copy(a, b, sem.at[i]) for i, (a, b) in enumerate(pairs)]
    for copy in copies:
        copy.start()
    for copy in copies:
        copy.wait()


def on_device(L, R, source, to_modes, from_modes, eigenvalue, shifts, weights, neighbors):
    slab, nodes = source.shape
    S = weights.shape[0]
    levels = to_modes.shape[0]
    T, X, K = CHUNKS, R // CORES, slab * CORES
    half = nodes // CORES
    NB = half // BLOCK
    CW = half // T
    E = NB + HALO
    A = -(-S // GROUP)
    M = L * CORES
    f32 = jnp.float32

    def window(count):
        return pltpu.VMEM((count * A * E, K, BLOCK), f32)

    dma = pltpu.SemaphoreType.DMA
    vmem = pl.BlockSpec(memory_space=pltpu.VMEM)
    hbm = pl.BlockSpec(memory_space=pltpu.HBM)
    smoothed, norm = pl.pallas_call(
        functools.partial(kernel, L, R, S),
        name="smoother",
        out_shape=(
            pltpu.VMEM((slab, nodes), f32),
            pltpu.VMEM((1, slab), f32),
        ),
        in_specs=[hbm] * 7,
        out_specs=(vmem, vmem),
        scratch_shapes=[
            pltpu.VMEM((T, levels, CW), f32),
            pltpu.VMEM((S, half), f32),
            pltpu.VMEM((NB, (A + 1) * GROUP, BLOCK), f32),
            pltpu.VMEM((S, NEAR * BLOCK), f32),
            pltpu.VMEM((NEAR, (A + 1) * GROUP, BLOCK), f32),
            pltpu.VMEM((A * (NEAR + 2 * HALO), K, BLOCK), f32),
            window(1), window(1), window(1), window(1), window(X - 1),
            pltpu.VMEM((X, NB, K, BLOCK), f32),
            pltpu.VMEM((X, NB, K, BLOCK), f32),
            pltpu.VMEM((NB, K, BLOCK), f32),
            pltpu.VMEM((levels, levels), f32),
            pltpu.VMEM((X, 2, K, BLOCK), f32),
            pltpu.VMEM((2, K, BLOCK), f32),
            pltpu.VMEM((PARTS, 2, slab, half // PARTS), f32),
            pltpu.VMEM((NB, BLOCK), f32),
            pltpu.VMEM((GROUP, BLOCK), f32),
            pltpu.VMEM((X, M, 1, BLOCK), f32),
            pltpu.VMEM((X, 1, BLOCK), f32),
            pltpu.VMEM((M, 1, BLOCK), f32),
            pltpu.VMEM((levels, levels), f32),
            pltpu.VMEM((levels, levels), f32),
            pltpu.VMEM((1, levels), f32),
            pltpu.SMEM(neighbors.shape, jnp.int32),
            pltpu.SMEM(neighbors.shape, jnp.int32),
            dma((5,)), dma(()), dma(()),
            dma((T,)), dma((X - 1,)),
            dma((15,)), dma((15,)), dma(()), pltpu.SemaphoreType.REGULAR((5,)),
        ],
        compiler_params=pltpu.CompilerParams(
            collective_id=0, has_side_effects=True, vmem_limit_bytes=67043328 - 4 * slab * nodes - 4096
        ),
    )(
        source, weights, to_modes, from_modes, eigenvalue.reshape(1, levels),
        shifts.reshape(nodes // BLOCK, BLOCK), neighbors,
    )
    smoothed, norm = pl.pallas_call(
        deliver,
        name="deliver",
        out_shape=(
            jax.ShapeDtypeStruct((slab, nodes), f32), jax.ShapeDtypeStruct((1, slab), f32)
        ),
        in_specs=[vmem, vmem],
        out_specs=(hbm, hbm),
        scratch_shapes=[dma((5,))],
    )(
        pltpu.with_memory_space_constraint(smoothed, pltpu.VMEM),
        pltpu.with_memory_space_constraint(norm, pltpu.VMEM),
    )
    return smoothed, norm.reshape(slab)


def solution(mesh):
    return jax.shard_map(
        functools.partial(on_device, mesh.shape["lat"], mesh.shape["rad"]),
        mesh=mesh,
        in_specs=(P("rad", "lat"), P(), P(), P(), P("lat"), P(None, "lat"), P(None, "lat")),
        out_specs=(P("rad", "lat"), P("rad")),
        check_vma=False,
    )
```
